512 devices in a mesh: seq: 128 (over y, z, core), tp: 4 (over x).
Axes of the slice: x: 4, y: 8, z: 8, core: 2. Of those that a mesh axis runs over, the one named last changes fastest.
Arguments:
- hidden_in: bfloat16 [16, 1024], P(None, 'tp'), may hold values from -6 to 6
- w_qkv: bfloat16 [3, 1024, 1024], P(None, None, 'tp'), may hold values from -0.1875 to 0.1875
- w_out: bfloat16 [1024, 1024], P('tp'), may hold values from -0.1875 to 0.1875
- key_cache: bfloat16 [16, 8192, 1024], P(None, 'seq', 'tp'), may hold values from -400 to 400
- value_cache: bfloat16 [16, 8192, 1024], P(None, 'seq', 'tp'), may hold values from -24 to 24
- lengths: int32 [16], replicated, may hold values from 256 to 8191, as said below
- ln_gain: float32 [1024], P('tp'), may hold values from 0.1 to 1.9
- ln_bias: float32 [1024], P('tp'), may hold values from -3 to 3
Outputs:
- layer_out: bfloat16 [16, 1024], P(None, 'tp')
- keys_out: bfloat16 [16, 8192, 1024], P(None, 'seq', 'tp')
- values_out: bfloat16 [16, 8192, 1024], P(None, 'seq', 'tp')
The draws below stay inside these ranges and needn't reach their ends.
Inputs may be any that keep to these rules, and one draw needn't show every extreme that they name: `lengths`: the shortest and the longest of these both occur in every draw.
All inputs are finite; a program needn't handle non-finite values.
Results may differ from the reference program's by a relative error of at most 0.0094.
Values may be sent and summed in bfloat16 or wider, within the bound.
A program may use at most 64 MiB of HBM per device.

```python
import jax
import jax.numpy as jnp
from jax import lax

D = 1024
HEADS = 16
HD = 64
REQUESTS = 16
LMAX = 8192


def draw_key_cache(key, part):
    key_one = jax.random.fold_in(key, 0)
    noise = jnp.clip(jax.random.normal(key_one, (REQUESTS, LMAX, D), jnp.float32), -6.0, 6.0)
    return (1.5 * noise).astype(jnp.bfloat16)


def draw_lengths(key, part):
    key_one, key_two = jax.random.split(key, 2)
    lowest = LMAX // 32
    drawn = jax.random.randint(key_one, (REQUESTS,), lowest, LMAX)
    order = jax.random.permutation(key_two, REQUESTS)
    drawn = drawn.at[order[0]].set(LMAX - 1)
    drawn = drawn.at[order[1]].set(lowest)
    return drawn.astype(jnp.int32)


def steps_of(own_key, dims, cuts, least, high):
    factor_of = 1.0
    for position, parts in cuts:
        draws = jax.random.uniform(jax.random.fold_in(jax.random.fold_in(own_key, 6), position), (parts,), jnp.float32, least / len(cuts), high / len(cuts))
        factor_of = factor_of * jnp.repeat(jnp.exp(draws), dims[position] // parts).reshape((-1,) + (1,) * (len(dims) - 1 - position))
    return factor_of


def normal_values(key, shape, deviation, limit, shards=(), held_as=jnp.bfloat16):
    entries = deviation * jax.random.normal(key, shape, jnp.float32)
    if shards:
        entries = entries * steps_of(key, shape, shards, -0.22, 0.18)
    return jnp.clip(entries, -limit, limit).astype(held_as)


def setup_inputs(seed: int = 0) -> dict:
    key_of = jax.random.split(jax.random.key(seed), 9)
    hidden_in = normal_values(key_of[0], (REQUESTS, D), 1.0, 6.0, ((1, 4),))
    w_qkv = normal_values(key_of[1], (3, D, D), D ** -0.5, 0.1875, ((2, 4),))
    w_out = normal_values(key_of[2], (D, D), D ** -0.5, 0.1875, ((0, 4),))
    key_cache = draw_key_cache(jax.random.fold_in(key_of[8], 71), 0)
    value_cache = normal_values(key_of[4], (REQUESTS, LMAX, D), 4.0, 24.0, ((1, 128), (2, 4)))
    lengths = draw_lengths(jax.random.fold_in(key_of[8], 71), 0)
    ln_gain = jnp.clip(1.0 + 0.18 * jax.random.normal(key_of[6], (D,), jnp.float32), 0.1, 1.9)
    ln_bias = normal_values(key_of[7], (D,), 0.5, 3.0, ((0, 4),), jnp.float32)
    return dict(hidden_in=hidden_in, w_qkv=w_qkv, w_out=w_out, key_cache=key_cache, value_cache=value_cache, lengths=lengths, ln_gain=ln_gain, ln_bias=ln_bias)


def reference(hidden_in, w_qkv, w_out, key_cache, value_cache, lengths, ln_gain, ln_bias):
    query = jnp.dot(hidden_in, w_qkv[0], preferred_element_type=jnp.float32).astype(jnp.bfloat16)
    new_key = jnp.dot(hidden_in, w_qkv[1], preferred_element_type=jnp.float32).astype(jnp.bfloat16)
    new_value = jnp.dot(hidden_in, w_qkv[2], preferred_element_type=jnp.float32).astype(jnp.bfloat16)
    positions = jnp.arange(LMAX, dtype=jnp.int32)
    hit = positions[None, :] == lengths[:, None].astype(jnp.int32)
    keys_out = jnp.where(hit[:, :, None], new_key[:, None, :], key_cache)
    values_out = jnp.where(hit[:, :, None], new_value[:, None, :], value_cache)
    scale_factor = HD ** (-0.5)

    def attend_one(items):
        query_row, key_rows, value_rows, length_one = items
        query_heads = query_row.astype(jnp.float32).reshape(HEADS, HD)
        key_heads = key_rows.astype(jnp.float32).reshape(LMAX, HEADS, HD)
        value_heads = value_rows.astype(jnp.float32).reshape(LMAX, HEADS, HD)
        scores = jnp.einsum('hd,phd->hp', query_heads, key_heads, precision=lax.Precision.HIGHEST) * scale_factor
        valid = positions[None, :] <= length_one
        largest = lax.optimization_barrier(jnp.max(jnp.where(valid, scores, -jnp.inf), axis=1))
        weights = jnp.where(valid, jnp.exp(scores - largest[:, None]), jnp.float32(0.0))
        total = lax.optimization_barrier(jnp.sum(weights, axis=1))
        summed = jnp.einsum('hp,phd->hd', weights, value_heads, precision=lax.Precision.HIGHEST)
        return (summed / total[:, None]).reshape(D)
    attended = lax.map(attend_one, (query, keys_out, values_out, lengths)).astype(jnp.bfloat16)
    mixed = jnp.dot(attended, w_out, preferred_element_type=jnp.float32)
    resid = hidden_in.astype(jnp.float32) + mixed
    mean_val = lax.optimization_barrier(jnp.mean(resid, axis=1, keepdims=True))
    centred = resid - mean_val
    var_val = lax.optimization_barrier(jnp.mean(centred * centred, axis=1, keepdims=True))
    normed = centred / jnp.sqrt(var_val + 1e-05) * ln_gain + ln_bias
    return (normed.astype(jnp.bfloat16), keys_out, values_out)
```

```python
import jax
import jax.numpy as jnp
from jax import lax
from jax.experimental import pallas as pl
from jax.experimental.pallas import tpu as pltpu
from jax.sharding import PartitionSpec as P

D = 1024
HD = 64
B = 16
W = 256
TP = 4
SPAN = 64
NEG = -1e30
F32 = jnp.float32
BF16 = jnp.bfloat16
MESH = pl.DeviceIdType.MESH


def tile_at(ref, index):
    return ref.at[pl.ds(pl.multiple_of(index * 8, 8), 8), :]


def merge(tiles):
    top = tiles[0]
    for tile in tiles[1:]:
        top = jnp.maximum(top, tile)
    total = None
    for tile in tiles:
        factor = pltpu.roll(jnp.exp(tile - top), 4, 0)
        total = tile * factor if total is None else total + tile * factor
    row = lax.broadcasted_iota(jnp.int32, (8, 128), 0)
    return jnp.where(row < 4, total, top)


def kernel(
    lens, hid, wqkv, wout, kc, vc, gain, bias,
    out, kout, vout,
    gath, wbuf, wobuf, kbuf, vbuf, gbuf, bbuf,
    send, rs, zb, newb, hidb, mixb, ag,
    lsem, h_s, h_r, rs_s, rs_r, z_s, z_r, m_s, m_r, a_s, a_r,
):
    seq = lax.axis_index("seq")
    tp = lax.axis_index("tp")
    y, z, c = seq // 16, (seq % 16) // 2, seq % 2
    mine = y * 2 + c

    loads = [
        pltpu.make_async_copy(hid, gath.at[tp], lsem.at[0]),
        pltpu.make_async_copy(wqkv.at[0], wbuf.at[0], lsem.at[1]),
        pltpu.make_async_copy(kc, kbuf, lsem.at[2]),
        pltpu.make_async_copy(vc, vbuf, lsem.at[3]),
        pltpu.make_async_copy(wqkv.at[1], wbuf.at[1], lsem.at[4]),
        pltpu.make_async_copy(wqkv.at[2], wbuf.at[2], lsem.at[5]),
        pltpu.make_async_copy(wout, wobuf, lsem.at[6]),
        pltpu.make_async_copy(gain, gbuf, lsem.at[7]),
        pltpu.make_async_copy(bias, bbuf, lsem.at[8]),
    ]
    for load in loads:
        load.start()

    tp_peers = [lax.rem(tp + d, TP) for d in range(1, TP)]
    yc_peers = []
    for k in range(1, 16):
        y2 = lax.rem(y + k // 2, 8)
        c2 = lax.rem(c + k % 2, 2)
        yc_peers.append((k, y2 * 16 + z * 2 + c2, y2 * 2 + c2))
    z_peers = []
    for d in range(1, 8):
        z2 = lax.rem(z + d, 8)
        z_peers.append((z2, y * 16 + z2 * 2 + c))

    barrier = pltpu.get_barrier_semaphore()
    for t in tp_peers:
        pl.semaphore_signal(barrier, inc=1, device_id=(seq, t), device_id_type=MESH)
    for _, s, _ in yc_peers:
        pl.semaphore_signal(barrier, inc=1, device_id=(s, tp), device_id_type=MESH)
    for _, s in z_peers:
        pl.semaphore_signal(barrier, inc=1, device_id=(s, tp), device_id_type=MESH)
    loads[0].wait()
    pl.semaphore_wait(barrier, 25)

    sends = []
    for d, t in enumerate(tp_peers):
        copy = pltpu.make_async_remote_copy(
            gath.at[tp], gath.at[tp], h_s.at[d], h_r.at[tp], device_id=(seq, t), device_id_type=MESH
        )
        copy.start()
        sends.append(copy)
    loads[1].wait()

    def project(index, t):
        rows = pl.ds(pl.multiple_of(t * W, W), W)
        return jnp.dot(gath[t], wbuf[index, rows, :], preferred_element_type=F32)

    acc = project(0, tp)
    for t in tp_peers:
        pltpu.make_async_remote_copy(
            gath.at[t], gath.at[t], h_s.at[0], h_r.at[t], device_id=(seq, t), device_id_type=MESH
        ).wait_recv()
        acc = acc + project(0, t)
    query = acc.astype(BF16)

    column_head = lax.broadcasted_iota(jnp.int32, (B, W), 1) // HD
    spread = jnp.concatenate(
        [jnp.where(column_head == h, query.astype(F32), 0.0) for h in range(TP)], axis=0
    ).astype(BF16)
    row_b = lax.broadcasted_iota(jnp.int32, (B, 1), 0)
    local_len = jnp.zeros((B, 1), jnp.int32)
    for b in range(B):
        local_len = jnp.where(row_b == b, lens[b] - seq * SPAN, local_len)
    low = jnp.concatenate([row_b * SPAN] * 4, axis=0)
    high = low + jnp.concatenate([jnp.clip(local_len, 0, SPAN)] * 4, axis=0)
    column = lax.broadcasted_iota(jnp.int32, (4 * B, B * SPAN), 1)
    valid = jnp.logical_and(column >= low, column < high)
    loads[2].wait()
    keys = kbuf[...].reshape(B * SPAN, W)
    scores = lax.dot_general(spread, keys, (((1,), (1,)), ((), ())), preferred_element_type=F32)
    scores = jnp.where(valid, scores * HD ** (-0.5), NEG)
    top = jnp.max(scores, axis=1, keepdims=True)
    weights = jnp.where(valid, jnp.exp(scores - top), 0.0)
    total = jnp.sum(weights, axis=1, keepdims=True)
    upper = weights.astype(BF16)
    lower = (weights - upper.astype(F32)).astype(BF16)
    loads[3].wait()
    values = vbuf[...].reshape(B * SPAN, W)
    both = jnp.dot(jnp.concatenate([upper, lower], axis=0), values, preferred_element_type=F32)
    summed = both[: 4 * B] + both[4 * B :]

    def fold(rows):
        result = jnp.broadcast_to(rows[0:B], (B, W))
        for h in range(1, 4):
            result = jnp.where(column_head == h, rows[h * B : (h + 1) * B], result)
        return result

    def store_tiles(ref, values16, totals16, tops16):
        for part in range(2):
            lanes = slice(part * 128, part * 128 + 128)
            ref[pl.ds(part, B, stride=8), :] = values16[:, lanes]
            ref[pl.ds(2 + part, B, stride=8), :] = totals16[:, lanes]
            ref[pl.ds(4 + part, B, stride=8), :] = tops16[:, lanes]
            ref[pl.ds(6 + part, B, stride=8), :] = tops16[:, lanes]

    store_tiles(send, fold(summed), fold(total), fold(top))
    for k, s, request in yc_peers:
        copy = pltpu.make_async_remote_copy(
            tile_at(send, request), tile_at(rs, k), rs_s.at[k], rs_r.at[k],
            device_id=(s, tp), device_id_type=MESH,
        )
        copy.start()
        sends.append(copy)

    loads[4].wait()
    loads[5].wait()
    new_key = sum(project(1, t) for t in range(TP)).astype(BF16)
    new_value = sum(project(2, t) for t in range(TP)).astype(BF16)
    product = query.astype(F32) * new_key.astype(F32)
    product_up = product.astype(BF16)
    product_low = (product - product_up.astype(F32)).astype(BF16)
    same_head = (
        lax.broadcasted_iota(jnp.int32, (W, W), 0) // HD == lax.broadcasted_iota(jnp.int32, (W, W), 1) // HD
    )
    ones = jnp.where(same_head, 1.0, 0.0).astype(BF16)
    new_both = jnp.dot(jnp.concatenate([product_up, product_low], axis=0), ones, preferred_element_type=F32)
    new_score = (new_both[:B] + new_both[B:]) * HD ** (-0.5)
    store_tiles(newb, new_value.astype(F32), jnp.ones((B, W), F32), new_score)

    position = lax.broadcasted_iota(jnp.int32, (SPAN, W), 0)
    for b in range(B):
        hit = position == lens[b] - seq * SPAN
        kout[b] = jnp.where(hit, new_key[b : b + 1].astype(F32), kbuf[b].astype(F32)).astype(BF16)
        vout[b] = jnp.where(hit, new_value[b : b + 1].astype(F32), vbuf[b].astype(F32)).astype(BF16)
    for t in range(TP):
        state = gath[t].astype(F32)
        for part in range(2):
            hidb[pl.ds(t * 2 + part, B, stride=8), :] = state[:, part * 128 : part * 128 + 128]

    tiles = [tile_at(send, mine)[...]]
    for k, s, request in yc_peers:
        pltpu.make_async_remote_copy(
            tile_at(send, request), tile_at(rs, k), rs_s.at[k], rs_r.at[k],
            device_id=(s, tp), device_id_type=MESH,
        ).wait_recv()
        tiles.append(rs[k * 8 : k * 8 + 8, :])
    tile_at(zb, z)[...] = merge(tiles)

    for d, (_, s) in enumerate(z_peers):
        copy = pltpu.make_async_remote_copy(
            tile_at(zb, z), tile_at(zb, z), z_s.at[d], z_r.at[z], device_id=(s, tp), device_id_type=MESH
        )
        copy.start()
        sends.append(copy)
    loads[6].wait()
    for z2, s in z_peers:
        pltpu.make_async_remote_copy(
            tile_at(zb, z2), tile_at(zb, z2), z_s.at[0], z_r.at[z2], device_id=(s, tp), device_id_type=MESH
        ).wait_recv()
    merged = merge([zb[k * 8 : k * 8 + 8, :] for k in range(8)] + [tile_at(newb, mine)[...]])

    attended = merged / pltpu.roll(merged, 6, 0)
    first = attended[0:1]
    second = attended[1:2]
    row_vec = jnp.concatenate([first, second], axis=1).astype(BF16)
    mixed = jnp.dot(
        jnp.broadcast_to(row_vec, (16, W)), wobuf[...], preferred_element_type=F32
    )
    base = pl.multiple_of(tp * 8, 8)
    mixb[pl.ds(base, 8), :] = jnp.concatenate(
        [mixed[0:1, j * 128 : j * 128 + 128] for j in range(8)], axis=0
    )
    for d, t in enumerate(tp_peers):
        copy = pltpu.make_async_remote_copy(
            tile_at(mixb, tp), tile_at(mixb, tp), m_s.at[d], m_r.at[tp], device_id=(seq, t), device_id_type=MESH
        )
        copy.start()
        sends.append(copy)
    loads[7].wait()
    loads[8].wait()
    for t in tp_peers:
        pltpu.make_async_remote_copy(
            tile_at(mixb, t), tile_at(mixb, t), m_s.at[0], m_r.at[t], device_id=(seq, t), device_id_type=MESH
        ).wait_recv()
    resid = tile_at(hidb, mine)[...] + (
        (mixb[0:8, :] + mixb[8:16, :]) + (mixb[16:24, :] + mixb[24:32, :])
    )
    mean = jnp.sum(jnp.sum(resid, axis=0, keepdims=True), axis=1, keepdims=True) / D
    centred = resid - mean
    var = jnp.sum(jnp.sum(centred * centred, axis=0, keepdims=True), axis=1, keepdims=True) / D
    scaled = centred / jnp.sqrt(var + 1e-05)
    own = scaled[0:2]
    for t in range(1, TP):
        own = jnp.where(tp == t, scaled[2 * t : 2 * t + 2], own)
    normed = own * gbuf[...] + bbuf[...]
    ag[pl.ds(pl.multiple_of(mine * 8, 8), 2), :] = normed
    for k, s, request in yc_peers:
        copy = pltpu.make_async_remote_copy(
            tile_at(ag, mine), tile_at(ag, mine), a_s.at[k], a_r.at[mine],
            device_id=(s, tp), device_id_type=MESH,
        )
        copy.start()
        sends.append(copy)
    for k, s, request in yc_peers:
        pltpu.make_async_remote_copy(
            tile_at(ag, request), tile_at(ag, request), a_s.at[k], a_r.at[request],
            device_id=(s, tp), device_id_type=MESH,
        ).wait_recv()
    for part in range(2):
        out[:, part * 128 : part * 128 + 128] = ag[pl.ds(part, B, stride=8), :].astype(BF16)
    for copy in sends:
        copy.wait_send()


def body(hidden_in, w_qkv, w_out, key_cache, value_cache, lengths, ln_gain, ln_bias):
    hbm = pl.BlockSpec(memory_space=pl.ANY)
    vmem = pl.BlockSpec(memory_space=pltpu.VMEM)
    cache = jax.ShapeDtypeStruct((B, SPAN, W), BF16)
    dma = pltpu.SemaphoreType.DMA
    return pl.pallas_call(
        kernel,
        out_shape=(jax.ShapeDtypeStruct((B, W), BF16), cache, cache),
        in_specs=[pl.BlockSpec(memory_space=pltpu.SMEM)] + [hbm] * 7,
        out_specs=(vmem, vmem, vmem),
        scratch_shapes=[
            pltpu.VMEM((TP, B, W), BF16),
            pltpu.VMEM((3, D, W), BF16),
            pltpu.VMEM((W, D), BF16),
            pltpu.VMEM((B, SPAN, W), BF16),
            pltpu.VMEM((B, SPAN, W), BF16),
            pltpu.VMEM((2, 128), F32),
            pltpu.VMEM((2, 128), F32),
            pltpu.VMEM((128, 128), F32),
            pltpu.VMEM((128, 128), F32),
            pltpu.VMEM((64, 128), F32),
            pltpu.VMEM((128, 128), F32),
            pltpu.VMEM((128, 128), F32),
            pltpu.VMEM((32, 128), F32),
            pltpu.VMEM((128, 128), F32),
            dma((9,)),
            dma((3,)), dma((4,)),
            dma((16,)), dma((16,)),
            dma((7,)), dma((8,)),
            dma((3,)), dma((4,)),
            dma((16,)), dma((16,)),
        ],
        compiler_params=pltpu.CompilerParams(collective_id=0, has_side_effects=True),
        name="sublayer",
    )(
        lengths, hidden_in, w_qkv, w_out, key_cache, value_cache,
        ln_gain.reshape(2, 128), ln_bias.reshape(2, 128),
    )


def solution(mesh):
    in_specs = (
        P(None, "tp"),
        P(None, None, "tp"),
        P("tp", None),
        P(None, "seq", "tp"),
        P(None, "seq", "tp"),
        P(),
        P("tp"),
        P("tp"),
    )
    out_specs = (P(None, "tp"), P(None, "seq", "tp"), P(None, "seq", "tp"))
    return jax.shard_map(body, mesh=mesh, in_specs=in_specs, out_specs=out_specs, check_vma=False)
```

```python
import jax
import jax.numpy as jnp
from jax import lax
from jax.experimental import pallas as pl
from jax.experimental.pallas import tpu as pltpu
from jax.sharding import PartitionSpec as P

D = 1024
HD = 64
B = 16
HALF = 8
W = 256
TP = 4
RING = 8
SPAN = 64
SLOT = 24
SENT = 17
NEG = -1e30
F32 = jnp.float32
BF16 = jnp.bfloat16
MESH = pl.DeviceIdType.MESH


def iota(shape, dim):
    return lax.broadcasted_iota(jnp.int32, shape, dim)


def split_dot(rows, matrix):
    upper = rows.astype(BF16)
    lower = (rows - upper.astype(F32)).astype(BF16)
    both = jnp.dot(jnp.concatenate([upper, lower], axis=0), matrix, preferred_element_type=F32)
    return both[: rows.shape[0]] + both[rows.shape[0] :]


def to_row(tops, totals):
    lane, request = iota((HALF, W), 1) % HD, iota((HALF, W), 0)
    picked = jnp.where(lane == request, tops, jnp.where(lane == request + HALF, totals, 0.0))
    row = jnp.sum(picked, axis=0, keepdims=True)
    return row[:, :128] + pltpu.roll(row[:, 128:], 16, 1)


def spread_rows(rows):
    entry = iota((HALF, 128), 1)
    keep = jnp.logical_and(entry % 16 == iota((HALF, 128), 0), entry % 64 < 32)
    picked = jnp.concatenate(
        [jnp.where(keep, rows[s : s + 1], 0.0) for s in range(rows.shape[0])], axis=0
    )
    lane, column = iota((128, W), 0), iota((128, W), 1)
    head = lane // 64 + 2 * ((lane % 64) // 16)
    matrix = jnp.where(jnp.logical_and(lane % 64 < 32, head == column // HD), 1.0, 0.0).astype(BF16)
    return split_dot(picked, matrix)


def kernel(
    lens, hid, wqkv, wout, kc, vc, gain, bias,
    out, kout, vout,
    gath, wbuf, wobuf, kbuf, vbuf, gbuf, bbuf,
    csend, crecv, yb, zb, mixb, fin, obuf,
    lsem, hsem, recv, sent,
):
    seq = lax.axis_index("seq")
    tp = lax.axis_index("tp")
    y, z, c = seq // 16, (seq % 16) // 2, seq % 2

    loads = [
        pltpu.make_async_copy(hid, gath.at[tp], lsem.at[0]),
        pltpu.make_async_copy(wqkv.at[0], wbuf.at[0], lsem.at[1]),
        pltpu.make_async_copy(kc, kbuf, lsem.at[2]),
        pltpu.make_async_copy(vc, vbuf, lsem.at[3]),
        pltpu.make_async_copy(wqkv.at[pl.ds(1, 2)], wbuf.at[pl.ds(1, 2)], lsem.at[4]),
        pltpu.make_async_copy(wout, wobuf, lsem.at[5]),
        pltpu.make_async_copy(gain, gbuf, lsem.at[6]),
        pltpu.make_async_copy(bias, bbuf, lsem.at[7]),
    ]
    for load in loads:
        load.start()

    tp_peers = [(seq, lax.rem(tp + d, TP)) for d in (2, 1, 3)]
    y_peers = [(lax.rem(y + d, RING) * 16 + z * 2 + c, tp) for d in (4, 3, 5, 2, 6, 1, 7)]
    z_peers = [(y * 16 + lax.rem(z + d, RING) * 2 + c, tp) for d in (4, 3, 5, 2, 6, 1, 7)]
    sibling = (y * 16 + z * 2 + (1 - c), tp)

    barrier = pltpu.get_barrier_semaphore()
    for peer in y_peers + z_peers + tp_peers + [sibling]:
        pl.semaphore_signal(barrier, inc=1, device_id=peer, device_id_type=MESH)
    loads[0].wait()
    pl.semaphore_wait(barrier, 18)

    def push(src, dst, stage, recv_sem, peer):
        pltpu.make_async_remote_copy(
            src, dst, sent.at[stage], recv_sem, device_id=peer, device_id_type=MESH
        ).start()

    def arrived(ref, sem):
        pltpu.make_async_copy(ref, ref, sem).wait()

    for i, peer in enumerate(tp_peers):
        push(gath.at[tp], gath.at[tp], 0, hsem.at[i], peer)
    loads[1].wait()

    def project(index, t):
        rows = pl.ds(pl.multiple_of(t * W, W), W)
        return jnp.dot(gath[t], wbuf[index, rows, :], preferred_element_type=F32)

    acc = project(0, tp)
    for i, d in ((1, 1), (2, 3), (0, 2)):
        t = lax.rem(tp + TP - d, TP)
        arrived(gath.at[t], hsem.at[i])
        acc = acc + project(0, t)
    query = acc.astype(BF16)

    column_head = iota((B, W), 1) // HD
    spread = jnp.concatenate(
        [jnp.where(column_head == h, query.astype(F32), 0.0) for h in range(4)], axis=0
    ).astype(BF16)
    row_b = iota((B, 1), 0)
    local_len = jnp.zeros((B, 1), jnp.int32)
    for b in range(B):
        local_len = jnp.where(row_b == b, lens[b] - seq * SPAN, local_len)
    low = jnp.concatenate([row_b * SPAN] * 4, axis=0)
    high = low + jnp.concatenate([jnp.clip(local_len, 0, SPAN)] * 4, axis=0)
    column = iota((4 * B, B * SPAN), 1)
    valid = jnp.logical_and(column >= low, column < high)
    loads[2].wait()
    keys = kbuf[...].reshape(B * SPAN, W)
    scores = lax.dot_general(spread, keys, (((1,), (1,)), ((), ())), preferred_element_type=F32)
    scores = jnp.where(valid, scores * HD ** (-0.5), NEG)
    top = jnp.max(scores, axis=1, keepdims=True)
    weights = jnp.where(valid, jnp.exp(scores - top), 0.0)
    total = jnp.sum(weights, axis=1, keepdims=True)
    loads[3].wait()
    summed = split_dot(weights, vbuf[...].reshape(B * SPAN, W))

    def fold(rows):
        result = jnp.broadcast_to(rows[0:B], (B, W))
        for h in range(1, 4):
            result = jnp.where(column_head == h, rows[h * B : (h + 1) * B], result)
        return result

    for core in range(2):
        for i, part in enumerate((fold(summed), fold(total), fold(top))):
            csend[core, i] = part[core * HALF : (core + 1) * HALF]
    push(csend.at[1 - c], crecv, 1, recv.at[0], sibling)

    loads[4].wait()
    new_key = sum(project(1, t) for t in range(TP)).astype(BF16)
    new_value = sum(project(2, t) for t in range(TP)).astype(BF16)

    arrived(crecv, recv.at[0])
    my_acc, my_total, my_top = csend[c, 0], csend[c, 1], csend[c, 2]
    both_top = jnp.maximum(my_top, crecv[2])
    mine, other = jnp.exp(my_top - both_top), jnp.exp(crecv[2] - both_top)
    both_acc = my_acc * mine + crecv[0] * other
    both_total = my_total * mine + crecv[1] * other

    def place(ref, slot, acc, row):
        base = pl.multiple_of(slot * SLOT, 8)
        ref[pl.ds(base, 8), :] = acc[:, :128]
        ref[pl.ds(base + 8, 8), :] = acc[:, 128:]
        ref[pl.ds(base + 16, 1), :] = row

    def slot_of(ref, slot, rows=SENT):
        return ref.at[pl.ds(pl.multiple_of(slot * SLOT, 8), rows), :]

    def wait_ring(ref, sem):
        arrived(ref.at[pl.ds(0, 7 * SENT), :], sem)

    def ring_acc(ref, factors):
        acc = None
        for s in range(RING):
            part = jnp.concatenate(
                [ref[s * SLOT : s * SLOT + 8, :], ref[s * SLOT + 8 : s * SLOT + 16, :]], axis=1
            ) * factors[s * 8 : s * 8 + 8]
            acc = part if acc is None else acc + part
        return acc

    place(yb, y, both_acc, to_row(both_top, both_total))
    for peer in y_peers:
        push(slot_of(yb, y), slot_of(yb, y), 2, recv.at[1], peer)

    same_head = iota((W, W), 0) // HD == iota((W, W), 1) // HD
    new_score = split_dot(
        query.astype(F32) * new_key.astype(F32), jnp.where(same_head, 1.0, 0.0).astype(BF16)
    ) * HD ** (-0.5)

    def own_half(rows):
        return jnp.where(c == 0, rows[:HALF], rows[HALF:])

    new_row = to_row(own_half(new_score), jnp.ones((HALF, W), F32))
    new_acc = own_half(new_value.astype(F32))
    position = iota((SPAN, W), 0)
    for b in range(B):
        hit = position == lens[b] - seq * SPAN
        kbuf[b] = jnp.where(hit, new_key[b : b + 1].astype(F32), kbuf[b].astype(F32)).astype(BF16)
        vbuf[b] = jnp.where(hit, new_value[b : b + 1].astype(F32), vbuf[b].astype(F32)).astype(BF16)
    stores = [
        pltpu.make_async_copy(kbuf, kout, lsem.at[2]),
        pltpu.make_async_copy(vbuf, vout, lsem.at[3]),
    ]
    for store in stores:
        store.start()

    wait_ring(yb, recv.at[1])
    max_lane = iota((1, 128), 1) % 16 < 8
    rows = yb[pl.ds(16, RING, stride=SLOT), :]
    ring_top = jnp.max(rows, axis=0, keepdims=True)
    factor = jnp.exp(rows - ring_top)
    ring_total = jnp.sum(rows * pltpu.roll(factor, 8, 1), axis=0, keepdims=True)
    place(zb, z, ring_acc(yb, spread_rows(factor)), jnp.where(max_lane, ring_top, ring_total))
    for peer in z_peers:
        push(slot_of(zb, z), slot_of(zb, z), 3, recv.at[2], peer)

    state = [own_half(gath[t].astype(F32)) for t in range(TP)]
    loads[5].wait()
    loads[6].wait()
    loads[7].wait()

    wait_ring(zb, recv.at[2])
    rows = zb[pl.ds(16, RING, stride=SLOT), :]
    last_top = jnp.maximum(jnp.max(rows, axis=0, keepdims=True), new_row)
    factor = jnp.exp(rows - last_top)
    new_factor = jnp.exp(new_row - last_top)
    last_total = jnp.sum(rows * pltpu.roll(factor, 8, 1), axis=0, keepdims=True)
    last_total = last_total + new_row * pltpu.roll(new_factor, 8, 1)
    share = pltpu.roll(last_total, 120, 1)
    factors = spread_rows(jnp.concatenate([factor / share, new_factor / share], axis=0))
    attended = ring_acc(zb, factors) + new_acc * factors[RING * 8 :]
    mixb[tp] = jnp.dot(attended.astype(BF16), wobuf[...], preferred_element_type=F32)
    for peer in tp_peers:
        push(mixb.at[tp], mixb.at[tp], 4, recv.at[3], peer)
    arrived(mixb.at[pl.ds(0, 3)], recv.at[3])
    resid = []
    for t in range(TP):
        lanes = slice(t * W, (t + 1) * W)
        resid.append(
            state[t] + ((mixb[0, :, lanes] + mixb[1, :, lanes]) + (mixb[2, :, lanes] + mixb[3, :, lanes]))
        )
    mean = jnp.sum((resid[0] + resid[1]) + (resid[2] + resid[3]), axis=1, keepdims=True) / D
    centred = [part - mean for part in resid]
    square = [part * part for part in centred]
    var = jnp.sum((square[0] + square[1]) + (square[2] + square[3]), axis=1, keepdims=True) / D
    own = centred[0]
    for t in range(1, TP):
        own = jnp.where(tp == t, centred[t], own)
    fin[c] = own / jnp.sqrt(var + 1e-05) * gbuf[...] + bbuf[...]
    push(fin.at[c], fin.at[c], 5, recv.at[4], sibling)

    for store in stores:
        store.wait()
    arrived(gath.at[pl.ds(0, 3)], sent.at[0])
    arrived(crecv, sent.at[1])
    wait_ring(yb, sent.at[2])
    wait_ring(zb, sent.at[3])
    arrived(mixb.at[pl.ds(0, 3)], sent.at[4])
    arrived(fin.at[0], recv.at[4])
    obuf[...] = jnp.concatenate([fin[0], fin[1]], axis=0).astype(BF16)
    last = pltpu.make_async_copy(obuf, out, lsem.at[0])
    last.start()
    arrived(fin.at[0], sent.at[5])
    last.wait()


def hand_out(o_in, k_in, v_in, o_out, k_out, v_out, obuf, kbuf, vbuf, sem):
    pairs = ((k_in, kbuf, k_out), (v_in, vbuf, v_out), (o_in, obuf, o_out))
    ins = [pltpu.make_async_copy(a, b, sem.at[i]) for i, (a, b, _) in enumerate(pairs)]
    outs = [pltpu.make_async_copy(b, d, sem.at[3 + i]) for i, (_, b, d) in enumerate(pairs)]
    for copy in ins:
        copy.start()
    for first, second in zip(ins, outs):
        first.wait()
        second.start()
    for copy in outs:
        copy.wait()


def body(hidden_in, w_qkv, w_out, key_cache, value_cache, lengths, ln_gain, ln_bias):
    hbm = pl.BlockSpec(memory_space=pl.ANY)
    cache = jax.ShapeDtypeStruct((B, SPAN, W), BF16)
    results = (jax.ShapeDtypeStruct((B, W), BF16), cache, cache)
    dma = pltpu.SemaphoreType.DMA
    done = pl.pallas_call(
        kernel,
        out_shape=results,
        in_specs=[pl.BlockSpec(memory_space=pltpu.SMEM)] + [hbm] * 7,
        out_specs=(hbm, hbm, hbm),
        scratch_shapes=[
            pltpu.VMEM((TP, B, W), BF16),
            pltpu.VMEM((3, D, W), BF16),
            pltpu.VMEM((W, D), BF16),
            pltpu.VMEM((B, SPAN, W), BF16),
            pltpu.VMEM((B, SPAN, W), BF16),
            pltpu.VMEM((1, W), F32),
            pltpu.VMEM((1, W), F32),
            pltpu.VMEM((2, 3, HALF, W), F32),
            pltpu.VMEM((3, HALF, W), F32),
            pltpu.VMEM((RING * SLOT, 128), F32),
            pltpu.VMEM((RING * SLOT, 128), F32),
            pltpu.VMEM((TP, HALF, D), F32),
            pltpu.VMEM((2, HALF, W), F32),
            pltpu.VMEM((B, W), BF16),
            dma((8,)), dma((3,)), dma((5,)), dma((6,)),
        ],
        compiler_params=pltpu.CompilerParams(collective_id=0, has_side_effects=True),
        name="sublayer",
    )(
        lengths, hidden_in, w_qkv, w_out, key_cache, value_cache,
        ln_gain.reshape(1, W), ln_bias.reshape(1, W),
    )
    return pl.pallas_call(
        hand_out,
        out_shape=results,
        in_specs=[hbm] * 3,
        out_specs=(hbm, hbm, hbm),
        scratch_shapes=[
            pltpu.VMEM((B, W), BF16),
            pltpu.VMEM((B, SPAN, W), BF16),
            pltpu.VMEM((B, SPAN, W), BF16),
            dma((6,)),
        ],
        name="hand_out",
    )(*done)


def solution(mesh):
    in_specs = (
        P(None, "tp"),
        P(None, None, "tp"),
        P("tp", None),
        P(None, "seq", "tp"),
        P(None, "seq", "tp"),
        P(),
        P("tp"),
        P("tp"),
    )
    out_specs = (P(None, "tp"), P(None, "seq", "tp"), P(None, "seq", "tp"))
    return jax.shard_map(body, mesh=mesh, in_specs=in_specs, out_specs=out_specs, check_vma=False)
```

```python
import jax
import jax.numpy as jnp
from jax import lax
from jax.experimental import pallas as pl
from jax.experimental.pallas import tpu as pltpu
from jax.sharding import PartitionSpec as P

D = 1024
HD = 64
B = 16
HALF = 8
W = 256
TP = 4
RING = 8
SPAN = 64
SLOT = 24
SENT = 17
NEG = -1e30
F32 = jnp.float32
BF16 = jnp.bfloat16
MESH = pl.DeviceIdType.MESH


def iota(shape, dim):
    return lax.broadcasted_iota(jnp.int32, shape, dim)


def split_dot(rows, matrix):
    upper = rows.astype(BF16)
    lower = (rows - upper.astype(F32)).astype(BF16)
    both = jnp.dot(jnp.concatenate([upper, lower], axis=0), matrix, preferred_element_type=F32)
    return both[: rows.shape[0]] + both[rows.shape[0] :]


def to_row(tops, totals):
    lane, request = iota((HALF, W), 1) % HD, iota((HALF, W), 0)
    picked = jnp.where(lane == request, tops, jnp.where(lane == request + HALF, totals, 0.0))
    row = jnp.sum(picked, axis=0, keepdims=True)
    return row[:, :128] + pltpu.roll(row[:, 128:], 16, 1)


def spread_rows(rows):
    entry = iota((HALF, 128), 1)
    keep = jnp.logical_and(entry % 16 == iota((HALF, 128), 0), entry % 64 < 32)
    picked = jnp.concatenate(
        [jnp.where(keep, rows[s : s + 1], 0.0) for s in range(rows.shape[0])], axis=0
    )
    lane, column = iota((128, W), 0), iota((128, W), 1)
    head = lane // 64 + 2 * ((lane % 64) // 16)
    matrix = jnp.where(jnp.logical_and(lane % 64 < 32, head == column // HD), 1.0, 0.0).astype(BF16)
    return split_dot(picked, matrix)


def kernel(
    lengths, hid, wqkv, wout, kc, vc, gain, bias,
    out, kbuf, vbuf,
    lens, gath, wbuf, wobuf, gbuf, bbuf,
    csend, crecv, yb, zb, mixb, fin,
    lsem, hsem, recv, sent,
):
    seq = lax.axis_index("seq")
    tp = lax.axis_index("tp")
    y, z, c = seq // 16, (seq % 16) // 2, seq % 2

    loads = [
        pltpu.make_async_copy(hid, gath.at[tp], lsem.at[0]),
        pltpu.make_async_copy(wqkv.at[0], wbuf.at[0], lsem.at[1]),
        pltpu.make_async_copy(kc, kbuf, lsem.at[2]),
        pltpu.make_async_copy(vc, vbuf, lsem.at[3]),
        pltpu.make_async_copy(wqkv.at[pl.ds(1, 2)], wbuf.at[pl.ds(1, 2)], lsem.at[4]),
        pltpu.make_async_copy(wout, wobuf, lsem.at[5]),
        pltpu.make_async_copy(gain, gbuf, lsem.at[6]),
        pltpu.make_async_copy(bias, bbuf, lsem.at[7]),
        pltpu.make_async_copy(lengths, lens, lsem.at[8]),
    ]
    for load in loads:
        load.start()

    tp_peers = [(seq, lax.rem(tp + d, TP)) for d in (2, 1, 3)]
    y_peers = [(lax.rem(y + d, RING) * 16 + z * 2 + c, tp) for d in (4, 3, 5, 2, 6, 1, 7)]
    z_peers = [(y * 16 + lax.rem(z + d, RING) * 2 + c, tp) for d in (4, 3, 5, 2, 6, 1, 7)]
    sibling = (y * 16 + z * 2 + (1 - c), tp)

    barrier = pltpu.get_barrier_semaphore()
    for peer in tp_peers + [sibling] + y_peers + z_peers:
        pl.semaphore_signal(barrier, inc=1, device_id=peer, device_id_type=MESH)
    loads[0].wait()
    pl.semaphore_wait(barrier, 18)

    def push(src, dst, stage, recv_sem, peer):
        pltpu.make_async_remote_copy(
            src, dst, sent.at[stage], recv_sem, device_id=peer, device_id_type=MESH
        ).start()

    def arrived(ref, sem):
        pltpu.make_async_copy(ref, ref, sem).wait()

    for i, peer in enumerate(tp_peers):
        push(gath.at[tp], gath.at[tp], 0, hsem.at[i], peer)
    loads[1].wait()

    def project(index, t):
        rows = pl.ds(pl.multiple_of(t * W, W), W)
        return jnp.dot(gath[t], wbuf[index, rows, :], preferred_element_type=F32)

    acc = project(0, tp)
    for i, d in ((1, 1), (2, 3), (0, 2)):
        t = lax.rem(tp + TP - d, TP)
        arrived(gath.at[t], hsem.at[i])
        acc = acc + project(0, t)
    query = acc.astype(BF16)

    column_head = iota((B, W), 1) // HD
    spread = jnp.concatenate(
        [jnp.where(column_head == h, query.astype(F32), 0.0) for h in range(4)], axis=0
    ).astype(BF16)
    row_b = iota((B, 1), 0)
    loads[8].wait()
    local_len = jnp.zeros((B, 1), jnp.int32)
    for b in range(B):
        local_len = jnp.where(row_b == b, lens[b] - seq * SPAN, local_len)
    low = jnp.concatenate([row_b * SPAN] * 4, axis=0)
    high = low + jnp.concatenate([jnp.clip(local_len, 0, SPAN)] * 4, axis=0)
    column = iota((4 * B, B * SPAN), 1)
    valid = jnp.logical_and(column >= low, column < high)
    loads[2].wait()
    keys = kbuf[...].reshape(B * SPAN, W)
    scores = lax.dot_general(spread, keys, (((1,), (1,)), ((), ())), preferred_element_type=F32)
    scores = jnp.where(valid, scores * HD ** (-0.5), NEG)
    top = jnp.max(scores, axis=1, keepdims=True)
    weights = jnp.where(valid, jnp.exp(scores - top), 0.0)
    total = jnp.sum(weights, axis=1, keepdims=True)
    loads[3].wait()
    summed = split_dot(weights, vbuf[...].reshape(B * SPAN, W))

    def fold(rows):
        result = jnp.broadcast_to(rows[0:B], (B, W))
        for h in range(1, 4):
            result = jnp.where(column_head == h, rows[h * B : (h + 1) * B], result)
        return result

    for core in range(2):
        for i, part in enumerate((fold(summed), fold(total), fold(top))):
            csend[core, i] = part[core * HALF : (core + 1) * HALF]
    push(csend.at[1 - c], crecv, 1, recv.at[0], sibling)

    loads[4].wait()
    new_key = sum(project(1, t) for t in range(TP)).astype(BF16)
    new_value = sum(project(2, t) for t in range(TP)).astype(BF16)

    arrived(crecv, recv.at[0])
    my_acc, my_total, my_top = csend[c, 0], csend[c, 1], csend[c, 2]
    both_top = jnp.maximum(my_top, crecv[2])
    mine, other = jnp.exp(my_top - both_top), jnp.exp(crecv[2] - both_top)
    both_acc = my_acc * mine + crecv[0] * other
    both_total = my_total * mine + crecv[1] * other

    def place(ref, slot, acc, row):
        base = pl.multiple_of(slot * SLOT, 8)
        ref[pl.ds(base, 8), :] = acc[:, :128]
        ref[pl.ds(base + 8, 8), :] = acc[:, 128:]
        ref[pl.ds(base + 16, 1), :] = row

    def slot_of(ref, slot, rows=SENT):
        return ref.at[pl.ds(pl.multiple_of(slot * SLOT, 8), rows), :]

    def wait_ring(ref, sem):
        arrived(ref.at[pl.ds(0, 7 * SENT), :], sem)

    def ring_acc(ref, factors):
        acc = None
        for s in range(RING):
            part = jnp.concatenate(
                [ref[s * SLOT : s * SLOT + 8, :], ref[s * SLOT + 8 : s * SLOT + 16, :]], axis=1
            ) * factors[s * 8 : s * 8 + 8]
            acc = part if acc is None else acc + part
        return acc

    place(yb, y, both_acc, to_row(both_top, both_total))
    for peer in y_peers:
        push(slot_of(yb, y), slot_of(yb, y), 2, recv.at[1], peer)

    same_head = iota((W, W), 0) // HD == iota((W, W), 1) // HD
    new_score = split_dot(
        query.astype(F32) * new_key.astype(F32), jnp.where(same_head, 1.0, 0.0).astype(BF16)
    ) * HD ** (-0.5)

    def own_half(rows):
        return jnp.where(c == 0, rows[:HALF], rows[HALF:])

    new_row = to_row(own_half(new_score), jnp.ones((HALF, W), F32))
    new_acc = own_half(new_value.astype(F32))
    position = iota((SPAN, W), 0)
    for b in range(B):
        hit = position == lens[b] - seq * SPAN
        kbuf[b] = jnp.where(hit, new_key[b : b + 1].astype(F32), kbuf[b].astype(F32)).astype(BF16)
        vbuf[b] = jnp.where(hit, new_value[b : b + 1].astype(F32), vbuf[b].astype(F32)).astype(BF16)
    wait_ring(yb, recv.at[1])
    max_lane = iota((1, 128), 1) % 16 < 8
    rows = yb[pl.ds(16, RING, stride=SLOT), :]
    ring_top = jnp.max(rows, axis=0, keepdims=True)
    factor = jnp.exp(rows - ring_top)
    ring_total = jnp.sum(rows * pltpu.roll(factor, 8, 1), axis=0, keepdims=True)
    place(zb, z, ring_acc(yb, spread_rows(factor)), jnp.where(max_lane, ring_top, ring_total))
    for peer in z_peers:
        push(slot_of(zb, z), slot_of(zb, z), 3, recv.at[2], peer)

    state = [own_half(gath[t].astype(F32)) for t in range(TP)]
    loads[5].wait()
    loads[6].wait()
    loads[7].wait()

    wait_ring(zb, recv.at[2])
    rows = zb[pl.ds(16, RING, stride=SLOT), :]
    last_top = jnp.maximum(jnp.max(rows, axis=0, keepdims=True), new_row)
    factor = jnp.exp(rows - last_top)
    new_factor = jnp.exp(new_row - last_top)
    last_total = jnp.sum(rows * pltpu.roll(factor, 8, 1), axis=0, keepdims=True)
    last_total = last_total + new_row * pltpu.roll(new_factor, 8, 1)
    share = pltpu.roll(last_total, 120, 1)
    factors = spread_rows(jnp.concatenate([factor / share, new_factor / share], axis=0))
    attended = ring_acc(zb, factors) + new_acc * factors[RING * 8 :]
    mixb[tp] = jnp.dot(attended.astype(BF16), wobuf[...], preferred_element_type=F32)
    for peer in tp_peers:
        push(mixb.at[tp], mixb.at[tp], 4, recv.at[3], peer)
    arrived(mixb.at[pl.ds(0, 3)], recv.at[3])
    resid = []
    for t in range(TP):
        lanes = slice(t * W, (t + 1) * W)
        resid.append(
            state[t] + ((mixb[0, :, lanes] + mixb[1, :, lanes]) + (mixb[2, :, lanes] + mixb[3, :, lanes]))
        )
    mean = jnp.sum((resid[0] + resid[1]) + (resid[2] + resid[3]), axis=1, keepdims=True) / D
    centred = [part - mean for part in resid]
    square = [part * part for part in centred]
    var = jnp.sum((square[0] + square[1]) + (square[2] + square[3]), axis=1, keepdims=True) / D
    own = centred[0]
    for t in range(1, TP):
        own = jnp.where(tp == t, centred[t], own)
    fin[c] = own / jnp.sqrt(var + 1e-05) * gbuf[...] + bbuf[...]
    push(fin.at[c], fin.at[c], 5, recv.at[4], sibling)

    arrived(gath.at[pl.ds(0, 3)], sent.at[0])
    arrived(crecv, sent.at[1])
    wait_ring(yb, sent.at[2])
    wait_ring(zb, sent.at[3])
    arrived(mixb.at[pl.ds(0, 3)], sent.at[4])
    arrived(fin.at[0], recv.at[4])
    out[...] = jnp.concatenate([fin[0], fin[1]], axis=0).astype(BF16)
    arrived(fin.at[0], sent.at[5])


def hand_out(o_in, k_in, v_in, o_out, k_out, v_out, sem):
    pairs = ((k_in, k_out), (v_in, v_out), (o_in, o_out))
    copies = [pltpu.make_async_copy(a, b, sem.at[i]) for i, (a, b) in enumerate(pairs)]
    for copy in copies:
        copy.start()
    for copy in copies:
        copy.wait()


def body(hidden_in, w_qkv, w_out, key_cache, value_cache, lengths, ln_gain, ln_bias):
    hbm = pl.BlockSpec(memory_space=pl.ANY)
    vmem = pl.BlockSpec(memory_space=pltpu.VMEM)
    cache = (B, SPAN, W)
    dma = pltpu.SemaphoreType.DMA
    done = pl.pallas_call(
        kernel,
        out_shape=(pltpu.VMEM((B, W), BF16), pltpu.VMEM(cache, BF16), pltpu.VMEM(cache, BF16)),
        in_specs=[hbm] * 8,
        out_specs=(vmem, vmem, vmem),
        scratch_shapes=[
            pltpu.SMEM((B,), jnp.int32),
            pltpu.VMEM((TP, B, W), BF16),
            pltpu.VMEM((3, D, W), BF16),
            pltpu.VMEM((W, D), BF16),
            pltpu.VMEM((1, W), F32),
            pltpu.VMEM((1, W), F32),
            pltpu.VMEM((2, 3, HALF, W), F32),
            pltpu.VMEM((3, HALF, W), F32),
            pltpu.VMEM((RING * SLOT, 128), F32),
            pltpu.VMEM((RING * SLOT, 128), F32),
            pltpu.VMEM((TP, HALF, D), F32),
            pltpu.VMEM((2, HALF, W), F32),
            dma((9,)), dma((3,)), dma((5,)), dma((6,)),
        ],
        compiler_params=pltpu.CompilerParams(collective_id=0, has_side_effects=True),
        name="sublayer",
    )(
        lengths, hidden_in, w_qkv, w_out, key_cache, value_cache,
        ln_gain.reshape(1, W), ln_bias.reshape(1, W),
    )
    return pl.pallas_call(
        hand_out,
        out_shape=(
            jax.ShapeDtypeStruct((B, W), BF16),
            jax.ShapeDtypeStruct(cache, BF16),
            jax.ShapeDtypeStruct(cache, BF16),
        ),
        in_specs=[vmem] * 3,
        out_specs=(hbm, hbm, hbm),
        scratch_shapes=[dma((3,))],
        name="hand_out",
    )(*[pltpu.with_memory_space_constraint(part, pltpu.VMEM) for part in done])


def solution(mesh):
    in_specs = (
        P(None, "tp"),
        P(None, None, "tp"),
        P("tp", None),
        P(None, "seq", "tp"),
        P(None, "seq", "tp"),
        P(),
        P("tp"),
        P("tp"),
    )
    out_specs = (P(None, "tp"), P(None, "seq", "tp"), P(None, "seq", "tp"))
    return jax.shard_map(body, mesh=mesh, in_specs=in_specs, out_specs=out_specs, check_vma=False)
```

```python
import jax
import jax.numpy as jnp
from jax import lax
from jax.experimental import pallas as pl
from jax.experimental.pallas import tpu as pltpu
from jax.sharding import PartitionSpec as P

D = 1024
HD = 64
B = 16
HALF = 8
W = 256
TP = 4
RING = 8
SPAN = 64
SLOT = 24
SENT = 17
NEG = -1e30
F32 = jnp.float32
BF16 = jnp.bfloat16
MESH = pl.DeviceIdType.MESH


def iota(shape, dim):
    return lax.broadcasted_iota(jnp.int32, shape, dim)


def split_dot(rows, matrix):
    upper = rows.astype(BF16)
    lower = (rows - upper.astype(F32)).astype(BF16)
    both = jnp.dot(jnp.concatenate([upper, lower], axis=0), matrix, preferred_element_type=F32)
    return both[: rows.shape[0]] + both[rows.shape[0] :]


def to_row(tops, totals):
    lane, request = iota((HALF, W), 1) % HD, iota((HALF, W), 0)
    picked = jnp.where(lane == request, tops, jnp.where(lane == request + HALF, totals, 0.0))
    row = jnp.sum(picked, axis=0, keepdims=True)
    return row[:, :128] + pltpu.roll(row[:, 128:], 16, 1)


def spread_rows(rows):
    entry = iota((HALF, 128), 1)
    keep = jnp.logical_and(entry % 16 == iota((HALF, 128), 0), entry % 64 < 32)
    picked = jnp.concatenate(
        [jnp.where(keep, rows[s : s + 1], 0.0) for s in range(rows.shape[0])], axis=0
    )
    lane, column = iota((128, W), 0), iota((128, W), 1)
    head = lane // 64 + 2 * ((lane % 64) // 16)
    matrix = jnp.where(jnp.logical_and(lane % 64 < 32, head == column // HD), 1.0, 0.0).astype(BF16)
    return split_dot(picked, matrix)


def kernel(
    lengths, hid, wqkv, wout, kc, vc, gain, bias,
    out, kbuf, vbuf,
    lens, gath, qkv, wbuf, wobuf, gbuf, bbuf,
    csend, crecv, yb, zb, mixb, fin,
    lsem, hsem, recv, sent, ready,
):
    seq = lax.axis_index("seq")
    tp = lax.axis_index("tp")
    y, z, c = seq // 16, (seq % 16) // 2, seq % 2

    is_src = jnp.logical_or(z == 0, z == 3)
    loads = [
        pltpu.make_async_copy(hid, gath.at[tp], lsem.at[0]),
        pltpu.make_async_copy(wqkv, wbuf, lsem.at[1]),
        pltpu.make_async_copy(kc, kbuf, lsem.at[2]),
        pltpu.make_async_copy(vc, vbuf, lsem.at[3]),
        pltpu.make_async_copy(lengths, lens, lsem.at[4]),
        pltpu.make_async_copy(wout, wobuf, lsem.at[5]),
        pltpu.make_async_copy(gain, gbuf, lsem.at[6]),
        pltpu.make_async_copy(bias, bbuf, lsem.at[7]),
    ]

    def at_z(other):
        return (y * 16 + other * 2 + c, tp)

    tp_peers = [(seq, lax.rem(tp + d, TP)) for d in (2, 1, 3)]
    y_peers = [(lax.rem(y + d, RING) * 16 + z * 2 + c, tp) for d in (4, 3, 5, 2, 6, 1, 7)]
    z_peers = [at_z(lax.rem(z + d, RING)) for d in (4, 3, 5, 2, 6, 1, 7)]
    sibling = (y * 16 + z * 2 + (1 - c), tp)

    step = jnp.where(z == 3, 1, RING - 1)
    served = [
        at_z(lax.rem(z + RING - step, RING)),
        at_z(lax.rem(z + step, RING)),
        at_z(lax.rem(z + 2 * step, RING)),
    ]
    my_src = jnp.where(jnp.logical_or(z == 1, z >= 6), 0, 3)
    my_index = jnp.where(z <= 2, 0, jnp.where(jnp.logical_or(z == 4, z == 7), 1, 2))
    def signal(sem, peer):
        pl.semaphore_signal(sem, inc=1, device_id=peer, device_id_type=MESH)

    barrier = pltpu.get_barrier_semaphore()

    def push(src, dst, stage, recv_sem, peer):
        pltpu.make_async_remote_copy(
            src, dst, sent.at[stage], recv_sem, device_id=peer, device_id_type=MESH
        ).start()

    def arrived(ref, sem):
        pltpu.make_async_copy(ref, ref, sem).wait()

    def project(index, t):
        rows = pl.ds(pl.multiple_of(t * W, W), W)
        return jnp.dot(gath[t], wbuf[index, rows, :], preferred_element_type=F32)

    @pl.when(is_src)
    def _():
        for peer in tp_peers + [sibling, at_z(3 - z)] + y_peers:
            signal(barrier, peer)
        for load in loads:
            load.start()
        loads[0].wait()
        pl.semaphore_wait(barrier, 12)
        for i, peer in enumerate(tp_peers):
            push(gath.at[tp], gath.at[tp], 0, hsem.at[i], peer)
        for peer in served:
            signal(barrier, peer)
        loads[1].wait()
        acc = [project(index, tp) for index in range(3)]
        for i, d in ((1, 1), (2, 3), (0, 2)):
            t = lax.rem(tp + TP - d, TP)
            arrived(gath.at[t], hsem.at[i])
            acc = [acc[index] + project(index, t) for index in range(3)]
        for index in range(3):
            qkv[index] = acc[index].astype(BF16)
        for i in (1, 2, 0):
            pl.semaphore_wait(ready.at[i], 1)
            push(qkv.at[0], qkv.at[0], 6, recv.at[5], served[i])
            push(qkv.at[pl.ds(1, 2)], qkv.at[pl.ds(1, 2)], 7, recv.at[6], served[i])
        signal(ready.at[3], sibling)
        for peer in y_peers + tp_peers + [at_z(3 - z)]:
            signal(ready.at[4], peer)

    @pl.when(jnp.logical_not(is_src))
    def _():
        pl.semaphore_wait(barrier, 1)
        signal(ready.at[my_index], at_z(my_src))
        for index, load in enumerate(loads):
            if index != 1:
                load.start()
        arrived(qkv.at[0], recv.at[5])

    query = qkv[0]

    column_head = iota((B, W), 1) // HD
    spread = jnp.concatenate(
        [jnp.where(column_head == h, query.astype(F32), 0.0) for h in range(4)], axis=0
    ).astype(BF16)
    row_b = iota((B, 1), 0)
    loads[4].wait()
    local_len = jnp.zeros((B, 1), jnp.int32)
    for b in range(B):
        local_len = jnp.where(row_b == b, lens[b] - seq * SPAN, local_len)
    low = jnp.concatenate([row_b * SPAN] * 4, axis=0)
    high = low + jnp.concatenate([jnp.clip(local_len, 0, SPAN)] * 4, axis=0)
    column = iota((4 * B, B * SPAN), 1)
    valid = jnp.logical_and(column >= low, column < high)
    loads[2].wait()
    keys = kbuf[...].reshape(B * SPAN, W)
    scores = lax.dot_general(spread, keys, (((1,), (1,)), ((), ())), preferred_element_type=F32)
    scores = jnp.where(valid, scores * HD ** (-0.5), NEG)
    top = jnp.max(scores, axis=1, keepdims=True)
    weights = jnp.where(valid, jnp.exp(scores - top), 0.0)
    total = jnp.sum(weights, axis=1, keepdims=True)
    loads[3].wait()
    summed = split_dot(weights, vbuf[...].reshape(B * SPAN, W))

    def fold(rows):
        result = jnp.broadcast_to(rows[0:B], (B, W))
        for h in range(1, 4):
            result = jnp.where(column_head == h, rows[h * B : (h + 1) * B], result)
        return result

    for core in range(2):
        for i, part in enumerate((fold(summed), fold(total), fold(top))):
            csend[core, i] = part[core * HALF : (core + 1) * HALF]

    @pl.when(is_src)
    def _():
        pl.semaphore_wait(ready.at[3], 1)
        for peer in served:
            signal(ready.at[5], peer)

    @pl.when(jnp.logical_not(is_src))
    def _():
        pl.semaphore_wait(ready.at[5], 1)

    push(csend.at[1 - c], crecv, 1, recv.at[0], sibling)

    arrived(crecv, recv.at[0])
    my_acc, my_total, my_top = csend[c, 0], csend[c, 1], csend[c, 2]
    both_top = jnp.maximum(my_top, crecv[2])
    mine, other = jnp.exp(my_top - both_top), jnp.exp(crecv[2] - both_top)
    both_acc = my_acc * mine + crecv[0] * other
    both_total = my_total * mine + crecv[1] * other

    def place(ref, slot, acc, row):
        base = pl.multiple_of(slot * SLOT, 8)
        ref[pl.ds(base, 8), :] = acc[:, :128]
        ref[pl.ds(base + 8, 8), :] = acc[:, 128:]
        ref[pl.ds(base + 16, 1), :] = row

    def slot_of(ref, slot, rows=SENT):
        return ref.at[pl.ds(pl.multiple_of(slot * SLOT, 8), rows), :]

    def wait_ring(ref, sem):
        arrived(ref.at[pl.ds(0, 7 * SENT), :], sem)

    def ring_acc(ref, factors):
        acc = None
        for s in range(RING):
            part = jnp.concatenate(
                [ref[s * SLOT : s * SLOT + 8, :], ref[s * SLOT + 8 : s * SLOT + 16, :]], axis=1
            ) * factors[s * 8 : s * 8 + 8]
            acc = part if acc is None else acc + part
        return acc

    place(yb, y, both_acc, to_row(both_top, both_total))

    @pl.when(is_src)
    def _():
        pl.semaphore_wait(ready.at[4], 11)
        for peer in served:
            signal(ready.at[6], peer)

    @pl.when(jnp.logical_not(is_src))
    def _():
        pl.semaphore_wait(ready.at[6], 1)

    for peer in y_peers:
        push(slot_of(yb, y), slot_of(yb, y), 2, recv.at[1], peer)

    @pl.when(jnp.logical_not(is_src))
    def _():
        loads[0].wait()
        arrived(qkv.at[pl.ds(1, 2)], recv.at[6])

    new_key, new_value = qkv[1], qkv[2]
    same_head = iota((W, W), 0) // HD == iota((W, W), 1) // HD
    new_score = split_dot(
        query.astype(F32) * new_key.astype(F32), jnp.where(same_head, 1.0, 0.0).astype(BF16)
    ) * HD ** (-0.5)

    def own_half(rows):
        return jnp.where(c == 0, rows[:HALF], rows[HALF:])

    new_row = to_row(own_half(new_score), jnp.ones((HALF, W), F32))
    new_acc = own_half(new_value.astype(F32))
    position = iota((SPAN, W), 0)
    for b in range(B):
        hit = position == lens[b] - seq * SPAN
        kbuf[b] = jnp.where(hit, new_key[b : b + 1].astype(F32), kbuf[b].astype(F32)).astype(BF16)
        vbuf[b] = jnp.where(hit, new_value[b : b + 1].astype(F32), vbuf[b].astype(F32)).astype(BF16)
    wait_ring(yb, recv.at[1])
    max_lane = iota((1, 128), 1) % 16 < 8
    rows = yb[pl.ds(16, RING, stride=SLOT), :]
    ring_top = jnp.max(rows, axis=0, keepdims=True)
    factor = jnp.exp(rows - ring_top)
    ring_total = jnp.sum(rows * pltpu.roll(factor, 8, 1), axis=0, keepdims=True)
    place(zb, z, ring_acc(yb, spread_rows(factor)), jnp.where(max_lane, ring_top, ring_total))
    for peer in z_peers:
        push(slot_of(zb, z), slot_of(zb, z), 3, recv.at[2], peer)

    loads[5].wait()
    loads[6].wait()
    loads[7].wait()

    wait_ring(zb, recv.at[2])
    rows = zb[pl.ds(16, RING, stride=SLOT), :]
    last_top = jnp.maximum(jnp.max(rows, axis=0, keepdims=True), new_row)
    factor = jnp.exp(rows - last_top)
    new_factor = jnp.exp(new_row - last_top)
    last_total = jnp.sum(rows * pltpu.roll(factor, 8, 1), axis=0, keepdims=True)
    last_total = last_total + new_row * pltpu.roll(new_factor, 8, 1)
    share = pltpu.roll(last_total, 120, 1)
    factors = spread_rows(jnp.concatenate([factor / share, new_factor / share], axis=0))
    attended = ring_acc(zb, factors) + new_acc * factors[RING * 8 :]
    mixb[tp] = jnp.dot(attended.astype(BF16), wobuf[...], preferred_element_type=F32)
    own_columns = pl.ds(pl.multiple_of(tp * W, W), W)
    mixb[tp, :, own_columns] = mixb[tp, :, own_columns] + own_half(gath[tp].astype(F32))
    for peer in tp_peers:
        push(mixb.at[tp], mixb.at[tp], 4, recv.at[3], peer)
    arrived(mixb.at[pl.ds(0, 3)], recv.at[3])
    resid = []
    for t in range(TP):
        lanes = slice(t * W, (t + 1) * W)
        resid.append((mixb[0, :, lanes] + mixb[1, :, lanes]) + (mixb[2, :, lanes] + mixb[3, :, lanes]))
    mean = jnp.sum((resid[0] + resid[1]) + (resid[2] + resid[3]), axis=1, keepdims=True) / D
    centred = [part - mean for part in resid]
    square = [part * part for part in centred]
    var = jnp.sum((square[0] + square[1]) + (square[2] + square[3]), axis=1, keepdims=True) / D
    own = centred[0]
    for t in range(1, TP):
        own = jnp.where(tp == t, centred[t], own)
    fin[c] = own / jnp.sqrt(var + 1e-05) * gbuf[...] + bbuf[...]
    push(fin.at[c], fin.at[c], 5, recv.at[4], sibling)

    @pl.when(is_src)
    def _():
        arrived(gath.at[pl.ds(0, 3)], sent.at[0])
        arrived(qkv, sent.at[6])
        arrived(wbuf.at[0, pl.ds(0, 6 * B), :], sent.at[7])

    arrived(crecv, sent.at[1])
    wait_ring(yb, sent.at[2])
    wait_ring(zb, sent.at[3])
    arrived(mixb.at[pl.ds(0, 3)], sent.at[4])
    arrived(fin.at[0], recv.at[4])
    out[...] = jnp.concatenate([fin[0], fin[1]], axis=0).astype(BF16)
    arrived(fin.at[0], sent.at[5])


def hand_out(o_in, k_in, v_in, o_out, k_out, v_out, sem):
    pairs = ((k_in, k_out), (v_in, v_out), (o_in, o_out))
    copies = [pltpu.make_async_copy(a, b, sem.at[i]) for i, (a, b) in enumerate(pairs)]
    for copy in copies:
        copy.start()
    for copy in copies:
        copy.wait()


def body(hidden_in, w_qkv, w_out, key_cache, value_cache, lengths, ln_gain, ln_bias):
    hbm = pl.BlockSpec(memory_space=pl.ANY)
    vmem = pl.BlockSpec(memory_space=pltpu.VMEM)
    cache = (B, SPAN, W)
    dma = pltpu.SemaphoreType.DMA
    done = pl.pallas_call(
        kernel,
        out_shape=(pltpu.VMEM((B, W), BF16), pltpu.VMEM(cache, BF16), pltpu.VMEM(cache, BF16)),
        in_specs=[hbm] * 8,
        out_specs=(vmem, vmem, vmem),
        scratch_shapes=[
            pltpu.SMEM((B,), jnp.int32),
            pltpu.VMEM((TP, B, W), BF16),
            pltpu.VMEM((3, B, W), BF16),
            pltpu.VMEM((3, D, W), BF16),
            pltpu.VMEM((W, D), BF16),
            pltpu.VMEM((1, W), F32),
            pltpu.VMEM((1, W), F32),
            pltpu.VMEM((2, 3, HALF, W), F32),
            pltpu.VMEM((3, HALF, W), F32),
            pltpu.VMEM((RING * SLOT, 128), F32),
            pltpu.VMEM((RING * SLOT, 128), F32),
            pltpu.VMEM((TP, HALF, D), F32),
            pltpu.VMEM((2, HALF, W), F32),
            dma((8,)), dma((3,)), dma((7,)), dma((8,)), pltpu.SemaphoreType.REGULAR((7,)),
        ],
        compiler_params=pltpu.CompilerParams(collective_id=0, has_side_effects=True),
        name="sublayer",
    )(
        lengths, hidden_in, w_qkv, w_out, key_cache, value_cache,
        ln_gain.reshape(1, W), ln_bias.reshape(1, W),
    )
    return pl.pallas_call(
        hand_out,
        out_shape=(
            jax.ShapeDtypeStruct((B, W), BF16),
            jax.ShapeDtypeStruct(cache, BF16),
            jax.ShapeDtypeStruct(cache, BF16),
        ),
        in_specs=[vmem] * 3,
        out_specs=(hbm, hbm, hbm),
        scratch_shapes=[dma((3,))],
        name="hand_out",
    )(*[pltpu.with_memory_space_constraint(part, pltpu.VMEM) for part in done])


def solution(mesh):
    in_specs = (
        P(None, "tp"),
        P(None, None, "tp"),
        P("tp", None),
        P(None, "seq", "tp"),
        P(None, "seq", "tp"),
        P(),
        P("tp"),
        P("tp"),
    )
    out_specs = (P(None, "tp"), P(None, "seq", "tp"), P(None, "seq", "tp"))
    return jax.shard_map(body, mesh=mesh, in_specs=in_specs, out_specs=out_specs, check_vma=False)
```

```python
import jax
import jax.numpy as jnp
from jax import lax
from jax.experimental import pallas as pl
from jax.experimental.pallas import tpu as pltpu
from jax.sharding import PartitionSpec as P

D = 1024
HD = 64
B = 16
HALF = 8
W = 256
TP = 4
RING = 8
SPAN = 64
SLOT = 16
SENT = 9
NEG = -1e30
F32 = jnp.float32
BF16 = jnp.bfloat16
MESH = pl.DeviceIdType.MESH


def iota(shape, dim):
    return lax.broadcasted_iota(jnp.int32, shape, dim)


def split_dot(rows, matrix):
    upper = rows.astype(BF16)
    lower = (rows - upper.astype(F32)).astype(BF16)
    both = jnp.dot(jnp.concatenate([upper, lower], axis=0), matrix, preferred_element_type=F32)
    return both[: rows.shape[0]] + both[rows.shape[0] :]


def to_row(tops, totals):
    lane, request = iota((HALF, W), 1) % HD, iota((HALF, W), 0)
    picked = jnp.where(lane == request, tops, jnp.where(lane == request + HALF, totals, 0.0))
    row = jnp.sum(picked, axis=0, keepdims=True)
    return row[:, :128], row[:, 128:]


def kernel(
    lengths, hid, wqkv, wout, kc, vc, gain, bias,
    out, kbuf, vbuf,
    lens, gath, wbuf, wobuf, gbuf, bbuf,
    csend, crecv, yb, zb, mixb, fin,
    lsem, hsem, recv, sent,
):
    seq = lax.axis_index("seq")
    tp = lax.axis_index("tp")
    y, z, c = seq // 16, (seq % 16) // 2, seq % 2

    loads = [
        pltpu.make_async_copy(hid, gath.at[tp], lsem.at[0]),
        pltpu.make_async_copy(wqkv.at[0], wbuf.at[0], lsem.at[1]),
        pltpu.make_async_copy(kc, kbuf, lsem.at[2]),
        pltpu.make_async_copy(vc, vbuf, lsem.at[3]),
        pltpu.make_async_copy(wqkv.at[pl.ds(1, 2)], wbuf.at[pl.ds(1, 2)], lsem.at[4]),
        pltpu.make_async_copy(wout, wobuf, lsem.at[5]),
        pltpu.make_async_copy(gain, gbuf, lsem.at[6]),
        pltpu.make_async_copy(bias, bbuf, lsem.at[7]),
        pltpu.make_async_copy(lengths, lens, lsem.at[8]),
    ]
    for load in loads:
        load.start()

    tp_peers = [(seq, lax.rem(tp + d, TP)) for d in (2, 1, 3)]
    y_peers = [(lax.rem(y + d, RING) * 16 + z * 2 + c, tp) for d in (4, 3, 5, 2, 6, 1, 7)]
    z_peers = [(y * 16 + lax.rem(z + d, RING) * 2 + c, tp) for d in (4, 3, 5, 2, 6, 1, 7)]
    sibling = (y * 16 + z * 2 + (1 - c), tp)

    barrier = pltpu.get_barrier_semaphore()
    for peer in tp_peers + [sibling] + y_peers + z_peers:
        pl.semaphore_signal(barrier, inc=1, device_id=peer, device_id_type=MESH)
    loads[0].wait()
    pl.semaphore_wait(barrier, 18)

    def push(src, dst, stage, recv_sem, peer):
        pltpu.make_async_remote_copy(
            src, dst, sent.at[stage], recv_sem, device_id=peer, device_id_type=MESH
        ).start()

    def arrived(ref, sem):
        pltpu.make_async_copy(ref, ref, sem).wait()

    for i, peer in enumerate(tp_peers):
        push(gath.at[tp], gath.at[tp], 0, hsem.at[i], peer)
    loads[1].wait()

    def project(index, t):
        rows = pl.ds(pl.multiple_of(t * W, W), W)
        return jnp.dot(gath[t], wbuf[index, rows, :], preferred_element_type=F32)

    column_head = iota((B, W), 1) // HD
    row_b = iota((B, 1), 0)
    loads[8].wait()
    local_len = jnp.zeros((B, 1), jnp.int32)
    for b in range(B):
        local_len = jnp.where(row_b == b, lens[b] - seq * SPAN, local_len)
    row_len = jnp.concatenate([local_len] * 4, axis=0)
    request = iota((4 * B, 128), 0) % B
    lane = iota((4 * B, 128), 1)
    valid = jnp.logical_and(lane // SPAN == request % 2, lane % SPAN < row_len)
    pair = request // 2
    same_head = jnp.where(iota((128, 128), 0) // HD == iota((128, 128), 1) // HD, 1.0, 0.0).astype(BF16)

    acc = project(0, tp)
    for i, d in ((1, 1), (2, 3), (0, 2)):
        t = lax.rem(tp + TP - d, TP)
        arrived(gath.at[t], hsem.at[i])
        acc = acc + project(0, t)
    query = acc.astype(BF16)

    spread = jnp.concatenate(
        [jnp.where(column_head == h, query.astype(F32), 0.0) for h in range(4)], axis=0
    ).astype(BF16)
    loads[2].wait()
    keys = kbuf[...].reshape(B * SPAN, W)
    every = lax.dot_general(spread, keys, (((1,), (1,)), ((), ())), preferred_element_type=F32)
    scores = every[:, :128]
    for j in range(1, 8):
        scores = jnp.where(pair == j, every[:, j * 128 : j * 128 + 128], scores)
    scores = jnp.where(valid, scores * HD ** (-0.5), NEG)
    top = jnp.max(scores, axis=1, keepdims=True)
    weights = jnp.where(valid, jnp.exp(scores - top), 0.0)
    total = jnp.sum(weights, axis=1, keepdims=True)
    upper = weights.astype(BF16).astype(F32)
    lower = weights - upper
    wide = jnp.concatenate(
        [
            jnp.concatenate([jnp.where(pair == j, part, 0.0).astype(BF16) for j in range(8)], axis=1)
            for part in (upper, lower)
        ],
        axis=0,
    )
    loads[3].wait()
    both = jnp.dot(wide, vbuf[...].reshape(B * SPAN, W), preferred_element_type=F32)
    summed = both[: 4 * B] + both[4 * B :]

    def fold(rows):
        result = jnp.broadcast_to(rows[0:B], (B, W))
        for h in range(1, 4):
            result = jnp.where(column_head == h, rows[h * B : (h + 1) * B], result)
        return result

    for core in range(2):
        for i, part in enumerate((fold(summed), fold(total), fold(top))):
            csend[core, i] = part[core * HALF : (core + 1) * HALF]
    push(csend.at[1 - c], crecv, 1, recv.at[0], sibling)

    loads[4].wait()
    new_key = sum(project(1, t) for t in range(TP)).astype(BF16)
    new_value = sum(project(2, t) for t in range(TP)).astype(BF16)

    arrived(crecv, recv.at[0])
    my_acc, my_total, my_top = csend[c, 0], csend[c, 1], csend[c, 2]
    both_top = jnp.maximum(my_top, crecv[2])
    mine, other = jnp.exp(my_top - both_top), jnp.exp(crecv[2] - both_top)
    both_acc = my_acc * mine + crecv[0] * other
    both_total = my_total * mine + crecv[1] * other

    def place(ref, slot, acc, row):
        base = pl.multiple_of(slot * SLOT, 8)
        ref[pl.ds(base, 8), :] = acc
        ref[pl.ds(base + 8, 1), :] = row

    def slot_of(ref, slot):
        return ref.at[pl.ds(pl.multiple_of(slot * SLOT, 8), SENT), :]

    def wait_ring(ref, sem):
        arrived(ref.at[pl.ds(0, 14 * SENT), :], sem)

    def push_ring(ref, slot_y, slot_z, stage, recv_sem):
        for y_peer, z_peer in zip(y_peers, z_peers):
            push(slot_of(ref, slot_y), slot_of(ref, slot_y), stage, recv_sem, y_peer)
            push(slot_of(ref, slot_z), slot_of(ref, slot_z), stage, recv_sem, z_peer)

    def spread_rows(rows):
        keep = iota((HALF, 128), 1) % HD == iota((HALF, 128), 0)
        return split_dot(
            jnp.concatenate(
                [jnp.where(keep, rows[s : s + 1], 0.0) for s in range(rows.shape[0])], axis=0
            ),
            same_head,
        )

    def ring_acc(ref, factors, first):
        acc = None
        for s in range(first, first + RING):
            part = ref[s * SLOT : s * SLOT + 8, :] * factors[s * 8 : s * 8 + 8]
            acc = part if acc is None else acc + part
        return acc

    def over(first, second):
        return jnp.where(iota((2 * RING, 128), 0) < RING, first, second)

    low_row, high_row = to_row(both_top, both_total)
    place(yb, y, both_acc[:, :128], low_row)
    place(yb, RING + z, both_acc[:, 128:], high_row)
    push_ring(yb, y, RING + z, 2, recv.at[1])

    product = query.astype(F32) * new_key.astype(F32)
    halves = split_dot(jnp.concatenate([product[:, :128], product[:, 128:]], axis=0), same_head)
    new_score = jnp.concatenate([halves[:B], halves[B:]], axis=1) * HD ** (-0.5)

    def own_half(rows):
        return jnp.where(c == 0, rows[:HALF], rows[HALF:])

    new_low, new_high = to_row(own_half(new_score), jnp.ones((HALF, W), F32))
    new_acc = own_half(new_value.astype(F32))
    position = iota((SPAN, W), 0)
    for b in range(B):
        hit = position == lens[b] - seq * SPAN
        kbuf[b] = jnp.where(hit, new_key[b : b + 1].astype(F32), kbuf[b].astype(F32)).astype(BF16)
        vbuf[b] = jnp.where(hit, new_value[b : b + 1].astype(F32), vbuf[b].astype(F32)).astype(BF16)
    max_lane = iota((1, 128), 1) % HD < HALF
    wait_ring(yb, recv.at[1])
    rows = yb[pl.ds(8, 2 * RING, stride=SLOT), :]
    low_top = jnp.max(rows[:RING], axis=0, keepdims=True)
    high_top = jnp.max(rows[RING:], axis=0, keepdims=True)
    factor = jnp.exp(rows - over(low_top, high_top))
    totals = rows * pltpu.roll(factor, HALF, 1)
    low_total = jnp.sum(totals[:RING], axis=0, keepdims=True)
    high_total = jnp.sum(totals[RING:], axis=0, keepdims=True)
    factors = spread_rows(factor)
    place(zb, z, ring_acc(yb, factors, 0), jnp.where(max_lane, low_top, low_total))
    place(zb, RING + y, ring_acc(yb, factors, RING), jnp.where(max_lane, high_top, high_total))
    push_ring(zb, RING + y, z, 3, recv.at[2])

    state = [own_half(gath[t].astype(F32)) for t in range(TP)]
    loads[5].wait()
    loads[6].wait()
    loads[7].wait()

    wait_ring(zb, recv.at[2])
    rows = zb[pl.ds(8, 2 * RING, stride=SLOT), :]
    low_top = jnp.maximum(jnp.max(rows[:RING], axis=0, keepdims=True), new_low)
    high_top = jnp.maximum(jnp.max(rows[RING:], axis=0, keepdims=True), new_high)
    factor = jnp.exp(rows - over(low_top, high_top))
    totals = rows * pltpu.roll(factor, HALF, 1)
    low_new, high_new = jnp.exp(new_low - low_top), jnp.exp(new_high - high_top)
    low_total = jnp.sum(totals[:RING], axis=0, keepdims=True) + new_low * pltpu.roll(low_new, HALF, 1)
    high_total = jnp.sum(totals[RING:], axis=0, keepdims=True) + new_high * pltpu.roll(high_new, HALF, 1)
    low_share, high_share = pltpu.roll(low_total, 128 - HALF, 1), pltpu.roll(high_total, 128 - HALF, 1)
    factors = spread_rows(
        jnp.concatenate(
            [factor / over(low_share, high_share), low_new / low_share, high_new / high_share], axis=0
        )
    )
    attended = jnp.concatenate(
        [
            ring_acc(zb, factors, 0) + new_acc[:, :128] * factors[128:136],
            ring_acc(zb, factors, RING) + new_acc[:, 128:] * factors[136:144],
        ],
        axis=1,
    )
    mixb[tp] = jnp.dot(attended.astype(BF16), wobuf[...], preferred_element_type=F32)
    for peer in tp_peers:
        push(mixb.at[tp], mixb.at[tp], 4, recv.at[3], peer)
    arrived(mixb.at[pl.ds(0, 3)], recv.at[3])
    resid = []
    for t in range(TP):
        lanes = slice(t * W, (t + 1) * W)
        resid.append(
            state[t] + ((mixb[0, :, lanes] + mixb[1, :, lanes]) + (mixb[2, :, lanes] + mixb[3, :, lanes]))
        )
    mean = jnp.sum((resid[0] + resid[1]) + (resid[2] + resid[3]), axis=1, keepdims=True) / D
    centred = [part - mean for part in resid]
    square = [part * part for part in centred]
    var = jnp.sum((square[0] + square[1]) + (square[2] + square[3]), axis=1, keepdims=True) / D
    own = centred[0]
    for t in range(1, TP):
        own = jnp.where(tp == t, centred[t], own)
    fin[c] = own / jnp.sqrt(var + 1e-05) * gbuf[...] + bbuf[...]
    push(fin.at[c], fin.at[c], 5, recv.at[4], sibling)

    arrived(gath.at[pl.ds(0, 3)], sent.at[0])
    arrived(crecv, sent.at[1])
    wait_ring(yb, sent.at[2])
    wait_ring(zb, sent.at[3])
    arrived(mixb.at[pl.ds(0, 3)], sent.at[4])
    arrived(fin.at[0], recv.at[4])
    out[...] = jnp.concatenate([fin[0], fin[1]], axis=0).astype(BF16)
    arrived(fin.at[0], sent.at[5])


def hand_out(o_in, k_in, v_in, o_out, k_out, v_out, sem):
    pairs = ((k_in, k_out), (v_in, v_out), (o_in, o_out))
    copies = [pltpu.make_async_copy(a, b, sem.at[i]) for i, (a, b) in enumerate(pairs)]
    for copy in copies:
        copy.start()
    for copy in copies:
        copy.wait()


def body(hidden_in, w_qkv, w_out, key_cache, value_cache, lengths, ln_gain, ln_bias):
    hbm = pl.BlockSpec(memory_space=pl.ANY)
    vmem = pl.BlockSpec(memory_space=pltpu.VMEM)
    cache = (B, SPAN, W)
    dma = pltpu.SemaphoreType.DMA
    done = pl.pallas_call(
        kernel,
        out_shape=(pltpu.VMEM((B, W), BF16), pltpu.VMEM(cache, BF16), pltpu.VMEM(cache, BF16)),
        in_specs=[hbm] * 8,
        out_specs=(vmem, vmem, vmem),
        scratch_shapes=[
            pltpu.SMEM((B,), jnp.int32),
            pltpu.VMEM((TP, B, W), BF16),
            pltpu.VMEM((3, D, W), BF16),
            pltpu.VMEM((W, D), BF16),
            pltpu.VMEM((1, W), F32),
            pltpu.VMEM((1, W), F32),
            pltpu.VMEM((2, 3, HALF, W), F32),
            pltpu.VMEM((3, HALF, W), F32),
            pltpu.VMEM((2 * RING * SLOT, 128), F32),
            pltpu.VMEM((2 * RING * SLOT, 128), F32),
            pltpu.VMEM((TP, HALF, D), F32),
            pltpu.VMEM((2, HALF, W), F32),
            dma((9,)), dma((3,)), dma((5,)), dma((6,)),
        ],
        compiler_params=pltpu.CompilerParams(collective_id=0, has_side_effects=True),
        name="sublayer",
    )(
        lengths, hidden_in, w_qkv, w_out, key_cache, value_cache,
        ln_gain.reshape(1, W), ln_bias.reshape(1, W),
    )
    return pl.pallas_call(
        hand_out,
        out_shape=(
            jax.ShapeDtypeStruct((B, W), BF16),
            jax.ShapeDtypeStruct(cache, BF16),
            jax.ShapeDtypeStruct(cache, BF16),
        ),
        in_specs=[vmem] * 3,
        out_specs=(hbm, hbm, hbm),
        scratch_shapes=[dma((3,))],
        name="hand_out",
    )(*[pltpu.with_memory_space_constraint(part, pltpu.VMEM) for part in done])


def solution(mesh):
    in_specs = (
        P(None, "tp"),
        P(None, None, "tp"),
        P("tp", None),
        P(None, "seq", "tp"),
        P(None, "seq", "tp"),
        P(),
        P("tp"),
        P("tp"),
    )
    out_specs = (P(None, "tp"), P(None, "seq", "tp"), P(None, "seq", "tp"))
    return jax.shard_map(body, mesh=mesh, in_specs=in_specs, out_specs=out_specs, check_vma=False)
```

```python
import jax
import jax.numpy as jnp
from jax import lax
from jax.experimental import pallas as pl
from jax.experimental.pallas import tpu as pltpu
from jax.sharding import PartitionSpec as P

D = 1024
HD = 64
B = 16
HALF = 8
W = 256
TP = 4
RING = 8
SPAN = 64
SLOT = 16
SENT = 9
NEG = -1e30
F32 = jnp.float32
BF16 = jnp.bfloat16
MESH = pl.DeviceIdType.MESH


def iota(shape, dim):
    return lax.broadcasted_iota(jnp.int32, shape, dim)


def split_dot(rows, matrix):
    upper = rows.astype(BF16)
    lower = (rows - upper.astype(F32)).astype(BF16)
    both = jnp.dot(jnp.concatenate([upper, lower], axis=0), matrix, preferred_element_type=F32)
    return both[: rows.shape[0]] + both[rows.shape[0] :]


def to_row(tops, totals):
    lane, request = iota((HALF, W), 1) % HD, iota((HALF, W), 0)
    picked = jnp.where(lane == request, tops, jnp.where(lane == request + HALF, totals, 0.0))
    row = jnp.sum(picked, axis=0, keepdims=True)
    return row[:, :128], row[:, 128:]


def kernel(
    lengths, hid, wqkv, wout, kc, vc, gain, bias,
    out, kbuf, vbuf,
    lens, gath, qkv, wbuf, wobuf, gbuf, bbuf,
    csend, crecv, yb, zb, mixb, fin,
    lsem, hsem, recv, sent,
):
    seq = lax.axis_index("seq")
    tp = lax.axis_index("tp")
    y, z, c = seq // 16, (seq % 16) // 2, seq % 2

    loads = [
        pltpu.make_async_copy(hid, gath.at[tp], lsem.at[0]),
        pltpu.make_async_copy(wqkv.at[0], wbuf.at[0], lsem.at[1]),
        pltpu.make_async_copy(kc, kbuf, lsem.at[2]),
        pltpu.make_async_copy(vc, vbuf, lsem.at[3]),
        pltpu.make_async_copy(wqkv.at[pl.ds(1, 2)], wbuf.at[pl.ds(1, 2)], lsem.at[4]),
        pltpu.make_async_copy(wout, wobuf, lsem.at[5]),
        pltpu.make_async_copy(gain, gbuf, lsem.at[6]),
        pltpu.make_async_copy(bias, bbuf, lsem.at[7]),
        pltpu.make_async_copy(lengths, lens, lsem.at[8]),
    ]
    tp_peers = [(seq, lax.rem(tp + d, TP)) for d in (2, 1, 3)]
    y_peers = [(lax.rem(y + d, RING) * 16 + z * 2 + c, tp) for d in (4, 3, 5, 2, 6, 1, 7)]
    z_peers = [(y * 16 + lax.rem(z + d, RING) * 2 + c, tp) for d in (4, 3, 5, 2, 6, 1, 7)]
    sibling = (y * 16 + z * 2 + (1 - c), tp)

    barrier = pltpu.get_barrier_semaphore()
    def signal(peer):
        pl.semaphore_signal(barrier, inc=1, device_id=peer, device_id_type=MESH)

    for peer in tp_peers:
        signal(peer)
    loads[0].start()
    for peer in [sibling] + z_peers + y_peers:
        signal(peer)

    @pl.when(c == 1)
    def _():
        loads[1].start()

    for index in (8, 2, 3, 5, 6, 7):
        loads[index].start()

    @pl.when(c == 1)
    def _():
        loads[4].start()

    loads[0].wait()
    pl.semaphore_wait(barrier, 18)

    def push(src, dst, stage, recv_sem, peer):
        pltpu.make_async_remote_copy(
            src, dst, sent.at[stage], recv_sem, device_id=peer, device_id_type=MESH
        ).start()

    def arrived(ref, sem):
        pltpu.make_async_copy(ref, ref, sem).wait()

    def project(index, t):
        rows = pl.ds(pl.multiple_of(t * W, W), W)
        return jnp.dot(gath[t], wbuf[index, rows, :], preferred_element_type=F32)

    @pl.when(c == 1)
    def _():
        for i, peer in enumerate(tp_peers):
            push(gath.at[tp], gath.at[tp], 0, hsem.at[i], peer)

    column_head = iota((B, W), 1) // HD
    row_b = iota((B, 1), 0)
    loads[8].wait()
    local_len = jnp.zeros((B, 1), jnp.int32)
    for b in range(B):
        local_len = jnp.where(row_b == b, lens[b] - seq * SPAN, local_len)
    row_len = jnp.concatenate([local_len] * 4, axis=0)
    request = iota((4 * B, 128), 0) % B
    lane = iota((4 * B, 128), 1)
    valid = jnp.logical_and(lane // SPAN == request % 2, lane % SPAN < row_len)
    pair = request // 2
    same_head = jnp.where(iota((128, 128), 0) // HD == iota((128, 128), 1) // HD, 1.0, 0.0).astype(BF16)

    @pl.when(c == 1)
    def _():
        loads[1].wait()
        acc = project(0, tp)
        for i, d in ((1, 1), (2, 3), (0, 2)):
            t = lax.rem(tp + TP - d, TP)
            arrived(gath.at[t], hsem.at[i])
            acc = acc + project(0, t)
        qkv[0] = acc.astype(BF16)
        push(qkv.at[0], qkv.at[0], 6, recv.at[5], sibling)

    @pl.when(c == 0)
    def _():
        arrived(qkv.at[0], recv.at[5])

    query = qkv[0]

    spread = jnp.concatenate(
        [jnp.where(column_head == h, query.astype(F32), 0.0) for h in range(4)], axis=0
    ).astype(BF16)
    loads[2].wait()
    keys = kbuf[...].reshape(B * SPAN, W)
    every = lax.dot_general(spread, keys, (((1,), (1,)), ((), ())), preferred_element_type=F32)
    scores = every[:, :128]
    for j in range(1, 8):
        scores = jnp.where(pair == j, every[:, j * 128 : j * 128 + 128], scores)
    scores = jnp.where(valid, scores * HD ** (-0.5), NEG)
    top = jnp.max(scores, axis=1, keepdims=True)
    weights = jnp.where(valid, jnp.exp(scores - top), 0.0)
    total = jnp.sum(weights, axis=1, keepdims=True)
    upper = weights.astype(BF16).astype(F32)
    lower = weights - upper
    wide = jnp.concatenate(
        [
            jnp.concatenate([jnp.where(pair == j, part, 0.0).astype(BF16) for j in range(8)], axis=1)
            for part in (upper, lower)
        ],
        axis=0,
    )
    loads[3].wait()
    both = jnp.dot(wide, vbuf[...].reshape(B * SPAN, W), preferred_element_type=F32)
    summed = both[: 4 * B] + both[4 * B :]

    def fold(rows):
        result = jnp.broadcast_to(rows[0:B], (B, W))
        for h in range(1, 4):
            result = jnp.where(column_head == h, rows[h * B : (h + 1) * B], result)
        return result

    for core in range(2):
        for i, part in enumerate((fold(summed), fold(total), fold(top))):
            csend[core, i] = part[core * HALF : (core + 1) * HALF]
    push(csend.at[1 - c], crecv, 1, recv.at[0], sibling)

    @pl.when(c == 1)
    def _():
        loads[4].wait()
        for index in (1, 2):
            qkv[index] = sum(project(index, t) for t in range(TP)).astype(BF16)
        push(qkv.at[pl.ds(1, 2)], qkv.at[pl.ds(1, 2)], 7, recv.at[6], sibling)

    arrived(crecv, recv.at[0])
    my_acc, my_total, my_top = csend[c, 0], csend[c, 1], csend[c, 2]
    both_top = jnp.maximum(my_top, crecv[2])
    mine, other = jnp.exp(my_top - both_top), jnp.exp(crecv[2] - both_top)
    both_acc = my_acc * mine + crecv[0] * other
    both_total = my_total * mine + crecv[1] * other

    def place(ref, slot, acc, row):
        base = pl.multiple_of(slot * SLOT, 8)
        ref[pl.ds(base, 8), :] = acc
        ref[pl.ds(base + 8, 1), :] = row

    def slot_of(ref, slot):
        return ref.at[pl.ds(pl.multiple_of(slot * SLOT, 8), SENT), :]

    def wait_ring(ref, sem):
        arrived(ref.at[pl.ds(0, 14 * SENT), :], sem)

    def push_ring(ref, slot_y, slot_z, stage, recv_sem):
        for y_peer, z_peer in zip(y_peers, z_peers):
            push(slot_of(ref, slot_y), slot_of(ref, slot_y), stage, recv_sem, y_peer)
            push(slot_of(ref, slot_z), slot_of(ref, slot_z), stage, recv_sem, z_peer)

    def spread_rows(rows):
        keep = iota((HALF, 128), 1) % HD == iota((HALF, 128), 0)
        return split_dot(
            jnp.concatenate(
                [jnp.where(keep, rows[s : s + 1], 0.0) for s in range(rows.shape[0])], axis=0
            ),
            same_head,
        )

    def ring_acc(ref, factors, first):
        acc = None
        for s in range(first, first + RING):
            part = ref[s * SLOT : s * SLOT + 8, :] * factors[s * 8 : s * 8 + 8]
            acc = part if acc is None else acc + part
        return acc

    def over(first, second):
        return jnp.where(iota((2 * RING, 128), 0) < RING, first, second)

    low_row, high_row = to_row(both_top, both_total)
    place(yb, y, both_acc[:, :128], low_row)
    place(yb, RING + z, both_acc[:, 128:], high_row)
    push_ring(yb, y, RING + z, 2, recv.at[1])

    @pl.when(c == 0)
    def _():
        arrived(qkv.at[pl.ds(1, 2)], recv.at[6])

    new_key, new_value = qkv[1], qkv[2]
    product = query.astype(F32) * new_key.astype(F32)
    halves = split_dot(jnp.concatenate([product[:, :128], product[:, 128:]], axis=0), same_head)
    new_score = jnp.concatenate([halves[:B], halves[B:]], axis=1) * HD ** (-0.5)

    def own_half(rows):
        return jnp.where(c == 0, rows[:HALF], rows[HALF:])

    new_low, new_high = to_row(own_half(new_score), jnp.ones((HALF, W), F32))
    new_acc = own_half(new_value.astype(F32))
    position = iota((SPAN, W), 0)
    for b in range(B):
        hit = position == lens[b] - seq * SPAN
        kbuf[b] = jnp.where(hit, new_key[b : b + 1].astype(F32), kbuf[b].astype(F32)).astype(BF16)
        vbuf[b] = jnp.where(hit, new_value[b : b + 1].astype(F32), vbuf[b].astype(F32)).astype(BF16)
    max_lane = iota((1, 128), 1) % HD < HALF
    wait_ring(yb, recv.at[1])
    rows = yb[pl.ds(8, 2 * RING, stride=SLOT), :]
    low_top = jnp.max(rows[:RING], axis=0, keepdims=True)
    high_top = jnp.max(rows[RING:], axis=0, keepdims=True)
    factor = jnp.exp(rows - over(low_top, high_top))
    totals = rows * pltpu.roll(factor, HALF, 1)
    low_total = jnp.sum(totals[:RING], axis=0, keepdims=True)
    high_total = jnp.sum(totals[RING:], axis=0, keepdims=True)
    factors = spread_rows(factor)
    place(zb, z, ring_acc(yb, factors, 0), jnp.where(max_lane, low_top, low_total))
    place(zb, RING + y, ring_acc(yb, factors, RING), jnp.where(max_lane, high_top, high_total))
    push_ring(zb, RING + y, z, 3, recv.at[2])

    own_hidden = own_half(gath[tp].astype(F32))
    loads[5].wait()
    loads[6].wait()
    loads[7].wait()

    wait_ring(zb, recv.at[2])
    rows = zb[pl.ds(8, 2 * RING, stride=SLOT), :]
    low_top = jnp.maximum(jnp.max(rows[:RING], axis=0, keepdims=True), new_low)
    high_top = jnp.maximum(jnp.max(rows[RING:], axis=0, keepdims=True), new_high)
    factor = jnp.exp(rows - over(low_top, high_top))
    totals = rows * pltpu.roll(factor, HALF, 1)
    low_new, high_new = jnp.exp(new_low - low_top), jnp.exp(new_high - high_top)
    low_total = jnp.sum(totals[:RING], axis=0, keepdims=True) + new_low * pltpu.roll(low_new, HALF, 1)
    high_total = jnp.sum(totals[RING:], axis=0, keepdims=True) + new_high * pltpu.roll(high_new, HALF, 1)
    low_share, high_share = pltpu.roll(low_total, 128 - HALF, 1), pltpu.roll(high_total, 128 - HALF, 1)
    factors = spread_rows(
        jnp.concatenate(
            [factor / over(low_share, high_share), low_new / low_share, high_new / high_share], axis=0
        )
    )
    attended = jnp.concatenate(
        [
            ring_acc(zb, factors, 0) + new_acc[:, :128] * factors[128:136],
            ring_acc(zb, factors, RING) + new_acc[:, 128:] * factors[136:144],
        ],
        axis=1,
    )
    attended = attended.astype(BF16)
    for half in range(2):
        lanes = slice(half * 2 * W, (half + 1) * 2 * W)
        mixed = jnp.dot(attended, wobuf[:, lanes], preferred_element_type=F32)
        for t in (2 * half, 2 * half + 1):
            part = mixed[:, t % 2 * W : (t % 2 + 1) * W]
            mixb[tp, :, t * W : (t + 1) * W] = part + jnp.where(tp == t, own_hidden, 0.0)
        for peer in tp_peers:
            push(mixb.at[tp, :, pl.ds(half * 2 * W, 2 * W)], mixb.at[tp, :, pl.ds(half * 2 * W, 2 * W)], 4, recv.at[3], peer)
    arrived(mixb.at[pl.ds(0, 3)], recv.at[3])
    resid = []
    for t in range(TP):
        lanes = slice(t * W, (t + 1) * W)
        resid.append((mixb[0, :, lanes] + mixb[1, :, lanes]) + (mixb[2, :, lanes] + mixb[3, :, lanes]))
    mean = jnp.sum((resid[0] + resid[1]) + (resid[2] + resid[3]), axis=1, keepdims=True) / D
    centred = [part - mean for part in resid]
    square = [part * part for part in centred]
    var = jnp.sum((square[0] + square[1]) + (square[2] + square[3]), axis=1, keepdims=True) / D
    own = centred[0]
    for t in range(1, TP):
        own = jnp.where(tp == t, centred[t], own)
    fin[c] = own / jnp.sqrt(var + 1e-05) * gbuf[...] + bbuf[...]
    push(fin.at[c], fin.at[c], 5, recv.at[4], sibling)

    @pl.when(c == 1)
    def _():
        arrived(gath.at[pl.ds(0, 3)], sent.at[0])
        arrived(qkv.at[0], sent.at[6])
        arrived(qkv.at[pl.ds(1, 2)], sent.at[7])

    arrived(crecv, sent.at[1])
    wait_ring(yb, sent.at[2])
    wait_ring(zb, sent.at[3])
    arrived(mixb.at[pl.ds(0, 3)], sent.at[4])
    arrived(fin.at[0], recv.at[4])
    out[...] = jnp.concatenate([fin[0], fin[1]], axis=0).astype(BF16)
    arrived(fin.at[0], sent.at[5])


def hand_out(o_in, k_in, v_in, o_out, k_out, v_out, sem):
    pairs = ((k_in, k_out), (v_in, v_out), (o_in, o_out))
    copies = [pltpu.make_async_copy(a, b, sem.at[i]) for i, (a, b) in enumerate(pairs)]
    for copy in copies:
        copy.start()
    for copy in copies:
        copy.wait()


def body(hidden_in, w_qkv, w_out, key_cache, value_cache, lengths, ln_gain, ln_bias):
    hbm = pl.BlockSpec(memory_space=pl.ANY)
    vmem = pl.BlockSpec(memory_space=pltpu.VMEM)
    cache = (B, SPAN, W)
    dma = pltpu.SemaphoreType.DMA
    done = pl.pallas_call(
        kernel,
        out_shape=(pltpu.VMEM((B, W), BF16), pltpu.VMEM(cache, BF16), pltpu.VMEM(cache, BF16)),
        in_specs=[hbm] * 8,
        out_specs=(vmem, vmem, vmem),
        scratch_shapes=[
            pltpu.SMEM((B,), jnp.int32),
            pltpu.VMEM((TP, B, W), BF16),
            pltpu.VMEM((3, B, W), BF16),
            pltpu.VMEM((3, D, W), BF16),
            pltpu.VMEM((W, D), BF16),
            pltpu.VMEM((1, W), F32),
            pltpu.VMEM((1, W), F32),
            pltpu.VMEM((2, 3, HALF, W), F32),
            pltpu.VMEM((3, HALF, W), F32),
            pltpu.VMEM((2 * RING * SLOT, 128), F32),
            pltpu.VMEM((2 * RING * SLOT, 128), F32),
            pltpu.VMEM((TP, HALF, D), F32),
            pltpu.VMEM((2, HALF, W), F32),
            dma((9,)), dma((3,)), dma((7,)), dma((8,)),
        ],
        compiler_params=pltpu.CompilerParams(collective_id=0, has_side_effects=True),
        name="sublayer",
    )(
        lengths, hidden_in, w_qkv, w_out, key_cache, value_cache,
        ln_gain.reshape(1, W), ln_bias.reshape(1, W),
    )
    return pl.pallas_call(
        hand_out,
        out_shape=(
            jax.ShapeDtypeStruct((B, W), BF16),
            jax.ShapeDtypeStruct(cache, BF16),
            jax.ShapeDtypeStruct(cache, BF16),
        ),
        in_specs=[vmem] * 3,
        out_specs=(hbm, hbm, hbm),
        scratch_shapes=[dma((3,))],
        name="hand_out",
    )(*[pltpu.with_memory_space_constraint(part, pltpu.VMEM) for part in done])


def solution(mesh):
    in_specs = (
        P(None, "tp"),
        P(None, None, "tp"),
        P("tp", None),
        P(None, "seq", "tp"),
        P(None, "seq", "tp"),
        P(),
        P("tp"),
        P("tp"),
    )
    out_specs = (P(None, "tp"), P(None, "seq", "tp"), P(None, "seq", "tp"))
    return jax.shard_map(body, mesh=mesh, in_specs=in_specs, out_specs=out_specs, check_vma=False)
```

```python
import jax
import jax.numpy as jnp
from jax import lax
from jax.experimental import pallas as pl
from jax.experimental.pallas import tpu as pltpu
from jax.sharding import PartitionSpec as P

D = 1024
HD = 64
B = 16
HALF = 8
W = 256
TP = 4
RING = 8
SPAN = 64
SLOT = 16
SENT = 9
NEG = -1e30
F32 = jnp.float32
BF16 = jnp.bfloat16
MESH = pl.DeviceIdType.MESH


def iota(shape, dim):
    return lax.broadcasted_iota(jnp.int32, shape, dim)


def split_dot(rows, matrix):
    upper = rows.astype(BF16)
    lower = (rows - upper.astype(F32)).astype(BF16)
    both = jnp.dot(jnp.concatenate([upper, lower], axis=0), matrix, preferred_element_type=F32)
    return both[: rows.shape[0]] + both[rows.shape[0] :]


def to_row(tops, totals):
    lane, request = iota((HALF, W), 1) % HD, iota((HALF, W), 0)
    picked = jnp.where(lane == request, tops, jnp.where(lane == request + HALF, totals, 0.0))
    row = jnp.sum(picked, axis=0, keepdims=True)
    return row[:, :128], row[:, 128:]


def kernel(
    lengths, hid, wqkv, wout, kc, vc, gain, bias,
    out, kbuf, vbuf,
    lens, gath, qkv, wbuf, wobuf, gbuf, bbuf,
    csend, crecv, yb, zb, mixb, fin,
    lsem, hsem, recv, sent, ready,
):
    seq = lax.axis_index("seq")
    tp = lax.axis_index("tp")
    y, z, c = seq // 16, (seq % 16) // 2, seq % 2

    loads = [
        pltpu.make_async_copy(hid, gath.at[tp], lsem.at[0]),
        pltpu.make_async_copy(wqkv.at[0], wbuf.at[0], lsem.at[1]),
        pltpu.make_async_copy(kc, kbuf, lsem.at[2]),
        pltpu.make_async_copy(vc, vbuf, lsem.at[3]),
        pltpu.make_async_copy(wqkv.at[pl.ds(1, 2)], wbuf.at[pl.ds(1, 2)], lsem.at[4]),
        pltpu.make_async_copy(wout, wobuf, lsem.at[5]),
        pltpu.make_async_copy(gain, gbuf, lsem.at[6]),
        pltpu.make_async_copy(bias, bbuf, lsem.at[7]),
        pltpu.make_async_copy(lengths, lens, lsem.at[8]),
    ]
    tp_peers = [(seq, lax.rem(tp + d, TP)) for d in (2, 1, 3)]
    y_peers = [(lax.rem(y + d, RING) * 16 + z * 2 + c, tp) for d in (4, 3, 5, 2, 6, 1, 7)]
    z_peers = [(y * 16 + lax.rem(z + d, RING) * 2 + c, tp) for d in (4, 3, 5, 2, 6, 1, 7)]
    sibling = (y * 16 + z * 2 + (1 - c), tp)
    y_zero = [(lax.rem(y + d, RING) * 16 + z * 2, tp) for d in (4, 3, 5, 2, 6, 1, 7)]
    z_zero = [(y * 16 + lax.rem(z + d, RING) * 2, tp) for d in (4, 3, 5, 2, 6, 1, 7)]

    barrier = pltpu.get_barrier_semaphore()

    def signal(peer):
        pl.semaphore_signal(barrier, inc=1, device_id=peer, device_id_type=MESH)

    @pl.when(c == 1)
    def _():
        for peer in tp_peers:
            signal(peer)
        loads[0].start()
        for z_peer, y_peer in zip(z_zero, y_zero):
            signal(z_peer)
            signal(y_peer)
        signal(sibling)
        for index in (1, 8, 2, 3, 4, 5, 6, 7):
            loads[index].start()
        loads[0].wait()
        pl.semaphore_wait(barrier, 3)

    @pl.when(c == 0)
    def _():
        for z_peer, y_peer in zip(z_peers, y_peers):
            signal(z_peer)
            signal(y_peer)
        for peer in tp_peers:
            signal(peer)
        for index in (8, 2, 3, 0, 5, 6, 7):
            loads[index].start()

    def push(src, dst, stage, recv_sem, peer):
        pltpu.make_async_remote_copy(
            src, dst, sent.at[stage], recv_sem, device_id=peer, device_id_type=MESH
        ).start()

    def arrived(ref, sem):
        pltpu.make_async_copy(ref, ref, sem).wait()

    def project(index, t):
        rows = pl.ds(pl.multiple_of(t * W, W), W)
        return jnp.dot(gath[t], wbuf[index, rows, :], preferred_element_type=F32)

    @pl.when(c == 1)
    def _():
        for i, peer in enumerate(tp_peers):
            push(gath.at[tp], gath.at[tp], 0, hsem.at[i], peer)

    column_head = iota((B, W), 1) // HD
    row_b = iota((B, 1), 0)
    loads[8].wait()
    local_len = jnp.zeros((B, 1), jnp.int32)
    for b in range(B):
        local_len = jnp.where(row_b == b, lens[b] - seq * SPAN, local_len)
    row_len = jnp.concatenate([local_len] * 4, axis=0)
    request = iota((4 * B, 128), 0) % B
    lane = iota((4 * B, 128), 1)
    valid = jnp.logical_and(lane // SPAN == request % 2, lane % SPAN < row_len)
    pair = request // 2
    same_head = jnp.where(iota((128, 128), 0) // HD == iota((128, 128), 1) // HD, 1.0, 0.0).astype(BF16)

    @pl.when(c == 1)
    def _():
        loads[1].wait()
        acc = project(0, tp)
        for i, d in ((1, 1), (2, 3), (0, 2)):
            t = lax.rem(tp + TP - d, TP)
            arrived(gath.at[t], hsem.at[i])
            acc = acc + project(0, t)
        qkv[0] = acc.astype(BF16)
        pl.semaphore_wait(ready, 1)
        push(qkv.at[0], qkv.at[0], 6, recv.at[5], sibling)

    @pl.when(c == 0)
    def _():
        pl.semaphore_wait(barrier, 32)
        pl.semaphore_signal(ready, inc=1, device_id=sibling, device_id_type=MESH)
        loads[0].wait()
        arrived(qkv.at[0], recv.at[5])

    query = qkv[0]

    spread = jnp.concatenate(
        [jnp.where(column_head == h, query.astype(F32), 0.0) for h in range(4)], axis=0
    ).astype(BF16)
    loads[2].wait()
    keys = kbuf[...].reshape(B * SPAN, W)
    every = lax.dot_general(spread, keys, (((1,), (1,)), ((), ())), preferred_element_type=F32)
    scores = every[:, :128]
    for j in range(1, 8):
        scores = jnp.where(pair == j, every[:, j * 128 : j * 128 + 128], scores)
    scores = jnp.where(valid, scores * HD ** (-0.5), NEG)
    top = jnp.max(scores, axis=1, keepdims=True)
    weights = jnp.where(valid, jnp.exp(scores - top), 0.0)
    total = jnp.sum(weights, axis=1, keepdims=True)
    upper = weights.astype(BF16).astype(F32)
    lower = weights - upper
    wide = jnp.concatenate(
        [
            jnp.concatenate([jnp.where(pair == j, part, 0.0).astype(BF16) for j in range(8)], axis=1)
            for part in (upper, lower)
        ],
        axis=0,
    )
    loads[3].wait()
    both = jnp.dot(wide, vbuf[...].reshape(B * SPAN, W), preferred_element_type=F32)
    summed = both[: 4 * B] + both[4 * B :]

    def fold(rows):
        result = jnp.broadcast_to(rows[0:B], (B, W))
        for h in range(1, 4):
            result = jnp.where(column_head == h, rows[h * B : (h + 1) * B], result)
        return result

    for core in range(2):
        for i, part in enumerate((fold(summed), fold(total), fold(top))):
            csend[core, i] = part[core * HALF : (core + 1) * HALF]
    push(csend.at[1 - c], crecv, 1, recv.at[0], sibling)

    @pl.when(c == 1)
    def _():
        loads[4].wait()
        for index in (1, 2):
            qkv[index] = sum(project(index, t) for t in range(TP)).astype(BF16)
        push(qkv.at[pl.ds(1, 2)], qkv.at[pl.ds(1, 2)], 7, recv.at[6], sibling)

    arrived(crecv, recv.at[0])
    my_acc, my_total, my_top = csend[c, 0], csend[c, 1], csend[c, 2]
    both_top = jnp.maximum(my_top, crecv[2])
    mine, other = jnp.exp(my_top - both_top), jnp.exp(crecv[2] - both_top)
    both_acc = my_acc * mine + crecv[0] * other
    both_total = my_total * mine + crecv[1] * other

    def place(ref, slot, acc, row):
        base = pl.multiple_of(slot * SLOT, 8)
        ref[pl.ds(base, 8), :] = acc
        ref[pl.ds(base + 8, 1), :] = row

    def slot_of(ref, slot):
        return ref.at[pl.ds(pl.multiple_of(slot * SLOT, 8), SENT), :]

    def wait_ring(ref, sem):
        arrived(ref.at[pl.ds(0, 14 * SENT), :], sem)

    def push_ring(ref, slot_y, slot_z, stage, recv_sem):
        for y_peer, z_peer in zip(y_peers, z_peers):
            push(slot_of(ref, slot_y), slot_of(ref, slot_y), stage, recv_sem, y_peer)
            push(slot_of(ref, slot_z), slot_of(ref, slot_z), stage, recv_sem, z_peer)

    def spread_rows(rows):
        keep = iota((HALF, 128), 1) % HD == iota((HALF, 128), 0)
        return split_dot(
            jnp.concatenate(
                [jnp.where(keep, rows[s : s + 1], 0.0) for s in range(rows.shape[0])], axis=0
            ),
            same_head,
        )

    def ring_acc(ref, factors, first):
        acc = None
        for s in range(first, first + RING):
            part = ref[s * SLOT : s * SLOT + 8, :] * factors[s * 8 : s * 8 + 8]
            acc = part if acc is None else acc + part
        return acc

    def over(first, second):
        return jnp.where(iota((2 * RING, 128), 0) < RING, first, second)

    low_row, high_row = to_row(both_top, both_total)
    place(yb, y, both_acc[:, :128], low_row)
    place(yb, RING + z, both_acc[:, 128:], high_row)
    push_ring(yb, y, RING + z, 2, recv.at[1])

    @pl.when(c == 0)
    def _():
        arrived(qkv.at[pl.ds(1, 2)], recv.at[6])

    new_key, new_value = qkv[1], qkv[2]
    product = query.astype(F32) * new_key.astype(F32)
    halves = split_dot(jnp.concatenate([product[:, :128], product[:, 128:]], axis=0), same_head)
    new_score = jnp.concatenate([halves[:B], halves[B:]], axis=1) * HD ** (-0.5)

    def own_half(rows):
        return jnp.where(c == 0, rows[:HALF], rows[HALF:])

    new_low, new_high = to_row(own_half(new_score), jnp.ones((HALF, W), F32))
    new_acc = own_half(new_value.astype(F32))
    position = iota((SPAN, W), 0)
    for b in range(B):
        hit = position == lens[b] - seq * SPAN
        kbuf[b] = jnp.where(hit, new_key[b : b + 1].astype(F32), kbuf[b].astype(F32)).astype(BF16)
        vbuf[b] = jnp.where(hit, new_value[b : b + 1].astype(F32), vbuf[b].astype(F32)).astype(BF16)
    max_lane = iota((1, 128), 1) % HD < HALF
    wait_ring(yb, recv.at[1])
    rows = yb[pl.ds(8, 2 * RING, stride=SLOT), :]
    low_top = jnp.max(rows[:RING], axis=0, keepdims=True)
    high_top = jnp.max(rows[RING:], axis=0, keepdims=True)
    factor = jnp.exp(rows - over(low_top, high_top))
    totals = rows * pltpu.roll(factor, HALF, 1)
    low_total = jnp.sum(totals[:RING], axis=0, keepdims=True)
    high_total = jnp.sum(totals[RING:], axis=0, keepdims=True)
    factors = spread_rows(factor)
    place(zb, z, ring_acc(yb, factors, 0), jnp.where(max_lane, low_top, low_total))
    place(zb, RING + y, ring_acc(yb, factors, RING), jnp.where(max_lane, high_top, high_total))
    push_ring(zb, RING + y, z, 3, recv.at[2])

    own_hidden = own_half(gath[tp].astype(F32))
    loads[5].wait()
    loads[6].wait()
    loads[7].wait()

    wait_ring(zb, recv.at[2])
    rows = zb[pl.ds(8, 2 * RING, stride=SLOT), :]
    low_top = jnp.maximum(jnp.max(rows[:RING], axis=0, keepdims=True), new_low)
    high_top = jnp.maximum(jnp.max(rows[RING:], axis=0, keepdims=True), new_high)
    factor = jnp.exp(rows - over(low_top, high_top))
    totals = rows * pltpu.roll(factor, HALF, 1)
    low_new, high_new = jnp.exp(new_low - low_top), jnp.exp(new_high - high_top)
    low_total = jnp.sum(totals[:RING], axis=0, keepdims=True) + new_low * pltpu.roll(low_new, HALF, 1)
    high_total = jnp.sum(totals[RING:], axis=0, keepdims=True) + new_high * pltpu.roll(high_new, HALF, 1)
    low_share, high_share = pltpu.roll(low_total, 128 - HALF, 1), pltpu.roll(high_total, 128 - HALF, 1)
    factors = spread_rows(
        jnp.concatenate(
            [factor / over(low_share, high_share), low_new / low_share, high_new / high_share], axis=0
        )
    )
    attended = jnp.concatenate(
        [
            ring_acc(zb, factors, 0) + new_acc[:, :128] * factors[128:136],
            ring_acc(zb, factors, RING) + new_acc[:, 128:] * factors[136:144],
        ],
        axis=1,
    )
    attended = attended.astype(BF16)
    for half in range(2):
        lanes = slice(half * 2 * W, (half + 1) * 2 * W)
        mixed = jnp.dot(attended, wobuf[:, lanes], preferred_element_type=F32)
        for t in (2 * half, 2 * half + 1):
            part = mixed[:, t % 2 * W : (t % 2 + 1) * W]
            mixb[tp, :, t * W : (t + 1) * W] = part + jnp.where(tp == t, own_hidden, 0.0)
        for peer in tp_peers:
            push(mixb.at[tp, :, pl.ds(half * 2 * W, 2 * W)], mixb.at[tp, :, pl.ds(half * 2 * W, 2 * W)], 4, recv.at[3], peer)
    arrived(mixb.at[pl.ds(0, 3)], recv.at[3])
    resid = []
    for t in range(TP):
        lanes = slice(t * W, (t + 1) * W)
        resid.append((mixb[0, :, lanes] + mixb[1, :, lanes]) + (mixb[2, :, lanes] + mixb[3, :, lanes]))
    mean = jnp.sum((resid[0] + resid[1]) + (resid[2] + resid[3]), axis=1, keepdims=True) / D
    centred = [part - mean for part in resid]
    square = [part * part for part in centred]
    var = jnp.sum((square[0] + square[1]) + (square[2] + square[3]), axis=1, keepdims=True) / D
    own = centred[0]
    for t in range(1, TP):
        own = jnp.where(tp == t, centred[t], own)
    fin[c] = own / jnp.sqrt(var + 1e-05) * gbuf[...] + bbuf[...]
    push(fin.at[c], fin.at[c], 5, recv.at[4], sibling)

    @pl.when(c == 1)
    def _():
        arrived(gath.at[pl.ds(0, 3)], sent.at[0])
        arrived(qkv.at[0], sent.at[6])
        arrived(qkv.at[pl.ds(1, 2)], sent.at[7])

    arrived(crecv, sent.at[1])
    wait_ring(yb, sent.at[2])
    wait_ring(zb, sent.at[3])
    arrived(mixb.at[pl.ds(0, 3)], sent.at[4])
    arrived(fin.at[0], recv.at[4])
    out[...] = jnp.concatenate([fin[0], fin[1]], axis=0).astype(BF16)
    arrived(fin.at[0], sent.at[5])


def hand_out(o_in, k_in, v_in, o_out, k_out, v_out, sem):
    pairs = ((k_in, k_out), (v_in, v_out), (o_in, o_out))
    copies = [pltpu.make_async_copy(a, b, sem.at[i]) for i, (a, b) in enumerate(pairs)]
    for copy in copies:
        copy.start()
    for copy in copies:
        copy.wait()


def body(hidden_in, w_qkv, w_out, key_cache, value_cache, lengths, ln_gain, ln_bias):
    hbm = pl.BlockSpec(memory_space=pl.ANY)
    vmem = pl.BlockSpec(memory_space=pltpu.VMEM)
    cache = (B, SPAN, W)
    dma = pltpu.SemaphoreType.DMA
    done = pl.pallas_call(
        kernel,
        out_shape=(pltpu.VMEM((B, W), BF16), pltpu.VMEM(cache, BF16), pltpu.VMEM(cache, BF16)),
        in_specs=[hbm] * 8,
        out_specs=(vmem, vmem, vmem),
        scratch_shapes=[
            pltpu.SMEM((B,), jnp.int32),
            pltpu.VMEM((TP, B, W), BF16),
            pltpu.VMEM((3, B, W), BF16),
            pltpu.VMEM((3, D, W), BF16),
            pltpu.VMEM((W, D), BF16),
            pltpu.VMEM((1, W), F32),
            pltpu.VMEM((1, W), F32),
            pltpu.VMEM((2, 3, HALF, W), F32),
            pltpu.VMEM((3, HALF, W), F32),
            pltpu.VMEM((2 * RING * SLOT, 128), F32),
            pltpu.VMEM((2 * RING * SLOT, 128), F32),
            pltpu.VMEM((TP, HALF, D), F32),
            pltpu.VMEM((2, HALF, W), F32),
            dma((9,)), dma((3,)), dma((7,)), dma((8,)), pltpu.SemaphoreType.REGULAR,
        ],
        compiler_params=pltpu.CompilerParams(collective_id=0, has_side_effects=True),
        name="sublayer",
    )(
        lengths, hidden_in, w_qkv, w_out, key_cache, value_cache,
        ln_gain.reshape(1, W), ln_bias.reshape(1, W),
    )
    return pl.pallas_call(
        hand_out,
        out_shape=(
            jax.ShapeDtypeStruct((B, W), BF16),
            jax.ShapeDtypeStruct(cache, BF16),
            jax.ShapeDtypeStruct(cache, BF16),
        ),
        in_specs=[vmem] * 3,
        out_specs=(hbm, hbm, hbm),
        scratch_shapes=[dma((3,))],
        name="hand_out",
    )(*[pltpu.with_memory_space_constraint(part, pltpu.VMEM) for part in done])


def solution(mesh):
    in_specs = (
        P(None, "tp"),
        P(None, None, "tp"),
        P("tp", None),
        P(None, "seq", "tp"),
        P(None, "seq", "tp"),
        P(),
        P("tp"),
        P("tp"),
    )
    out_specs = (P(None, "tp"), P(None, "seq", "tp"), P(None, "seq", "tp"))
    return jax.shard_map(body, mesh=mesh, in_specs=in_specs, out_specs=out_specs, check_vma=False)
```

```python
import jax
import jax.numpy as jnp
from jax import lax
from jax.experimental import pallas as pl
from jax.experimental.pallas import tpu as pltpu
from jax.sharding import PartitionSpec as P

D = 1024
HD = 64
B = 16
HALF = 8
W = 256
TP = 4
RING = 8
SPAN = 64
SLOT = 16
SENT = 9
NEG = -1e30
F32 = jnp.float32
BF16 = jnp.bfloat16
MESH = pl.DeviceIdType.MESH


def iota(shape, dim):
    return lax.broadcasted_iota(jnp.int32, shape, dim)


def split_dot(rows, matrix):
    upper = rows.astype(BF16)
    lower = (rows - upper.astype(F32)).astype(BF16)
    both = jnp.dot(jnp.concatenate([upper, lower], axis=0), matrix, preferred_element_type=F32)
    return both[: rows.shape[0]] + both[rows.shape[0] :]


def to_row(tops, totals):
    lane, request = iota((HALF, W), 1) % HD, iota((HALF, W), 0)
    picked = jnp.where(lane == request, tops, jnp.where(lane == request + HALF, totals, 0.0))
    row = jnp.sum(picked, axis=0, keepdims=True)
    return row[:, :128], row[:, 128:]


def kernel(
    lengths, hid, wqkv, wout, kc, vc, gain, bias,
    out, kbuf, vbuf,
    lens, across, gath, qkv, wbuf, wobuf, gbuf, bbuf,
    csend, crecv, yb, zb, mixb, fin,
    lsem, hsem, recv, sent, ready,
):
    seq = lax.axis_index("seq")
    tp = lax.axis_index("tp")
    y, z, c = seq // 16, (seq % 16) // 2, seq % 2

    loads = [
        pltpu.make_async_copy(hid, gath.at[tp], lsem.at[0]),
        pltpu.make_async_copy(wqkv.at[0], wbuf.at[0], lsem.at[1]),
        pltpu.make_async_copy(kc, kbuf, lsem.at[2]),
        pltpu.make_async_copy(vc, vbuf, lsem.at[3]),
        pltpu.make_async_copy(wqkv.at[pl.ds(1, 2)], wbuf.at[pl.ds(1, 2)], lsem.at[4]),
        pltpu.make_async_copy(wout, wobuf, lsem.at[5]),
        pltpu.make_async_copy(gain, gbuf, lsem.at[6]),
        pltpu.make_async_copy(bias, bbuf, lsem.at[7]),
        pltpu.make_async_copy(lengths, lens, lsem.at[8]),
    ]
    tp_peers = [(seq, lax.rem(tp + d, TP)) for d in (2, 1, 3)]
    y_peers = [(lax.rem(y + d, RING) * 16 + z * 2 + c, tp) for d in (4, 3, 5, 2, 6, 1, 7)]
    z_peers = [(y * 16 + lax.rem(z + d, RING) * 2 + c, tp) for d in (4, 3, 5, 2, 6, 1, 7)]
    sibling = (y * 16 + z * 2 + (1 - c), tp)
    y_zero = [(lax.rem(y + d, RING) * 16 + z * 2, tp) for d in (4, 3, 5, 2, 6, 1, 7)]
    z_zero = [(y * 16 + lax.rem(z + d, RING) * 2, tp) for d in (4, 3, 5, 2, 6, 1, 7)]

    barrier = pltpu.get_barrier_semaphore()

    def signal(peer):
        pl.semaphore_signal(barrier, inc=1, device_id=peer, device_id_type=MESH)

    @pl.when(c == 1)
    def _():
        for peer in tp_peers:
            signal(peer)
        loads[0].start()
        for z_peer, y_peer in zip(z_zero, y_zero):
            signal(z_peer)
            signal(y_peer)
        signal(sibling)
        for index in (1, 8, 2, 3, 4, 5, 6, 7):
            loads[index].start()
        loads[0].wait()
        pl.semaphore_wait(barrier, 3)

    @pl.when(c == 0)
    def _():
        for z_peer, y_peer in zip(z_peers, y_peers):
            signal(z_peer)
            signal(y_peer)
        for peer in tp_peers:
            signal(peer)
        for index in (8, 2, 3, 0, 5, 6, 7):
            loads[index].start()

    def push(src, dst, stage, recv_sem, peer):
        pltpu.make_async_remote_copy(
            src, dst, sent.at[stage], recv_sem, device_id=peer, device_id_type=MESH
        ).start()

    def arrived(ref, sem):
        pltpu.make_async_copy(ref, ref, sem).wait()

    def project(index, t):
        rows = pl.ds(pl.multiple_of(t * W, W), W)
        return jnp.dot(gath[t], wbuf[index, rows, :], preferred_element_type=F32)

    @pl.when(c == 1)
    def _():
        for i, peer in enumerate(tp_peers):
            push(gath.at[tp], gath.at[tp], 0, hsem.at[i], peer)

    column_head = iota((B, W), 1) // HD
    row_b = iota((B, 1), 0)
    loads[8].wait()
    local_len = jnp.zeros((B, 1), jnp.int32)
    for b in range(B):
        local_len = jnp.where(row_b == b, lens[b] - seq * SPAN, local_len)
    row_len = jnp.concatenate([local_len] * 4, axis=0)
    request = iota((4 * B, 128), 0) % B
    lane = iota((4 * B, 128), 1)
    valid = jnp.logical_and(lane // SPAN == request % 2, lane % SPAN < row_len)
    pair = request // 2
    loads[2].wait()
    across[...] = kbuf[...].reshape(B * SPAN, W).T
    same_head = jnp.where(iota((128, 128), 0) // HD == iota((128, 128), 1) // HD, 1.0, 0.0).astype(BF16)

    @pl.when(c == 1)
    def _():
        loads[1].wait()
        acc = project(0, tp)
        for i, d in ((1, 1), (2, 3), (0, 2)):
            t = lax.rem(tp + TP - d, TP)
            arrived(gath.at[t], hsem.at[i])
            acc = acc + project(0, t)
        qkv[0] = acc.astype(BF16)
        pl.semaphore_wait(ready, 1)
        push(qkv.at[0], qkv.at[0], 6, recv.at[5], sibling)

    @pl.when(c == 0)
    def _():
        pl.semaphore_wait(barrier, 32)
        pl.semaphore_signal(ready, inc=1, device_id=sibling, device_id_type=MESH)
        loads[0].wait()
        arrived(qkv.at[0], recv.at[5])

    query = qkv[0]

    spread = jnp.concatenate(
        [jnp.where(column_head == h, query.astype(F32), 0.0) for h in range(4)], axis=0
    ).astype(BF16)
    every = jnp.dot(spread, across[...], preferred_element_type=F32)
    scores = every[:, :128]
    for j in range(1, 8):
        scores = jnp.where(pair == j, every[:, j * 128 : j * 128 + 128], scores)
    scores = jnp.where(valid, scores * HD ** (-0.5), NEG)
    top = jnp.max(scores, axis=1, keepdims=True)
    weights = jnp.where(valid, jnp.exp(scores - top), 0.0)
    total = jnp.sum(weights, axis=1, keepdims=True)
    upper = weights.astype(BF16).astype(F32)
    lower = weights - upper
    wide = jnp.concatenate(
        [
            jnp.concatenate([jnp.where(pair == j, part, 0.0).astype(BF16) for j in range(8)], axis=1)
            for part in (upper, lower)
        ],
        axis=0,
    )
    loads[3].wait()
    both = jnp.dot(wide, vbuf[...].reshape(B * SPAN, W), preferred_element_type=F32)
    summed = both[: 4 * B] + both[4 * B :]

    def fold(rows):
        result = jnp.broadcast_to(rows[0:B], (B, W))
        for h in range(1, 4):
            result = jnp.where(column_head == h, rows[h * B : (h + 1) * B], result)
        return result

    for core in range(2):
        for i, part in enumerate((fold(summed), fold(total), fold(top))):
            csend[core, i] = part[core * HALF : (core + 1) * HALF]
    push(csend.at[1 - c], crecv, 1, recv.at[0], sibling)

    @pl.when(c == 1)
    def _():
        loads[4].wait()
        for index in (1, 2):
            qkv[index] = sum(project(index, t) for t in range(TP)).astype(BF16)
        push(qkv.at[pl.ds(1, 2)], qkv.at[pl.ds(1, 2)], 7, recv.at[6], sibling)

    arrived(crecv, recv.at[0])
    my_acc, my_total, my_top = csend[c, 0], csend[c, 1], csend[c, 2]
    both_top = jnp.maximum(my_top, crecv[2])
    mine, other = jnp.exp(my_top - both_top), jnp.exp(crecv[2] - both_top)
    both_acc = my_acc * mine + crecv[0] * other
    both_total = my_total * mine + crecv[1] * other

    def place(ref, slot, acc, row):
        base = pl.multiple_of(slot * SLOT, 8)
        ref[pl.ds(base, 8), :] = acc
        ref[pl.ds(base + 8, 1), :] = row

    def slot_of(ref, slot):
        return ref.at[pl.ds(pl.multiple_of(slot * SLOT, 8), SENT), :]

    def wait_ring(ref, sem):
        arrived(ref.at[pl.ds(0, 14 * SENT), :], sem)

    def push_ring(ref, slot_y, slot_z, stage, recv_sem):
        for y_peer, z_peer in zip(y_peers, z_peers):
            push(slot_of(ref, slot_y), slot_of(ref, slot_y), stage, recv_sem, y_peer)
            push(slot_of(ref, slot_z), slot_of(ref, slot_z), stage, recv_sem, z_peer)

    def spread_rows(rows):
        keep = iota((HALF, 128), 1) % HD == iota((HALF, 128), 0)
        return split_dot(
            jnp.concatenate(
                [jnp.where(keep, rows[s : s + 1], 0.0) for s in range(rows.shape[0])], axis=0
            ),
            same_head,
        )

    def ring_acc(ref, factors, first):
        acc = None
        for s in range(first, first + RING):
            part = ref[s * SLOT : s * SLOT + 8, :] * factors[s * 8 : s * 8 + 8]
            acc = part if acc is None else acc + part
        return acc

    def over(first, second):
        return jnp.where(iota((2 * RING, 128), 0) < RING, first, second)

    low_row, high_row = to_row(both_top, both_total)
    place(yb, y, both_acc[:, :128], low_row)
    place(yb, RING + z, both_acc[:, 128:], high_row)
    push_ring(yb, y, RING + z, 2, recv.at[1])

    @pl.when(c == 0)
    def _():
        arrived(qkv.at[pl.ds(1, 2)], recv.at[6])

    new_key, new_value = qkv[1], qkv[2]
    product = query.astype(F32) * new_key.astype(F32)
    halves = split_dot(jnp.concatenate([product[:, :128], product[:, 128:]], axis=0), same_head)
    new_score = jnp.concatenate([halves[:B], halves[B:]], axis=1) * HD ** (-0.5)

    def own_half(rows):
        return jnp.where(c == 0, rows[:HALF], rows[HALF:])

    new_low, new_high = to_row(own_half(new_score), jnp.ones((HALF, W), F32))
    new_acc = own_half(new_value.astype(F32))
    position = iota((SPAN, W), 0)
    for b in range(B):
        hit = position == lens[b] - seq * SPAN
        kbuf[b] = jnp.where(hit, new_key[b : b + 1].astype(F32), kbuf[b].astype(F32)).astype(BF16)
        vbuf[b] = jnp.where(hit, new_value[b : b + 1].astype(F32), vbuf[b].astype(F32)).astype(BF16)
    max_lane = iota((1, 128), 1) % HD < HALF
    wait_ring(yb, recv.at[1])
    rows = yb[pl.ds(8, 2 * RING, stride=SLOT), :]
    low_top = jnp.max(rows[:RING], axis=0, keepdims=True)
    high_top = jnp.max(rows[RING:], axis=0, keepdims=True)
    factor = jnp.exp(rows - over(low_top, high_top))
    totals = rows * pltpu.roll(factor, HALF, 1)
    low_total = jnp.sum(totals[:RING], axis=0, keepdims=True)
    high_total = jnp.sum(totals[RING:], axis=0, keepdims=True)
    factors = spread_rows(factor)
    place(zb, z, ring_acc(yb, factors, 0), jnp.where(max_lane, low_top, low_total))
    place(zb, RING + y, ring_acc(yb, factors, RING), jnp.where(max_lane, high_top, high_total))
    push_ring(zb, RING + y, z, 3, recv.at[2])

    own_hidden = own_half(gath[tp].astype(F32))
    loads[5].wait()
    loads[6].wait()
    loads[7].wait()

    wait_ring(zb, recv.at[2])
    rows = zb[pl.ds(8, 2 * RING, stride=SLOT), :]
    low_top = jnp.maximum(jnp.max(rows[:RING], axis=0, keepdims=True), new_low)
    high_top = jnp.maximum(jnp.max(rows[RING:], axis=0, keepdims=True), new_high)
    factor = jnp.exp(rows - over(low_top, high_top))
    totals = rows * pltpu.roll(factor, HALF, 1)
    low_new, high_new = jnp.exp(new_low - low_top), jnp.exp(new_high - high_top)
    low_total = jnp.sum(totals[:RING], axis=0, keepdims=True) + new_low * pltpu.roll(low_new, HALF, 1)
    high_total = jnp.sum(totals[RING:], axis=0, keepdims=True) + new_high * pltpu.roll(high_new, HALF, 1)
    low_share, high_share = pltpu.roll(low_total, 128 - HALF, 1), pltpu.roll(high_total, 128 - HALF, 1)
    factors = spread_rows(
        jnp.concatenate(
            [factor / over(low_share, high_share), low_new / low_share, high_new / high_share], axis=0
        )
    )
    attended = jnp.concatenate(
        [
            ring_acc(zb, factors, 0) + new_acc[:, :128] * factors[128:136],
            ring_acc(zb, factors, RING) + new_acc[:, 128:] * factors[136:144],
        ],
        axis=1,
    )
    attended = attended.astype(BF16)
    for half in range(2):
        lanes = slice(half * 2 * W, (half + 1) * 2 * W)
        mixed = jnp.dot(attended, wobuf[:, lanes], preferred_element_type=F32)
        for t in (2 * half, 2 * half + 1):
            part = mixed[:, t % 2 * W : (t % 2 + 1) * W]
            mixb[tp, :, t * W : (t + 1) * W] = part + jnp.where(tp == t, own_hidden, 0.0)
        for peer in tp_peers:
            push(mixb.at[tp, :, pl.ds(half * 2 * W, 2 * W)], mixb.at[tp, :, pl.ds(half * 2 * W, 2 * W)], 4, recv.at[3], peer)
    arrived(mixb.at[pl.ds(0, 3)], recv.at[3])
    resid = []
    for t in range(TP):
        lanes = slice(t * W, (t + 1) * W)
        resid.append((mixb[0, :, lanes] + mixb[1, :, lanes]) + (mixb[2, :, lanes] + mixb[3, :, lanes]))
    mean = jnp.sum((resid[0] + resid[1]) + (resid[2] + resid[3]), axis=1, keepdims=True) / D
    centred = [part - mean for part in resid]
    square = [part * part for part in centred]
    var = jnp.sum((square[0] + square[1]) + (square[2] + square[3]), axis=1, keepdims=True) / D
    own = centred[0]
    for t in range(1, TP):
        own = jnp.where(tp == t, centred[t], own)
    fin[c] = own / jnp.sqrt(var + 1e-05) * gbuf[...] + bbuf[...]
    push(fin.at[c], fin.at[c], 5, recv.at[4], sibling)

    @pl.when(c == 1)
    def _():
        arrived(gath.at[pl.ds(0, 3)], sent.at[0])
        arrived(qkv.at[0], sent.at[6])
        arrived(qkv.at[pl.ds(1, 2)], sent.at[7])

    arrived(crecv, sent.at[1])
    wait_ring(yb, sent.at[2])
    wait_ring(zb, sent.at[3])
    arrived(mixb.at[pl.ds(0, 3)], sent.at[4])
    arrived(fin.at[0], recv.at[4])
    out[...] = jnp.concatenate([fin[0], fin[1]], axis=0).astype(BF16)
    arrived(fin.at[0], sent.at[5])


def hand_out(o_in, k_in, v_in, o_out, k_out, v_out, sem):
    copies = [pltpu.make_async_copy(o_in, o_out, sem.at[0])]
    for i in range(4):
        part = pl.ds(i * B // 4, B // 4)
        copies.append(pltpu.make_async_copy(k_in.at[part], k_out.at[part], sem.at[1 + 2 * i]))
        copies.append(pltpu.make_async_copy(v_in.at[part], v_out.at[part], sem.at[2 + 2 * i]))
    for copy in copies:
        copy.start()
    for copy in copies:
        copy.wait()


def body(hidden_in, w_qkv, w_out, key_cache, value_cache, lengths, ln_gain, ln_bias):
    hbm = pl.BlockSpec(memory_space=pl.ANY)
    vmem = pl.BlockSpec(memory_space=pltpu.VMEM)
    cache = (B, SPAN, W)
    dma = pltpu.SemaphoreType.DMA
    done = pl.pallas_call(
        kernel,
        out_shape=(pltpu.VMEM((B, W), BF16), pltpu.VMEM(cache, BF16), pltpu.VMEM(cache, BF16)),
        in_specs=[hbm] * 8,
        out_specs=(vmem, vmem, vmem),
        scratch_shapes=[
            pltpu.SMEM((B,), jnp.int32),
            pltpu.VMEM((W, B * SPAN), BF16),
            pltpu.VMEM((TP, B, W), BF16),
            pltpu.VMEM((3, B, W), BF16),
            pltpu.VMEM((3, D, W), BF16),
            pltpu.VMEM((W, D), BF16),
            pltpu.VMEM((1, W), F32),
            pltpu.VMEM((1, W), F32),
            pltpu.VMEM((2, 3, HALF, W), F32),
            pltpu.VMEM((3, HALF, W), F32),
            pltpu.VMEM((2 * RING * SLOT, 128), F32),
            pltpu.VMEM((2 * RING * SLOT, 128), F32),
            pltpu.VMEM((TP, HALF, D), F32),
            pltpu.VMEM((2, HALF, W), F32),
            dma((9,)), dma((3,)), dma((7,)), dma((8,)), pltpu.SemaphoreType.REGULAR,
        ],
        compiler_params=pltpu.CompilerParams(collective_id=0, has_side_effects=True),
        name="sublayer",
    )(
        lengths, hidden_in, w_qkv, w_out, key_cache, value_cache,
        ln_gain.reshape(1, W), ln_bias.reshape(1, W),
    )
    return pl.pallas_call(
        hand_out,
        out_shape=(
            jax.ShapeDtypeStruct((B, W), BF16),
            jax.ShapeDtypeStruct(cache, BF16),
            jax.ShapeDtypeStruct(cache, BF16),
        ),
        in_specs=[vmem] * 3,
        out_specs=(hbm, hbm, hbm),
        scratch_shapes=[dma((9,))],
        name="hand_out",
    )(*[pltpu.with_memory_space_constraint(part, pltpu.VMEM) for part in done])


def solution(mesh):
    in_specs = (
        P(None, "tp"),
        P(None, None, "tp"),
        P("tp", None),
        P(None, "seq", "tp"),
        P(None, "seq", "tp"),
        P(),
        P("tp"),
        P("tp"),
    )
    out_specs = (P(None, "tp"), P(None, "seq", "tp"), P(None, "seq", "tp"))
    return jax.shard_map(body, mesh=mesh, in_specs=in_specs, out_specs=out_specs, check_vma=False)
```

```python
import jax
import jax.numpy as jnp
from jax import lax
from jax.experimental import pallas as pl
from jax.experimental.pallas import tpu as pltpu
from jax.sharding import PartitionSpec as P

D = 1024
HD = 64
B = 16
HALF = 8
W = 256
TP = 4
RING = 8
SPAN = 64
SLOT = 16
SENT = 9
NEG = -1e30
F32 = jnp.float32
BF16 = jnp.bfloat16
MESH = pl.DeviceIdType.MESH


def iota(shape, dim):
    return lax.broadcasted_iota(jnp.int32, shape, dim)


def split_dot(rows, matrix):
    upper = rows.astype(BF16)
    lower = (rows - upper.astype(F32)).astype(BF16)
    both = jnp.dot(jnp.concatenate([upper, lower], axis=0), matrix, preferred_element_type=F32)
    return both[: rows.shape[0]] + both[rows.shape[0] :]


def to_row(tops, totals):
    lane, request = iota((HALF, W), 1) % HD, iota((HALF, W), 0)
    picked = jnp.where(lane == request, tops, jnp.where(lane == request + HALF, totals, 0.0))
    row = jnp.sum(picked, axis=0, keepdims=True)
    return row[:, :128], row[:, 128:]


def kernel(
    lengths, hid, wqkv, wout, kc, vc, gain, bias,
    out, kbuf, vbuf,
    lens, across, gath, qkv, wbuf, wobuf, gbuf, bbuf,
    csend, crecv, yb, zb, mixb, fin,
    lsem, hsem, recv, sent, ready,
):
    seq = lax.axis_index("seq")
    tp = lax.axis_index("tp")
    y, z, c = seq // 16, (seq % 16) // 2, seq % 2

    loads = [
        pltpu.make_async_copy(hid, gath.at[tp], lsem.at[0]),
        pltpu.make_async_copy(wqkv.at[0], wbuf.at[0], lsem.at[1]),
        pltpu.make_async_copy(kc, kbuf, lsem.at[2]),
        pltpu.make_async_copy(vc, vbuf, lsem.at[3]),
        pltpu.make_async_copy(wqkv.at[pl.ds(1, 2)], wbuf.at[pl.ds(1, 2)], lsem.at[4]),
        pltpu.make_async_copy(wout, wobuf, lsem.at[5]),
        pltpu.make_async_copy(gain, gbuf, lsem.at[6]),
        pltpu.make_async_copy(bias, bbuf, lsem.at[7]),
        pltpu.make_async_copy(lengths, lens, lsem.at[8]),
    ]
    tp_peers = [(seq, lax.rem(tp + d, TP)) for d in (2, 1, 3)]
    y_peers = [(lax.rem(y + d, RING) * 16 + z * 2 + c, tp) for d in (4, 3, 5, 2, 6, 1, 7)]
    z_peers = [(y * 16 + lax.rem(z + d, RING) * 2 + c, tp) for d in (4, 3, 5, 2, 6, 1, 7)]
    sibling = (y * 16 + z * 2 + (1 - c), tp)
    y_zero = [(lax.rem(y + d, RING) * 16 + z * 2, tp) for d in (4, 3, 5, 2, 6, 1, 7)]
    z_zero = [(y * 16 + lax.rem(z + d, RING) * 2, tp) for d in (4, 3, 5, 2, 6, 1, 7)]

    t_zero = [(y * 16 + z * 2, peer[1]) for peer in tp_peers]

    def at_z(other):
        return (y * 16 + other * 2 + c, tp)

    is_src = jnp.logical_or(z == 0, z == 3)
    step = jnp.where(z == 3, 1, RING - 1)
    served = [
        at_z(lax.rem(z + RING - step, RING)),
        at_z(lax.rem(z + step, RING)),
        at_z(lax.rem(z + 2 * step, RING)),
    ]
    my_src = jnp.where(jnp.logical_or(z == 1, z >= 6), 0, 3)
    my_index = jnp.where(z <= 2, 0, jnp.where(jnp.logical_or(z == 4, z == 7), 1, 2))
    core0 = c == 0
    source = jnp.logical_and(c == 1, is_src)
    fed = jnp.logical_and(c == 1, jnp.logical_not(is_src))
    core0_source = jnp.logical_and(core0, is_src)
    core0_fed = jnp.logical_and(core0, jnp.logical_not(is_src))

    barrier = pltpu.get_barrier_semaphore()

    def signal(peer, sem=barrier):
        pl.semaphore_signal(sem, inc=1, device_id=peer, device_id_type=MESH)

    @pl.when(source)
    def _():
        for peer in tp_peers + served:
            signal(peer)
        loads[0].start()
        for peer in z_zero + y_zero + t_zero + [sibling]:
            signal(peer)
        for index in (1, 8, 2, 3, 4, 5, 6, 7):
            loads[index].start()
        loads[0].wait()
        pl.semaphore_wait(barrier, 4)

    @pl.when(fed)
    def _():
        pl.semaphore_wait(barrier, 1)
        signal(at_z(my_src), ready.at[my_index])
        for peer in z_zero + y_zero + t_zero + [sibling]:
            signal(peer)
        for index in (8, 2, 3, 0, 5, 6, 7):
            loads[index].start()

    @pl.when(core0_source)
    def _():
        signal(sibling)

    @pl.when(core0)
    def _():
        for peer in z_peers + y_peers + tp_peers:
            signal(peer)
        for index in (8, 2, 3, 0, 5, 6, 7):
            loads[index].start()

    def push(src, dst, stage, recv_sem, peer):
        pltpu.make_async_remote_copy(
            src, dst, sent.at[stage], recv_sem, device_id=peer, device_id_type=MESH
        ).start()

    def arrived(ref, sem):
        pltpu.make_async_copy(ref, ref, sem).wait()

    def project(index, t):
        rows = pl.ds(pl.multiple_of(t * W, W), W)
        return jnp.dot(gath[t], wbuf[index, rows, :], preferred_element_type=F32)

    def tell_core1():
        pl.semaphore_wait(barrier, 35)
        signal(sibling, ready.at[3])

    @pl.when(source)
    def _():
        for i, peer in enumerate(tp_peers):
            push(gath.at[tp], gath.at[tp], 0, hsem.at[i], peer)

    column_head = iota((B, W), 1) // HD
    row_b = iota((B, 1), 0)
    loads[8].wait()
    local_len = jnp.zeros((B, 1), jnp.int32)
    for b in range(B):
        local_len = jnp.where(row_b == b, lens[b] - seq * SPAN, local_len)
    row_len = jnp.concatenate([local_len] * 4, axis=0)
    request = iota((4 * B, 128), 0) % B
    lane = iota((4 * B, 128), 1)
    valid = jnp.logical_and(lane // SPAN == request % 2, lane % SPAN < row_len)
    pair = request // 2
    loads[2].wait()
    across[...] = kbuf[...].reshape(B * SPAN, W).T
    same_head = jnp.where(iota((128, 128), 0) // HD == iota((128, 128), 1) // HD, 1.0, 0.0).astype(BF16)

    @pl.when(source)
    def _():
        loads[1].wait()
        acc = project(0, tp)
        for i, d in ((1, 1), (2, 3), (0, 2)):
            t = lax.rem(tp + TP - d, TP)
            arrived(gath.at[t], hsem.at[i])
            acc = acc + project(0, t)
        qkv[0] = acc.astype(BF16)
        push(qkv.at[0], qkv.at[0], 6, recv.at[5], sibling)
        loads[4].wait()
        for index in (1, 2):
            qkv[index] = sum(project(index, t) for t in range(TP)).astype(BF16)
        push(qkv.at[pl.ds(1, 2)], qkv.at[pl.ds(1, 2)], 7, recv.at[6], sibling)
        for i in range(3):
            pl.semaphore_wait(ready.at[i], 1)
            push(qkv.at[0], qkv.at[0], 6, recv.at[5], served[i])
            push(qkv.at[pl.ds(1, 2)], qkv.at[pl.ds(1, 2)], 7, recv.at[6], served[i])

    @pl.when(fed)
    def _():
        arrived(qkv.at[0], recv.at[5])
        pl.semaphore_wait(ready.at[3], 1)
        push(qkv.at[0], qkv.at[0], 6, recv.at[5], sibling)

    @pl.when(core0_fed)
    def _():
        tell_core1()

    @pl.when(core0)
    def _():
        arrived(qkv.at[0], recv.at[5])

    query = qkv[0]

    spread = jnp.concatenate(
        [jnp.where(column_head == h, query.astype(F32), 0.0) for h in range(4)], axis=0
    ).astype(BF16)
    every = jnp.dot(spread, across[...], preferred_element_type=F32)
    scores = every[:, :128]
    for j in range(1, 8):
        scores = jnp.where(pair == j, every[:, j * 128 : j * 128 + 128], scores)
    scores = jnp.where(valid, scores * HD ** (-0.5), NEG)
    top = jnp.max(scores, axis=1, keepdims=True)
    weights = jnp.where(valid, jnp.exp(scores - top), 0.0)
    total = jnp.sum(weights, axis=1, keepdims=True)
    upper = weights.astype(BF16).astype(F32)
    lower = weights - upper
    wide = jnp.concatenate(
        [
            jnp.concatenate([jnp.where(pair == j, part, 0.0).astype(BF16) for j in range(8)], axis=1)
            for part in (upper, lower)
        ],
        axis=0,
    )
    loads[3].wait()
    both = jnp.dot(wide, vbuf[...].reshape(B * SPAN, W), preferred_element_type=F32)
    summed = both[: 4 * B] + both[4 * B :]

    def fold(rows):
        result = jnp.broadcast_to(rows[0:B], (B, W))
        for h in range(1, 4):
            result = jnp.where(column_head == h, rows[h * B : (h + 1) * B], result)
        return result

    for core in range(2):
        for i, part in enumerate((fold(summed), fold(total), fold(top))):
            csend[core, i] = part[core * HALF : (core + 1) * HALF]
    push(csend.at[1 - c], crecv, 1, recv.at[0], sibling)

    @pl.when(fed)
    def _():
        arrived(qkv.at[pl.ds(1, 2)], recv.at[6])
        push(qkv.at[pl.ds(1, 2)], qkv.at[pl.ds(1, 2)], 7, recv.at[6], sibling)

    arrived(crecv, recv.at[0])
    my_acc, my_total, my_top = csend[c, 0], csend[c, 1], csend[c, 2]
    both_top = jnp.maximum(my_top, crecv[2])
    mine, other = jnp.exp(my_top - both_top), jnp.exp(crecv[2] - both_top)
    both_acc = my_acc * mine + crecv[0] * other
    both_total = my_total * mine + crecv[1] * other

    def place(ref, slot, acc, row):
        base = pl.multiple_of(slot * SLOT, 8)
        ref[pl.ds(base, 8), :] = acc
        ref[pl.ds(base + 8, 1), :] = row

    def slot_of(ref, slot):
        return ref.at[pl.ds(pl.multiple_of(slot * SLOT, 8), SENT), :]

    def wait_ring(ref, sem):
        arrived(ref.at[pl.ds(0, 14 * SENT), :], sem)

    def push_ring(ref, slot_y, slot_z, stage, recv_sem):
        for y_peer, z_peer in zip(y_peers, z_peers):
            push(slot_of(ref, slot_y), slot_of(ref, slot_y), stage, recv_sem, y_peer)
            push(slot_of(ref, slot_z), slot_of(ref, slot_z), stage, recv_sem, z_peer)

    def spread_rows(rows):
        keep = iota((HALF, 128), 1) % HD == iota((HALF, 128), 0)
        return split_dot(
            jnp.concatenate(
                [jnp.where(keep, rows[s : s + 1], 0.0) for s in range(rows.shape[0])], axis=0
            ),
            same_head,
        )

    def ring_acc(ref, factors, first):
        acc = None
        for s in range(first, first + RING):
            part = ref[s * SLOT : s * SLOT + 8, :] * factors[s * 8 : s * 8 + 8]
            acc = part if acc is None else acc + part
        return acc

    def over(first, second):
        return jnp.where(iota((2 * RING, 128), 0) < RING, first, second)

    low_row, high_row = to_row(both_top, both_total)
    place(yb, y, both_acc[:, :128], low_row)
    place(yb, RING + z, both_acc[:, 128:], high_row)

    @pl.when(core0_source)
    def _():
        tell_core1()

    @pl.when(source)
    def _():
        pl.semaphore_wait(ready.at[3], 1)

    push_ring(yb, y, RING + z, 2, recv.at[1])

    @pl.when(core0)
    def _():
        arrived(qkv.at[pl.ds(1, 2)], recv.at[6])

    @pl.when(jnp.logical_not(source))
    def _():
        loads[0].wait()

    new_key, new_value = qkv[1], qkv[2]
    product = query.astype(F32) * new_key.astype(F32)
    halves = split_dot(jnp.concatenate([product[:, :128], product[:, 128:]], axis=0), same_head)
    new_score = jnp.concatenate([halves[:B], halves[B:]], axis=1) * HD ** (-0.5)

    def own_half(rows):
        return jnp.where(c == 0, rows[:HALF], rows[HALF:])

    new_low, new_high = to_row(own_half(new_score), jnp.ones((HALF, W), F32))
    new_acc = own_half(new_value.astype(F32))
    position = iota((SPAN, W), 0)
    for b in range(B):
        hit = position == lens[b] - seq * SPAN
        kbuf[b] = jnp.where(hit, new_key[b : b + 1].astype(F32), kbuf[b].astype(F32)).astype(BF16)
        vbuf[b] = jnp.where(hit, new_value[b : b + 1].astype(F32), vbuf[b].astype(F32)).astype(BF16)
    max_lane = iota((1, 128), 1) % HD < HALF
    wait_ring(yb, recv.at[1])
    rows = yb[pl.ds(8, 2 * RING, stride=SLOT), :]
    low_top = jnp.max(rows[:RING], axis=0, keepdims=True)
    high_top = jnp.max(rows[RING:], axis=0, keepdims=True)
    factor = jnp.exp(rows - over(low_top, high_top))
    totals = rows * pltpu.roll(factor, HALF, 1)
    low_total = jnp.sum(totals[:RING], axis=0, keepdims=True)
    high_total = jnp.sum(totals[RING:], axis=0, keepdims=True)
    factors = spread_rows(factor)
    place(zb, z, ring_acc(yb, factors, 0), jnp.where(max_lane, low_top, low_total))
    place(zb, RING + y, ring_acc(yb, factors, RING), jnp.where(max_lane, high_top, high_total))
    push_ring(zb, RING + y, z, 3, recv.at[2])

    own_hidden = own_half(gath[tp].astype(F32))
    loads[5].wait()
    loads[6].wait()
    loads[7].wait()

    wait_ring(zb, recv.at[2])
    rows = zb[pl.ds(8, 2 * RING, stride=SLOT), :]
    low_top = jnp.maximum(jnp.max(rows[:RING], axis=0, keepdims=True), new_low)
    high_top = jnp.maximum(jnp.max(rows[RING:], axis=0, keepdims=True), new_high)
    factor = jnp.exp(rows - over(low_top, high_top))
    totals = rows * pltpu.roll(factor, HALF, 1)
    low_new, high_new = jnp.exp(new_low - low_top), jnp.exp(new_high - high_top)
    low_total = jnp.sum(totals[:RING], axis=0, keepdims=True) + new_low * pltpu.roll(low_new, HALF, 1)
    high_total = jnp.sum(totals[RING:], axis=0, keepdims=True) + new_high * pltpu.roll(high_new, HALF, 1)
    low_share, high_share = pltpu.roll(low_total, 128 - HALF, 1), pltpu.roll(high_total, 128 - HALF, 1)
    factors = spread_rows(
        jnp.concatenate(
            [factor / over(low_share, high_share), low_new / low_share, high_new / high_share], axis=0
        )
    )
    attended = jnp.concatenate(
        [
            ring_acc(zb, factors, 0) + new_acc[:, :128] * factors[128:136],
            ring_acc(zb, factors, RING) + new_acc[:, 128:] * factors[136:144],
        ],
        axis=1,
    )
    attended = attended.astype(BF16)
    for half in range(2):
        lanes = slice(half * 2 * W, (half + 1) * 2 * W)
        mixed = jnp.dot(attended, wobuf[:, lanes], preferred_element_type=F32)
        for t in (2 * half, 2 * half + 1):
            part = mixed[:, t % 2 * W : (t % 2 + 1) * W]
            mixb[tp, :, t * W : (t + 1) * W] = part + jnp.where(tp == t, own_hidden, 0.0)
        for peer in tp_peers:
            push(mixb.at[tp, :, pl.ds(half * 2 * W, 2 * W)], mixb.at[tp, :, pl.ds(half * 2 * W, 2 * W)], 4, recv.at[3], peer)
    arrived(mixb.at[pl.ds(0, 3)], recv.at[3])
    resid = []
    for t in range(TP):
        lanes = slice(t * W, (t + 1) * W)
        resid.append((mixb[0, :, lanes] + mixb[1, :, lanes]) + (mixb[2, :, lanes] + mixb[3, :, lanes]))
    mean = jnp.sum((resid[0] + resid[1]) + (resid[2] + resid[3]), axis=1, keepdims=True) / D
    centred = [part - mean for part in resid]
    square = [part * part for part in centred]
    var = jnp.sum((square[0] + square[1]) + (square[2] + square[3]), axis=1, keepdims=True) / D
    own = centred[0]
    for t in range(1, TP):
        own = jnp.where(tp == t, centred[t], own)
    fin[c] = own / jnp.sqrt(var + 1e-05) * gbuf[...] + bbuf[...]
    push(fin.at[c], fin.at[c], 5, recv.at[4], sibling)

    @pl.when(source)
    def _():
        arrived(gath.at[pl.ds(0, 3)], sent.at[0])
        arrived(gath, sent.at[6])
        arrived(wbuf.at[0, pl.ds(0, 8 * B), :], sent.at[7])

    @pl.when(fed)
    def _():
        arrived(qkv.at[0], sent.at[6])
        arrived(qkv.at[pl.ds(1, 2)], sent.at[7])

    arrived(crecv, sent.at[1])
    wait_ring(yb, sent.at[2])
    wait_ring(zb, sent.at[3])
    arrived(mixb.at[pl.ds(0, 3)], sent.at[4])
    arrived(fin.at[0], recv.at[4])
    out[...] = jnp.concatenate([fin[0], fin[1]], axis=0).astype(BF16)
    arrived(fin.at[0], sent.at[5])


def hand_out(o_in, k_in, v_in, o_out, k_out, v_out, sem):
    copies = [pltpu.make_async_copy(o_in, o_out, sem.at[0])]
    for i in range(4):
        part = pl.ds(i * B // 4, B // 4)
        copies.append(pltpu.make_async_copy(k_in.at[part], k_out.at[part], sem.at[1 + 2 * i]))
        copies.append(pltpu.make_async_copy(v_in.at[part], v_out.at[part], sem.at[2 + 2 * i]))
    for copy in copies:
        copy.start()
    for copy in copies:
        copy.wait()


def body(hidden_in, w_qkv, w_out, key_cache, value_cache, lengths, ln_gain, ln_bias):
    hbm = pl.BlockSpec(memory_space=pl.ANY)
    vmem = pl.BlockSpec(memory_space=pltpu.VMEM)
    cache = (B, SPAN, W)
    dma = pltpu.SemaphoreType.DMA
    done = pl.pallas_call(
        kernel,
        out_shape=(pltpu.VMEM((B, W), BF16), pltpu.VMEM(cache, BF16), pltpu.VMEM(cache, BF16)),
        in_specs=[hbm] * 8,
        out_specs=(vmem, vmem, vmem),
        scratch_shapes=[
            pltpu.SMEM((B,), jnp.int32),
            pltpu.VMEM((W, B * SPAN), BF16),
            pltpu.VMEM((TP, B, W), BF16),
            pltpu.VMEM((3, B, W), BF16),
            pltpu.VMEM((3, D, W), BF16),
            pltpu.VMEM((W, D), BF16),
            pltpu.VMEM((1, W), F32),
            pltpu.VMEM((1, W), F32),
            pltpu.VMEM((2, 3, HALF, W), F32),
            pltpu.VMEM((3, HALF, W), F32),
            pltpu.VMEM((2 * RING * SLOT, 128), F32),
            pltpu.VMEM((2 * RING * SLOT, 128), F32),
            pltpu.VMEM((TP, HALF, D), F32),
            pltpu.VMEM((2, HALF, W), F32),
            dma((9,)), dma((3,)), dma((7,)), dma((8,)), pltpu.SemaphoreType.REGULAR((4,)),
        ],
        compiler_params=pltpu.CompilerParams(collective_id=0, has_side_effects=True),
        name="sublayer",
    )(
        lengths, hidden_in, w_qkv, w_out, key_cache, value_cache,
        ln_gain.reshape(1, W), ln_bias.reshape(1, W),
    )
    return pl.pallas_call(
        hand_out,
        out_shape=(
            jax.ShapeDtypeStruct((B, W), BF16),
            jax.ShapeDtypeStruct(cache, BF16),
            jax.ShapeDtypeStruct(cache, BF16),
        ),
        in_specs=[vmem] * 3,
        out_specs=(hbm, hbm, hbm),
        scratch_shapes=[dma((9,))],
        name="hand_out",
    )(*[pltpu.with_memory_space_constraint(part, pltpu.VMEM) for part in done])


def solution(mesh):
    in_specs = (
        P(None, "tp"),
        P(None, None, "tp"),
        P("tp", None),
        P(None, "seq", "tp"),
        P(None, "seq", "tp"),
        P(),
        P("tp"),
        P("tp"),
    )
    out_specs = (P(None, "tp"), P(None, "seq", "tp"), P(None, "seq", "tp"))
    return jax.shard_map(body, mesh=mesh, in_specs=in_specs, out_specs=out_specs, check_vma=False)
```

```python
import jax
import jax.numpy as jnp
from jax import lax
from jax.experimental import pallas as pl
from jax.experimental.pallas import tpu as pltpu
from jax.sharding import PartitionSpec as P

D = 1024
HD = 64
B = 16
HALF = 8
W = 256
TP = 4
RING = 8
SPAN = 64
SLOT = 16
SENT = 9
NEG = -1e30
F32 = jnp.float32
BF16 = jnp.bfloat16
MESH = pl.DeviceIdType.MESH


def iota(shape, dim):
    return lax.broadcasted_iota(jnp.int32, shape, dim)


def split_dot(rows, matrix):
    upper = rows.astype(BF16)
    lower = (rows - upper.astype(F32)).astype(BF16)
    both = jnp.dot(jnp.concatenate([upper, lower], axis=0), matrix, preferred_element_type=F32)
    return both[: rows.shape[0]] + both[rows.shape[0] :]


def to_row(tops, totals):
    lane, request = iota((HALF, W), 1) % HD, iota((HALF, W), 0)
    picked = jnp.where(lane == request, tops, jnp.where(lane == request + HALF, totals, 0.0))
    row = jnp.sum(picked, axis=0, keepdims=True)
    return row[:, :128], row[:, 128:]


def kernel(
    lengths, hid, wqkv, wout, kc, vc, gain, bias,
    out, kbuf, vbuf,
    lens, across, gath, qkv, wbuf, wobuf, gbuf, bbuf,
    csend, crecv, yb, zb, mixb, fin,
    lsem, hsem, recv, sent, ready,
):
    seq = lax.axis_index("seq")
    tp = lax.axis_index("tp")
    y, z, c = seq // 16, (seq % 16) // 2, seq % 2

    loads = [
        pltpu.make_async_copy(hid, gath.at[tp], lsem.at[0]),
        pltpu.make_async_copy(wqkv.at[0], wbuf.at[0], lsem.at[1]),
        pltpu.make_async_copy(kc, kbuf, lsem.at[2]),
        pltpu.make_async_copy(vc, vbuf, lsem.at[3]),
        pltpu.make_async_copy(wqkv.at[pl.ds(1, 2)], wbuf.at[pl.ds(1, 2)], lsem.at[4]),
        pltpu.make_async_copy(wout, wobuf, lsem.at[5]),
        pltpu.make_async_copy(gain, gbuf, lsem.at[6]),
        pltpu.make_async_copy(bias, bbuf, lsem.at[7]),
        pltpu.make_async_copy(lengths, lens, lsem.at[8]),
    ]
    tp_peers = [(seq, lax.rem(tp + d, TP)) for d in (2, 1, 3)]
    y_peers = [(lax.rem(y + d, RING) * 16 + z * 2 + c, tp) for d in (4, 3, 5, 2, 6, 1, 7)]
    z_peers = [(y * 16 + lax.rem(z + d, RING) * 2 + c, tp) for d in (4, 3, 5, 2, 6, 1, 7)]
    sibling = (y * 16 + z * 2 + (1 - c), tp)
    y_zero = [(lax.rem(y + d, RING) * 16 + z * 2, tp) for d in (4, 3, 5, 2, 6, 1, 7)]
    z_zero = [(y * 16 + lax.rem(z + d, RING) * 2, tp) for d in (4, 3, 5, 2, 6, 1, 7)]

    barrier = pltpu.get_barrier_semaphore()

    def signal(peer):
        pl.semaphore_signal(barrier, inc=1, device_id=peer, device_id_type=MESH)

    @pl.when(c == 1)
    def _():
        for peer in tp_peers:
            signal(peer)
        loads[0].start()
        for z_peer, y_peer in zip(z_zero, y_zero):
            signal(z_peer)
            signal(y_peer)
        signal(sibling)
        for index in (1, 8, 2, 3, 4, 5, 6, 7):
            loads[index].start()
        loads[0].wait()
        pl.semaphore_wait(barrier, 4)

    @pl.when(c == 0)
    def _():
        signal(sibling)
        for z_peer, y_peer in zip(z_peers, y_peers):
            signal(z_peer)
            signal(y_peer)
        for peer in tp_peers:
            signal(peer)
        for index in (8, 2, 3, 0, 5, 6, 7):
            loads[index].start()

    def push(src, dst, stage, recv_sem, peer):
        pltpu.make_async_remote_copy(
            src, dst, sent.at[stage], recv_sem, device_id=peer, device_id_type=MESH
        ).start()

    def arrived(ref, sem):
        pltpu.make_async_copy(ref, ref, sem).wait()

    def project(index, t):
        rows = pl.ds(pl.multiple_of(t * W, W), W)
        return jnp.dot(gath[t], wbuf[index, rows, :], preferred_element_type=F32)

    @pl.when(c == 1)
    def _():
        for i, peer in enumerate(tp_peers):
            push(gath.at[tp], gath.at[tp], 0, hsem.at[i], peer)

    column_head = iota((B, W), 1) // HD
    row_b = iota((B, 1), 0)
    loads[8].wait()
    local_len = jnp.zeros((B, 1), jnp.int32)
    for b in range(B):
        local_len = jnp.where(row_b == b, lens[b] - seq * SPAN, local_len)
    row_len = jnp.concatenate([local_len] * 4, axis=0)
    request = iota((4 * B, 128), 0) % B
    lane = iota((4 * B, 128), 1)
    valid = jnp.logical_and(lane // SPAN == request % 2, lane % SPAN < row_len)
    pair = request // 2
    loads[2].wait()
    across[...] = kbuf[...].reshape(B * SPAN, W).T
    same_head = jnp.where(iota((128, 128), 0) // HD == iota((128, 128), 1) // HD, 1.0, 0.0).astype(BF16)

    @pl.when(c == 1)
    def _():
        loads[1].wait()
        acc = project(0, tp)
        for i, d in ((1, 1), (2, 3), (0, 2)):
            t = lax.rem(tp + TP - d, TP)
            arrived(gath.at[t], hsem.at[i])
            acc = acc + project(0, t)
        qkv[0] = acc.astype(BF16)
        push(qkv.at[0], qkv.at[0], 6, recv.at[5], sibling)

    @pl.when(c == 0)
    def _():
        loads[0].wait()
        arrived(qkv.at[0], recv.at[5])

    query = qkv[0]

    spread = jnp.concatenate(
        [jnp.where(column_head == h, query.astype(F32), 0.0) for h in range(4)], axis=0
    ).astype(BF16)
    every = jnp.dot(spread, across[...], preferred_element_type=F32)
    scores = every[:, :128]
    for j in range(1, 8):
        scores = jnp.where(pair == j, every[:, j * 128 : j * 128 + 128], scores)
    scores = jnp.where(valid, scores * HD ** (-0.5), NEG)
    top = jnp.max(scores, axis=1, keepdims=True)
    weights = jnp.where(valid, jnp.exp(scores - top), 0.0)
    total = jnp.sum(weights, axis=1, keepdims=True)
    upper = weights.astype(BF16).astype(F32)
    lower = weights - upper
    wide = jnp.concatenate(
        [
            jnp.concatenate([jnp.where(pair == j, part, 0.0).astype(BF16) for j in range(8)], axis=1)
            for part in (upper, lower)
        ],
        axis=0,
    )
    loads[3].wait()
    both = jnp.dot(wide, vbuf[...].reshape(B * SPAN, W), preferred_element_type=F32)
    summed = both[: 4 * B] + both[4 * B :]

    def fold(rows):
        result = jnp.broadcast_to(rows[0:B], (B, W))
        for h in range(1, 4):
            result = jnp.where(column_head == h, rows[h * B : (h + 1) * B], result)
        return result

    for core in range(2):
        for i, part in enumerate((fold(summed), fold(total), fold(top))):
            csend[core, i] = part[core * HALF : (core + 1) * HALF]
    push(csend.at[1 - c], crecv, 1, recv.at[0], sibling)

    @pl.when(c == 1)
    def _():
        loads[4].wait()
        for index in (1, 2):
            qkv[index] = sum(project(index, t) for t in range(TP)).astype(BF16)
        push(qkv.at[pl.ds(1, 2)], qkv.at[pl.ds(1, 2)], 7, recv.at[6], sibling)

    @pl.when(c == 0)
    def _():
        pl.semaphore_wait(barrier, 32)
        pl.semaphore_signal(ready, inc=1, device_id=sibling, device_id_type=MESH)

    arrived(crecv, recv.at[0])
    my_acc, my_total, my_top = csend[c, 0], csend[c, 1], csend[c, 2]
    both_top = jnp.maximum(my_top, crecv[2])
    mine, other = jnp.exp(my_top - both_top), jnp.exp(crecv[2] - both_top)
    both_acc = my_acc * mine + crecv[0] * other
    both_total = my_total * mine + crecv[1] * other

    def place(ref, slot, acc, row):
        base = pl.multiple_of(slot * SLOT, 8)
        ref[pl.ds(base, 8), :] = acc
        ref[pl.ds(base + 8, 1), :] = row

    def slot_of(ref, slot):
        return ref.at[pl.ds(pl.multiple_of(slot * SLOT, 8), SENT), :]

    def wait_ring(ref, sem):
        arrived(ref.at[pl.ds(0, 14 * SENT), :], sem)

    def push_ring(ref, slot_y, slot_z, stage, recv_sem):
        for y_peer, z_peer in zip(y_peers, z_peers):
            push(slot_of(ref, slot_y), slot_of(ref, slot_y), stage, recv_sem, y_peer)
            push(slot_of(ref, slot_z), slot_of(ref, slot_z), stage, recv_sem, z_peer)

    def spread_rows(rows):
        keep = iota((HALF, 128), 1) % HD == iota((HALF, 128), 0)
        return split_dot(
            jnp.concatenate(
                [jnp.where(keep, rows[s : s + 1], 0.0) for s in range(rows.shape[0])], axis=0
            ),
            same_head,
        )

    def ring_acc(ref, factors, first):
        acc = None
        for s in range(first, first + RING):
            part = ref[s * SLOT : s * SLOT + 8, :] * factors[s * 8 : s * 8 + 8]
            acc = part if acc is None else acc + part
        return acc

    def over(first, second):
        return jnp.where(iota((2 * RING, 128), 0) < RING, first, second)

    low_row, high_row = to_row(both_top, both_total)
    place(yb, y, both_acc[:, :128], low_row)
    place(yb, RING + z, both_acc[:, 128:], high_row)

    @pl.when(c == 1)
    def _():
        pl.semaphore_wait(ready, 1)

    push_ring(yb, y, RING + z, 2, recv.at[1])

    @pl.when(c == 0)
    def _():
        arrived(qkv.at[pl.ds(1, 2)], recv.at[6])

    new_key, new_value = qkv[1], qkv[2]
    product = query.astype(F32) * new_key.astype(F32)
    halves = split_dot(jnp.concatenate([product[:, :128], product[:, 128:]], axis=0), same_head)
    new_score = jnp.concatenate([halves[:B], halves[B:]], axis=1) * HD ** (-0.5)

    def own_half(rows):
        return jnp.where(c == 0, rows[:HALF], rows[HALF:])

    new_low, new_high = to_row(own_half(new_score), jnp.ones((HALF, W), F32))
    new_acc = own_half(new_value.astype(F32))
    position = iota((SPAN, W), 0)
    for b in range(B):
        hit = position == lens[b] - seq * SPAN
        kbuf[b] = jnp.where(hit, new_key[b : b + 1].astype(F32), kbuf[b].astype(F32)).astype(BF16)
        vbuf[b] = jnp.where(hit, new_value[b : b + 1].astype(F32), vbuf[b].astype(F32)).astype(BF16)
    max_lane = iota((1, 128), 1) % HD < HALF
    wait_ring(yb, recv.at[1])
    rows = yb[pl.ds(8, 2 * RING, stride=SLOT), :]
    low_top = jnp.max(rows[:RING], axis=0, keepdims=True)
    high_top = jnp.max(rows[RING:], axis=0, keepdims=True)
    factor = jnp.exp(rows - over(low_top, high_top))
    totals = rows * pltpu.roll(factor, HALF, 1)
    low_total = jnp.sum(totals[:RING], axis=0, keepdims=True)
    high_total = jnp.sum(totals[RING:], axis=0, keepdims=True)
    factors = spread_rows(factor)
    place(zb, z, ring_acc(yb, factors, 0), jnp.where(max_lane, low_top, low_total))
    place(zb, RING + y, ring_acc(yb, factors, RING), jnp.where(max_lane, high_top, high_total))
    push_ring(zb, RING + y, z, 3, recv.at[2])

    own_hidden = own_half(gath[tp].astype(F32))
    loads[5].wait()
    loads[6].wait()
    loads[7].wait()

    wait_ring(zb, recv.at[2])
    rows = zb[pl.ds(8, 2 * RING, stride=SLOT), :]
    low_top = jnp.maximum(jnp.max(rows[:RING], axis=0, keepdims=True), new_low)
    high_top = jnp.maximum(jnp.max(rows[RING:], axis=0, keepdims=True), new_high)
    factor = jnp.exp(rows - over(low_top, high_top))
    totals = rows * pltpu.roll(factor, HALF, 1)
    low_new, high_new = jnp.exp(new_low - low_top), jnp.exp(new_high - high_top)
    low_total = jnp.sum(totals[:RING], axis=0, keepdims=True) + new_low * pltpu.roll(low_new, HALF, 1)
    high_total = jnp.sum(totals[RING:], axis=0, keepdims=True) + new_high * pltpu.roll(high_new, HALF, 1)
    low_share, high_share = pltpu.roll(low_total, 128 - HALF, 1), pltpu.roll(high_total, 128 - HALF, 1)
    factors = spread_rows(
        jnp.concatenate(
            [factor / over(low_share, high_share), low_new / low_share, high_new / high_share], axis=0
        )
    )
    attended = jnp.concatenate(
        [
            ring_acc(zb, factors, 0) + new_acc[:, :128] * factors[128:136],
            ring_acc(zb, factors, RING) + new_acc[:, 128:] * factors[136:144],
        ],
        axis=1,
    )
    attended = attended.astype(BF16)
    for half in range(2):
        lanes = slice(half * 2 * W, (half + 1) * 2 * W)
        mixed = jnp.dot(attended, wobuf[:, lanes], preferred_element_type=F32)
        for t in (2 * half, 2 * half + 1):
            part = mixed[:, t % 2 * W : (t % 2 + 1) * W]
            mixb[tp, :, t * W : (t + 1) * W] = part + jnp.where(tp == t, own_hidden, 0.0)
        for peer in tp_peers:
            push(mixb.at[tp, :, pl.ds(half * 2 * W, 2 * W)], mixb.at[tp, :, pl.ds(half * 2 * W, 2 * W)], 4, recv.at[3], peer)
    arrived(mixb.at[pl.ds(0, 3)], recv.at[3])
    resid = []
    for t in range(TP):
        lanes = slice(t * W, (t + 1) * W)
        resid.append((mixb[0, :, lanes] + mixb[1, :, lanes]) + (mixb[2, :, lanes] + mixb[3, :, lanes]))
    mean = jnp.sum((resid[0] + resid[1]) + (resid[2] + resid[3]), axis=1, keepdims=True) / D
    centred = [part - mean for part in resid]
    square = [part * part for part in centred]
    var = jnp.sum((square[0] + square[1]) + (square[2] + square[3]), axis=1, keepdims=True) / D
    own = centred[0]
    for t in range(1, TP):
        own = jnp.where(tp == t, centred[t], own)
    fin[c] = own / jnp.sqrt(var + 1e-05) * gbuf[...] + bbuf[...]
    push(fin.at[c], fin.at[c], 5, recv.at[4], sibling)

    @pl.when(c == 1)
    def _():
        arrived(gath.at[pl.ds(0, 3)], sent.at[0])
        arrived(qkv.at[0], sent.at[6])
        arrived(qkv.at[pl.ds(1, 2)], sent.at[7])

    arrived(crecv, sent.at[1])
    wait_ring(yb, sent.at[2])
    wait_ring(zb, sent.at[3])
    arrived(mixb.at[pl.ds(0, 3)], sent.at[4])
    arrived(fin.at[0], recv.at[4])
    out[...] = jnp.concatenate([fin[0], fin[1]], axis=0).astype(BF16)
    arrived(fin.at[0], sent.at[5])


def hand_out(o_in, k_in, v_in, o_out, k_out, v_out, sem):
    copies = [pltpu.make_async_copy(o_in, o_out, sem.at[0])]
    for i in range(4):
        part = pl.ds(i * B // 4, B // 4)
        copies.append(pltpu.make_async_copy(k_in.at[part], k_out.at[part], sem.at[1 + 2 * i]))
        copies.append(pltpu.make_async_copy(v_in.at[part], v_out.at[part], sem.at[2 + 2 * i]))
    for copy in copies:
        copy.start()
    for copy in copies:
        copy.wait()


def body(hidden_in, w_qkv, w_out, key_cache, value_cache, lengths, ln_gain, ln_bias):
    hbm = pl.BlockSpec(memory_space=pl.ANY)
    vmem = pl.BlockSpec(memory_space=pltpu.VMEM)
    cache = (B, SPAN, W)
    dma = pltpu.SemaphoreType.DMA
    done = pl.pallas_call(
        kernel,
        out_shape=(pltpu.VMEM((B, W), BF16), pltpu.VMEM(cache, BF16), pltpu.VMEM(cache, BF16)),
        in_specs=[hbm] * 8,
        out_specs=(vmem, vmem, vmem),
        scratch_shapes=[
            pltpu.SMEM((B,), jnp.int32),
            pltpu.VMEM((W, B * SPAN), BF16),
            pltpu.VMEM((TP, B, W), BF16),
            pltpu.VMEM((3, B, W), BF16),
            pltpu.VMEM((3, D, W), BF16),
            pltpu.VMEM((W, D), BF16),
            pltpu.VMEM((1, W), F32),
            pltpu.VMEM((1, W), F32),
            pltpu.VMEM((2, 3, HALF, W), F32),
            pltpu.VMEM((3, HALF, W), F32),
            pltpu.VMEM((2 * RING * SLOT, 128), F32),
            pltpu.VMEM((2 * RING * SLOT, 128), F32),
            pltpu.VMEM((TP, HALF, D), F32),
            pltpu.VMEM((2, HALF, W), F32),
            dma((9,)), dma((3,)), dma((7,)), dma((8,)), pltpu.SemaphoreType.REGULAR,
        ],
        compiler_params=pltpu.CompilerParams(collective_id=0, has_side_effects=True),
        name="sublayer",
    )(
        lengths, hidden_in, w_qkv, w_out, key_cache, value_cache,
        ln_gain.reshape(1, W), ln_bias.reshape(1, W),
    )
    return pl.pallas_call(
        hand_out,
        out_shape=(
            jax.ShapeDtypeStruct((B, W), BF16),
            jax.ShapeDtypeStruct(cache, BF16),
            jax.ShapeDtypeStruct(cache, BF16),
        ),
        in_specs=[vmem] * 3,
        out_specs=(hbm, hbm, hbm),
        scratch_shapes=[dma((9,))],
        name="hand_out",
    )(*[pltpu.with_memory_space_constraint(part, pltpu.VMEM) for part in done])


def solution(mesh):
    in_specs = (
        P(None, "tp"),
        P(None, None, "tp"),
        P("tp", None),
        P(None, "seq", "tp"),
        P(None, "seq", "tp"),
        P(),
        P("tp"),
        P("tp"),
    )
    out_specs = (P(None, "tp"), P(None, "seq", "tp"), P(None, "seq", "tp"))
    return jax.shard_map(body, mesh=mesh, in_specs=in_specs, out_specs=out_specs, check_vma=False)
```

```python
import jax
import jax.numpy as jnp
from jax import lax
from jax.experimental import pallas as pl
from jax.experimental.pallas import tpu as pltpu
from jax.sharding import PartitionSpec as P

D = 1024
HD = 64
B = 16
HALF = 8
W = 256
TP = 4
RING = 8
SPAN = 64
SLOT = 16
SENT = 9
NEG = -1e30
F32 = jnp.float32
BF16 = jnp.bfloat16
MESH = pl.DeviceIdType.MESH


def iota(shape, dim):
    return lax.broadcasted_iota(jnp.int32, shape, dim)


def split_dot(rows, matrix):
    upper = rows.astype(BF16)
    lower = (rows - upper.astype(F32)).astype(BF16)
    both = jnp.dot(jnp.concatenate([upper, lower], axis=0), matrix, preferred_element_type=F32)
    return both[: rows.shape[0]] + both[rows.shape[0] :]


def to_row(tops, totals):
    lane, request = iota((HALF, W), 1) % HD, iota((HALF, W), 0)
    picked = jnp.where(lane == request, tops, jnp.where(lane == request + HALF, totals, 0.0))
    row = jnp.sum(picked, axis=0, keepdims=True)
    return row[:, :128], row[:, 128:]


def kernel(
    lengths, hid, wqkv, wout, kc, vc, gain, bias,
    out, kbuf, vbuf,
    lens, across, gath, qkv, wbuf, wobuf, gbuf, bbuf,
    csend, crecv, staged, yb, zb, mixb, fin,
    lsem, hsem, recv, sent, ready,
):
    seq = lax.axis_index("seq")
    tp = lax.axis_index("tp")
    y, z, c = seq // 16, (seq % 16) // 2, seq % 2

    loads = [
        pltpu.make_async_copy(hid, gath.at[tp], lsem.at[0]),
        pltpu.make_async_copy(wqkv.at[0], wbuf.at[0], lsem.at[1]),
        pltpu.make_async_copy(kc, kbuf, lsem.at[2]),
        pltpu.make_async_copy(vc, vbuf, lsem.at[3]),
        pltpu.make_async_copy(wqkv.at[pl.ds(1, 2)], wbuf.at[pl.ds(1, 2)], lsem.at[4]),
        pltpu.make_async_copy(wout, wobuf, lsem.at[5]),
        pltpu.make_async_copy(gain, gbuf, lsem.at[6]),
        pltpu.make_async_copy(bias, bbuf, lsem.at[7]),
        pltpu.make_async_copy(lengths, lens, lsem.at[8]),
    ]
    tp_peers = [(seq, lax.rem(tp + d, TP)) for d in (2, 1, 3)]
    y_peers = [(lax.rem(y + d, RING) * 16 + z * 2 + c, tp) for d in (4, 3, 5, 2, 6, 1, 7)]
    z_peers = [(y * 16 + lax.rem(z + d, RING) * 2 + c, tp) for d in (4, 3, 5, 2, 6, 1, 7)]
    sibling = (y * 16 + z * 2 + (1 - c), tp)
    y_zero = [(lax.rem(y + d, RING) * 16 + z * 2, tp) for d in (4, 3, 5, 2, 6, 1, 7)]
    z_zero = [(y * 16 + lax.rem(z + d, RING) * 2, tp) for d in (4, 3, 5, 2, 6, 1, 7)]

    y_one = [(peer[0] + 1, tp) for peer in y_zero]
    z_one = [(peer[0] + 1, tp) for peer in z_zero]

    barrier = pltpu.get_barrier_semaphore()

    def signal(peer):
        pl.semaphore_signal(barrier, inc=1, device_id=peer, device_id_type=MESH)

    @pl.when(c == 1)
    def _():
        for peer in tp_peers:
            signal(peer)
        loads[0].start()
        for z_peer, y_peer in zip(z_zero, y_zero):
            signal(z_peer)
            signal(y_peer)
        signal(sibling)
        for index in (1, 8, 2, 3, 4, 5, 6, 7):
            loads[index].start()
        loads[0].wait()
        pl.semaphore_wait(barrier, 4)

    @pl.when(c == 0)
    def _():
        signal(sibling)
        for z_peer, y_peer in zip(z_peers, y_peers):
            signal(z_peer)
            signal(y_peer)
        for peer in tp_peers:
            signal(peer)
        for index in (8, 2, 3, 0, 5, 6, 7):
            loads[index].start()

    def push(src, dst, stage, recv_sem, peer):
        pltpu.make_async_remote_copy(
            src, dst, sent.at[stage], recv_sem, device_id=peer, device_id_type=MESH
        ).start()

    def arrived(ref, sem):
        pltpu.make_async_copy(ref, ref, sem).wait()

    def project(index, t):
        rows = pl.ds(pl.multiple_of(t * W, W), W)
        return jnp.dot(gath[t], wbuf[index, rows, :], preferred_element_type=F32)

    @pl.when(c == 1)
    def _():
        for i, peer in enumerate(tp_peers):
            push(gath.at[tp], gath.at[tp], 0, hsem.at[i], peer)

    column_head = iota((B, W), 1) // HD
    row_b = iota((B, 1), 0)
    loads[8].wait()
    local_len = jnp.zeros((B, 1), jnp.int32)
    for b in range(B):
        local_len = jnp.where(row_b == b, lens[b] - seq * SPAN, local_len)
    row_len = jnp.concatenate([local_len] * 4, axis=0)
    request = iota((4 * B, 128), 0) % B
    lane = iota((4 * B, 128), 1)
    valid = jnp.logical_and(lane // SPAN == request % 2, lane % SPAN < row_len)
    pair = request // 2
    loads[2].wait()
    across[...] = kbuf[...].reshape(B * SPAN, W).T
    same_head = jnp.where(iota((128, 128), 0) // HD == iota((128, 128), 1) // HD, 1.0, 0.0).astype(BF16)

    @pl.when(c == 1)
    def _():
        loads[1].wait()
        acc = project(0, tp)
        for i, d in ((1, 1), (2, 3), (0, 2)):
            t = lax.rem(tp + TP - d, TP)
            arrived(gath.at[t], hsem.at[i])
            acc = acc + project(0, t)
        qkv[0] = acc.astype(BF16)
        push(qkv.at[0], qkv.at[0], 6, recv.at[5], sibling)

    @pl.when(c == 0)
    def _():
        loads[0].wait()
        arrived(qkv.at[0], recv.at[5])

    query = qkv[0]

    spread = jnp.concatenate(
        [jnp.where(column_head == h, query.astype(F32), 0.0) for h in range(4)], axis=0
    ).astype(BF16)
    every = jnp.dot(spread, across[...], preferred_element_type=F32)
    scores = every[:, :128]
    for j in range(1, 8):
        scores = jnp.where(pair == j, every[:, j * 128 : j * 128 + 128], scores)
    scores = jnp.where(valid, scores * HD ** (-0.5), NEG)
    top = jnp.max(scores, axis=1, keepdims=True)
    weights = jnp.where(valid, jnp.exp(scores - top), 0.0)
    total = jnp.sum(weights, axis=1, keepdims=True)
    upper = weights.astype(BF16).astype(F32)
    lower = weights - upper
    wide = jnp.concatenate(
        [
            jnp.concatenate([jnp.where(pair == j, part, 0.0).astype(BF16) for j in range(8)], axis=1)
            for part in (upper, lower)
        ],
        axis=0,
    )
    loads[3].wait()
    both = jnp.dot(wide, vbuf[...].reshape(B * SPAN, W), preferred_element_type=F32)
    summed = both[: 4 * B] + both[4 * B :]

    def fold(rows):
        result = jnp.broadcast_to(rows[0:B], (B, W))
        for h in range(1, 4):
            result = jnp.where(column_head == h, rows[h * B : (h + 1) * B], result)
        return result

    for core in range(2):
        for i, part in enumerate((fold(summed), fold(total), fold(top))):
            csend[core, i] = part[core * HALF : (core + 1) * HALF]

    @pl.when(c == 1)
    def _():
        push(csend, crecv, 1, recv.at[0], sibling)

    @pl.when(c == 1)
    def _():
        loads[4].wait()
        for index in (1, 2):
            qkv[index] = sum(project(index, t) for t in range(TP)).astype(BF16)
        push(qkv.at[pl.ds(1, 2)], qkv.at[pl.ds(1, 2)], 7, recv.at[6], sibling)

    @pl.when(c == 0)
    def _():
        pl.semaphore_wait(barrier, 32)
        pl.semaphore_signal(ready, inc=1, device_id=sibling, device_id_type=MESH)

    def place(ref, slot, acc, row):
        base = pl.multiple_of(slot * SLOT, 8)
        ref[pl.ds(base, 8), :] = acc
        ref[pl.ds(base + 8, 1), :] = row

    def slot_of(ref, slot):
        return ref.at[pl.ds(pl.multiple_of(slot * SLOT, 8), SENT), :]

    def wait_ring(ref, sem, slots=14):
        arrived(ref.at[pl.ds(0, slots * SENT), :], sem)

    def push_ring(ref, slot_y, slot_z, stage, recv_sem):
        for y_peer, z_peer in zip(y_peers, z_peers):
            push(slot_of(ref, slot_y), slot_of(ref, slot_y), stage, recv_sem, y_peer)
            push(slot_of(ref, slot_z), slot_of(ref, slot_z), stage, recv_sem, z_peer)

    def spread_rows(rows):
        keep = iota((HALF, 128), 1) % HD == iota((HALF, 128), 0)
        return split_dot(
            jnp.concatenate(
                [jnp.where(keep, rows[s : s + 1], 0.0) for s in range(rows.shape[0])], axis=0
            ),
            same_head,
        )

    def ring_acc(ref, factors, first):
        acc = None
        for s in range(first, first + RING):
            part = ref[s * SLOT : s * SLOT + 8, :] * factors[s * 8 : s * 8 + 8]
            acc = part if acc is None else acc + part
        return acc

    def over(first, second):
        return jnp.where(iota((2 * RING, 128), 0) < RING, first, second)

    @pl.when(c == 0)
    def _():
        arrived(crecv, recv.at[0])
        for core, ref, low_slot, high_slot in ((0, yb, y, RING + z), (1, staged, 0, 1)):
            both_top = jnp.maximum(csend[core, 2], crecv[core, 2])
            mine, other = jnp.exp(csend[core, 2] - both_top), jnp.exp(crecv[core, 2] - both_top)
            both_acc = csend[core, 0] * mine + crecv[core, 0] * other
            both_total = csend[core, 1] * mine + crecv[core, 1] * other
            low_row, high_row = to_row(both_top, both_total)
            place(ref, low_slot, both_acc[:, :128], low_row)
            place(ref, high_slot, both_acc[:, 128:], high_row)
        for i in range(RING - 1):
            push(slot_of(yb, y), slot_of(yb, y), 2, recv.at[1], y_peers[i])
            push(slot_of(yb, RING + z), slot_of(yb, RING + z), 2, recv.at[1], z_peers[i])
            push(slot_of(staged, 0), slot_of(yb, y), 2, recv.at[1], y_one[i])
            push(slot_of(staged, 1), slot_of(yb, RING + z), 2, recv.at[1], z_one[i])
        push(slot_of(staged, 0), slot_of(yb, y), 2, recv.at[1], sibling)
        push(slot_of(staged, 1), slot_of(yb, RING + z), 2, recv.at[1], sibling)

    @pl.when(c == 0)
    def _():
        arrived(qkv.at[pl.ds(1, 2)], recv.at[6])

    new_key, new_value = qkv[1], qkv[2]
    product = query.astype(F32) * new_key.astype(F32)
    halves = split_dot(jnp.concatenate([product[:, :128], product[:, 128:]], axis=0), same_head)
    new_score = jnp.concatenate([halves[:B], halves[B:]], axis=1) * HD ** (-0.5)

    def own_half(rows):
        return jnp.where(c == 0, rows[:HALF], rows[HALF:])

    new_low, new_high = to_row(own_half(new_score), jnp.ones((HALF, W), F32))
    new_acc = own_half(new_value.astype(F32))
    position = iota((SPAN, W), 0)
    for b in range(B):
        hit = position == lens[b] - seq * SPAN
        kbuf[b] = jnp.where(hit, new_key[b : b + 1].astype(F32), kbuf[b].astype(F32)).astype(BF16)
        vbuf[b] = jnp.where(hit, new_value[b : b + 1].astype(F32), vbuf[b].astype(F32)).astype(BF16)
    max_lane = iota((1, 128), 1) % HD < HALF

    @pl.when(c == 0)
    def _():
        wait_ring(yb, recv.at[1])

    @pl.when(c == 1)
    def _():
        wait_ring(yb, recv.at[1], 16)

    rows = yb[pl.ds(8, 2 * RING, stride=SLOT), :]
    low_top = jnp.max(rows[:RING], axis=0, keepdims=True)
    high_top = jnp.max(rows[RING:], axis=0, keepdims=True)
    factor = jnp.exp(rows - over(low_top, high_top))
    totals = rows * pltpu.roll(factor, HALF, 1)
    low_total = jnp.sum(totals[:RING], axis=0, keepdims=True)
    high_total = jnp.sum(totals[RING:], axis=0, keepdims=True)
    factors = spread_rows(factor)
    place(zb, z, ring_acc(yb, factors, 0), jnp.where(max_lane, low_top, low_total))
    place(zb, RING + y, ring_acc(yb, factors, RING), jnp.where(max_lane, high_top, high_total))

    @pl.when(c == 1)
    def _():
        pl.semaphore_wait(ready, 1)

    push_ring(zb, RING + y, z, 3, recv.at[2])

    own_hidden = own_half(gath[tp].astype(F32))
    loads[5].wait()
    loads[6].wait()
    loads[7].wait()

    wait_ring(zb, recv.at[2])
    rows = zb[pl.ds(8, 2 * RING, stride=SLOT), :]
    low_top = jnp.maximum(jnp.max(rows[:RING], axis=0, keepdims=True), new_low)
    high_top = jnp.maximum(jnp.max(rows[RING:], axis=0, keepdims=True), new_high)
    factor = jnp.exp(rows - over(low_top, high_top))
    totals = rows * pltpu.roll(factor, HALF, 1)
    low_new, high_new = jnp.exp(new_low - low_top), jnp.exp(new_high - high_top)
    low_total = jnp.sum(totals[:RING], axis=0, keepdims=True) + new_low * pltpu.roll(low_new, HALF, 1)
    high_total = jnp.sum(totals[RING:], axis=0, keepdims=True) + new_high * pltpu.roll(high_new, HALF, 1)
    low_share, high_share = pltpu.roll(low_total, 128 - HALF, 1), pltpu.roll(high_total, 128 - HALF, 1)
    factors = spread_rows(
        jnp.concatenate(
            [factor / over(low_share, high_share), low_new / low_share, high_new / high_share], axis=0
        )
    )
    attended = jnp.concatenate(
        [
            ring_acc(zb, factors, 0) + new_acc[:, :128] * factors[128:136],
            ring_acc(zb, factors, RING) + new_acc[:, 128:] * factors[136:144],
        ],
        axis=1,
    )
    attended = attended.astype(BF16)
    for half in range(2):
        lanes = slice(half * 2 * W, (half + 1) * 2 * W)
        mixed = jnp.dot(attended, wobuf[:, lanes], preferred_element_type=F32)
        for t in (2 * half, 2 * half + 1):
            part = mixed[:, t % 2 * W : (t % 2 + 1) * W]
            mixb[tp, :, t * W : (t + 1) * W] = part + jnp.where(tp == t, own_hidden, 0.0)
        for peer in tp_peers:
            push(mixb.at[tp, :, pl.ds(half * 2 * W, 2 * W)], mixb.at[tp, :, pl.ds(half * 2 * W, 2 * W)], 4, recv.at[3], peer)
    arrived(mixb.at[pl.ds(0, 3)], recv.at[3])
    resid = []
    for t in range(TP):
        lanes = slice(t * W, (t + 1) * W)
        resid.append((mixb[0, :, lanes] + mixb[1, :, lanes]) + (mixb[2, :, lanes] + mixb[3, :, lanes]))
    mean = jnp.sum((resid[0] + resid[1]) + (resid[2] + resid[3]), axis=1, keepdims=True) / D
    centred = [part - mean for part in resid]
    square = [part * part for part in centred]
    var = jnp.sum((square[0] + square[1]) + (square[2] + square[3]), axis=1, keepdims=True) / D
    own = centred[0]
    for t in range(1, TP):
        own = jnp.where(tp == t, centred[t], own)
    fin[c] = own / jnp.sqrt(var + 1e-05) * gbuf[...] + bbuf[...]
    push(fin.at[c], fin.at[c], 5, recv.at[4], sibling)

    @pl.when(c == 1)
    def _():
        arrived(gath.at[pl.ds(0, 3)], sent.at[0])
        arrived(qkv.at[0], sent.at[6])
        arrived(qkv.at[pl.ds(1, 2)], sent.at[7])

    @pl.when(c == 1)
    def _():
        arrived(csend, sent.at[1])

    @pl.when(c == 0)
    def _():
        arrived(yb.at[pl.ds(0, 30 * SENT), :], sent.at[2])

    wait_ring(zb, sent.at[3])
    arrived(mixb.at[pl.ds(0, 3)], sent.at[4])
    arrived(fin.at[0], recv.at[4])
    out[...] = jnp.concatenate([fin[0], fin[1]], axis=0).astype(BF16)
    arrived(fin.at[0], sent.at[5])


def hand_out(o_in, k_in, v_in, o_out, k_out, v_out, sem):
    copies = [pltpu.make_async_copy(o_in, o_out, sem.at[0])]
    for i in range(4):
        part = pl.ds(i * B // 4, B // 4)
        copies.append(pltpu.make_async_copy(k_in.at[part], k_out.at[part], sem.at[1 + 2 * i]))
        copies.append(pltpu.make_async_copy(v_in.at[part], v_out.at[part], sem.at[2 + 2 * i]))
    for copy in copies:
        copy.start()
    for copy in copies:
        copy.wait()


def body(hidden_in, w_qkv, w_out, key_cache, value_cache, lengths, ln_gain, ln_bias):
    hbm = pl.BlockSpec(memory_space=pl.ANY)
    vmem = pl.BlockSpec(memory_space=pltpu.VMEM)
    cache = (B, SPAN, W)
    dma = pltpu.SemaphoreType.DMA
    done = pl.pallas_call(
        kernel,
        out_shape=(pltpu.VMEM((B, W), BF16), pltpu.VMEM(cache, BF16), pltpu.VMEM(cache, BF16)),
        in_specs=[hbm] * 8,
        out_specs=(vmem, vmem, vmem),
        scratch_shapes=[
            pltpu.SMEM((B,), jnp.int32),
            pltpu.VMEM((W, B * SPAN), BF16),
            pltpu.VMEM((TP, B, W), BF16),
            pltpu.VMEM((3, B, W), BF16),
            pltpu.VMEM((3, D, W), BF16),
            pltpu.VMEM((W, D), BF16),
            pltpu.VMEM((1, W), F32),
            pltpu.VMEM((1, W), F32),
            pltpu.VMEM((2, 3, HALF, W), F32),
            pltpu.VMEM((2, 3, HALF, W), F32),
            pltpu.VMEM((2 * SLOT, 128), F32),
            pltpu.VMEM((2 * (RING + 1) * SLOT, 128), F32),
            pltpu.VMEM((2 * RING * SLOT, 128), F32),
            pltpu.VMEM((TP, HALF, D), F32),
            pltpu.VMEM((2, HALF, W), F32),
            dma((9,)), dma((3,)), dma((7,)), dma((8,)), pltpu.SemaphoreType.REGULAR,
        ],
        compiler_params=pltpu.CompilerParams(collective_id=0, has_side_effects=True),
        name="sublayer",
    )(
        lengths, hidden_in, w_qkv, w_out, key_cache, value_cache,
        ln_gain.reshape(1, W), ln_bias.reshape(1, W),
    )
    return pl.pallas_call(
        hand_out,
        out_shape=(
            jax.ShapeDtypeStruct((B, W), BF16),
            jax.ShapeDtypeStruct(cache, BF16),
            jax.ShapeDtypeStruct(cache, BF16),
        ),
        in_specs=[vmem] * 3,
        out_specs=(hbm, hbm, hbm),
        scratch_shapes=[dma((9,))],
        name="hand_out",
    )(*[pltpu.with_memory_space_constraint(part, pltpu.VMEM) for part in done])


def solution(mesh):
    in_specs = (
        P(None, "tp"),
        P(None, None, "tp"),
        P("tp", None),
        P(None, "seq", "tp"),
        P(None, "seq", "tp"),
        P(),
        P("tp"),
        P("tp"),
    )
    out_specs = (P(None, "tp"), P(None, "seq", "tp"), P(None, "seq", "tp"))
    return jax.shard_map(body, mesh=mesh, in_specs=in_specs, out_specs=out_specs, check_vma=False)
```

```python
import jax
import jax.numpy as jnp
from jax import lax
from jax.experimental import pallas as pl
from jax.experimental.pallas import tpu as pltpu
from jax.sharding import PartitionSpec as P

D = 1024
HD = 64
B = 16
HALF = 8
W = 256
TP = 4
RING = 8
SPAN = 64
SLOT = 16
SENT = 9
NEG = -1e30
F32 = jnp.float32
BF16 = jnp.bfloat16
MESH = pl.DeviceIdType.MESH


def iota(shape, dim):
    return lax.broadcasted_iota(jnp.int32, shape, dim)


def split_dot(rows, matrix):
    upper = rows.astype(BF16)
    lower = (rows - upper.astype(F32)).astype(BF16)
    both = jnp.dot(jnp.concatenate([upper, lower], axis=0), matrix, preferred_element_type=F32)
    return both[: rows.shape[0]] + both[rows.shape[0] :]


def to_row(tops, totals):
    lane, request = iota((HALF, W), 1) % HD, iota((HALF, W), 0)
    picked = jnp.where(lane == request, tops, jnp.where(lane == request + HALF, totals, 0.0))
    row = jnp.sum(picked, axis=0, keepdims=True)
    return row[:, :128], row[:, 128:]


def kernel(
    lengths, hid, wqkv, wout, kc, vc, gain, bias,
    out, kbuf, vbuf,
    lens, across, gath, qkv, wbuf, wobuf, gbuf, bbuf,
    csend, crecv, yb, zb, mixb, fin,
    lsem, hsem, recv, sent, ready,
):
    seq = lax.axis_index("seq")
    tp = lax.axis_index("tp")
    y, z, c = seq // 16, (seq % 16) // 2, seq % 2

    loads = [
        pltpu.make_async_copy(hid, gath.at[tp], lsem.at[0]),
        pltpu.make_async_copy(wqkv.at[0], wbuf.at[0], lsem.at[1]),
        pltpu.make_async_copy(kc, kbuf, lsem.at[2]),
        pltpu.make_async_copy(vc, vbuf, lsem.at[3]),
        pltpu.make_async_copy(wqkv.at[pl.ds(1, 2)], wbuf.at[pl.ds(1, 2)], lsem.at[4]),
        pltpu.make_async_copy(wout, wobuf, lsem.at[5]),
        pltpu.make_async_copy(gain, gbuf, lsem.at[6]),
        pltpu.make_async_copy(bias, bbuf, lsem.at[7]),
        pltpu.make_async_copy(lengths, lens, lsem.at[8]),
    ]
    tp_peers = [(seq, lax.rem(tp + d, TP)) for d in (2, 1, 3)]
    y_peers = [(lax.rem(y + d, RING) * 16 + z * 2 + c, tp) for d in (4, 3, 5, 2, 6, 1, 7)]
    z_peers = [(y * 16 + lax.rem(z + d, RING) * 2 + c, tp) for d in (4, 3, 5, 2, 6, 1, 7)]
    sibling = (y * 16 + z * 2 + (1 - c), tp)
    y_zero = [(lax.rem(y + d, RING) * 16 + z * 2, tp) for d in (4, 3, 5, 2, 6, 1, 7)]
    z_zero = [(y * 16 + lax.rem(z + d, RING) * 2, tp) for d in (4, 3, 5, 2, 6, 1, 7)]

    barrier = pltpu.get_barrier_semaphore()

    def signal(peer):
        pl.semaphore_signal(barrier, inc=1, device_id=peer, device_id_type=MESH)

    @pl.when(c == 1)
    def _():
        for peer in tp_peers:
            signal(peer)
        loads[0].start()
        for z_peer, y_peer in zip(z_zero, y_zero):
            signal(z_peer)
            signal(y_peer)
        signal(sibling)
        for index in (1, 8, 2, 3, 4, 5, 6, 7):
            loads[index].start()
        loads[0].wait()
        pl.semaphore_wait(barrier, 4)

    @pl.when(c == 0)
    def _():
        signal(sibling)
        for z_peer, y_peer in zip(z_peers, y_peers):
            signal(z_peer)
            signal(y_peer)
        for peer in tp_peers:
            signal(peer)
        for index in (8, 2, 3, 0, 5, 6, 7):
            loads[index].start()

    def push(src, dst, stage, recv_sem, peer):
        pltpu.make_async_remote_copy(
            src, dst, sent.at[stage], recv_sem, device_id=peer, device_id_type=MESH
        ).start()

    def arrived(ref, sem):
        pltpu.make_async_copy(ref, ref, sem).wait()

    def project(index, t):
        rows = pl.ds(pl.multiple_of(t * W, W), W)
        return jnp.dot(gath[t], wbuf[index, rows, :], preferred_element_type=F32)

    @pl.when(c == 1)
    def _():
        for i, peer in enumerate(tp_peers):
            push(gath.at[tp], gath.at[tp], 0, hsem.at[i], peer)

    column_head = iota((B, W), 1) // HD
    row_b = iota((B, 1), 0)
    loads[8].wait()
    local_len = jnp.zeros((B, 1), jnp.int32)
    for b in range(B):
        local_len = jnp.where(row_b == b, lens[b] - seq * SPAN, local_len)
    row_len = jnp.concatenate([local_len] * 4, axis=0)
    request = iota((4 * B, 128), 0) % B
    lane = iota((4 * B, 128), 1)
    valid = jnp.logical_and(lane // SPAN == request % 2, lane % SPAN < row_len)
    pair = request // 2
    loads[2].wait()
    across[...] = kbuf[...].reshape(B * SPAN, W).T
    same_head = jnp.where(iota((128, 128), 0) // HD == iota((128, 128), 1) // HD, 1.0, 0.0).astype(BF16)

    @pl.when(c == 1)
    def _():
        loads[1].wait()
        acc = project(0, tp)
        for i, d in ((1, 1), (2, 3), (0, 2)):
            t = lax.rem(tp + TP - d, TP)
            arrived(gath.at[t], hsem.at[i])
            acc = acc + project(0, t)
        qkv[0] = acc.astype(BF16)
        push(qkv.at[0], qkv.at[0], 6, recv.at[5], sibling)

    @pl.when(c == 0)
    def _():
        loads[0].wait()
        arrived(qkv.at[0], recv.at[5])

    query = qkv[0]

    spread = jnp.concatenate(
        [jnp.where(column_head == h, query.astype(F32), 0.0) for h in range(4)], axis=0
    ).astype(BF16)
    every = jnp.dot(spread, across[...], preferred_element_type=F32)
    scores = every[:, :128]
    for j in range(1, 8):
        scores = jnp.where(pair == j, every[:, j * 128 : j * 128 + 128], scores)
    scores = jnp.where(valid, scores * HD ** (-0.5), NEG)
    top = jnp.max(scores, axis=1, keepdims=True)
    weights = jnp.where(valid, jnp.exp(scores - top), 0.0)
    total = jnp.sum(weights, axis=1, keepdims=True)
    upper = weights.astype(BF16).astype(F32)
    lower = weights - upper
    wide = jnp.concatenate(
        [
            jnp.concatenate([jnp.where(pair == j, part, 0.0).astype(BF16) for j in range(8)], axis=1)
            for part in (upper, lower)
        ],
        axis=0,
    )
    loads[3].wait()
    both = jnp.dot(wide, vbuf[...].reshape(B * SPAN, W), preferred_element_type=F32)
    summed = both[: 4 * B] + both[4 * B :]

    def fold(rows):
        result = jnp.broadcast_to(rows[0:B], (B, W))
        for h in range(1, 4):
            result = jnp.where(column_head == h, rows[h * B : (h + 1) * B], result)
        return result

    for core in range(2):
        for i, part in enumerate((fold(summed), fold(total), fold(top))):
            csend[core, i] = part[core * HALF : (core + 1) * HALF]
    push(csend.at[1 - c], crecv, 1, recv.at[0], sibling)

    @pl.when(c == 1)
    def _():
        loads[4].wait()
        for index in (1, 2):
            qkv[index] = sum(project(index, t) for t in range(TP)).astype(BF16)
        push(qkv.at[pl.ds(1, 2)], qkv.at[pl.ds(1, 2)], 7, recv.at[6], sibling)

    @pl.when(c == 0)
    def _():
        pl.semaphore_wait(barrier, 32)
        pl.semaphore_signal(ready, inc=1, device_id=sibling, device_id_type=MESH)

    arrived(crecv, recv.at[0])
    my_acc, my_total, my_top = csend[c, 0], csend[c, 1], csend[c, 2]
    both_top = jnp.maximum(my_top, crecv[2])
    mine, other = jnp.exp(my_top - both_top), jnp.exp(crecv[2] - both_top)
    both_acc = my_acc * mine + crecv[0] * other
    both_total = my_total * mine + crecv[1] * other

    def place(ref, slot, acc, row):
        base = pl.multiple_of(slot * SLOT, 8)
        ref[pl.ds(base, 8), :] = acc
        ref[pl.ds(base + 8, 1), :] = row

    def slot_of(ref, slot):
        return ref.at[pl.ds(pl.multiple_of(slot * SLOT, 8), SENT), :]

    def wait_ring(ref, sem):
        arrived(ref.at[pl.ds(0, 14 * SENT), :], sem)

    def push_ring(ref, slot_y, slot_z, stage, recv_sem):
        for y_peer, z_peer in zip(y_peers, z_peers):
            push(slot_of(ref, slot_y), slot_of(ref, slot_y), stage, recv_sem, y_peer)
            push(slot_of(ref, slot_z), slot_of(ref, slot_z), stage, recv_sem, z_peer)

    def spread_rows(rows):
        keep = iota((HALF, 128), 1) % HD == iota((HALF, 128), 0)
        return split_dot(
            jnp.concatenate(
                [jnp.where(keep, rows[s : s + 1], 0.0) for s in range(rows.shape[0])], axis=0
            ),
            same_head,
        )

    def ring_acc(ref, factors, first):
        acc = None
        for s in range(first, first + RING):
            part = ref[s * SLOT : s * SLOT + 8, :] * factors[s * 8 : s * 8 + 8]
            acc = part if acc is None else acc + part
        return acc

    def over(first, second):
        return jnp.where(iota((2 * RING, 128), 0) < RING, first, second)

    low_row, high_row = to_row(both_top, both_total)
    place(yb, y, both_acc[:, :128], low_row)
    place(yb, RING + z, both_acc[:, 128:], high_row)

    @pl.when(c == 1)
    def _():
        pl.semaphore_wait(ready, 1)

    push_ring(yb, y, RING + z, 2, recv.at[1])

    @pl.when(c == 0)
    def _():
        arrived(qkv.at[pl.ds(1, 2)], recv.at[6])

    new_key, new_value = qkv[1], qkv[2]
    product = query.astype(F32) * new_key.astype(F32)
    halves = split_dot(jnp.concatenate([product[:, :128], product[:, 128:]], axis=0), same_head)
    new_score = jnp.concatenate([halves[:B], halves[B:]], axis=1) * HD ** (-0.5)

    def own_half(rows):
        return jnp.where(c == 0, rows[:HALF], rows[HALF:])

    new_low, new_high = to_row(own_half(new_score), jnp.ones((HALF, W), F32))
    new_acc = own_half(new_value.astype(F32))
    position = iota((SPAN, W), 0)
    for b in range(B):
        hit = position == lens[b] - seq * SPAN
        kbuf[b] = jnp.where(hit, new_key[b : b + 1].astype(F32), kbuf[b].astype(F32)).astype(BF16)
        vbuf[b] = jnp.where(hit, new_value[b : b + 1].astype(F32), vbuf[b].astype(F32)).astype(BF16)
    max_lane = iota((1, 128), 1) % HD < HALF
    wait_ring(yb, recv.at[1])
    rows = yb[pl.ds(8, 2 * RING, stride=SLOT), :]
    low_top = jnp.max(rows[:RING], axis=0, keepdims=True)
    high_top = jnp.max(rows[RING:], axis=0, keepdims=True)
    factor = jnp.exp(rows - over(low_top, high_top))
    totals = rows * pltpu.roll(factor, HALF, 1)
    low_total = jnp.sum(totals[:RING], axis=0, keepdims=True)
    high_total = jnp.sum(totals[RING:], axis=0, keepdims=True)
    factors = spread_rows(factor)
    place(zb, z, ring_acc(yb, factors, 0), jnp.where(max_lane, low_top, low_total))
    place(zb, RING + y, ring_acc(yb, factors, RING), jnp.where(max_lane, high_top, high_total))
    push_ring(zb, RING + y, z, 3, recv.at[2])

    own_hidden = own_half(gath[tp].astype(F32))
    loads[5].wait()
    loads[6].wait()
    loads[7].wait()

    wait_ring(zb, recv.at[2])
    rows = zb[pl.ds(8, 2 * RING, stride=SLOT), :]
    low_top = jnp.maximum(jnp.max(rows[:RING], axis=0, keepdims=True), new_low)
    high_top = jnp.maximum(jnp.max(rows[RING:], axis=0, keepdims=True), new_high)
    factor = jnp.exp(rows - over(low_top, high_top))
    totals = rows * pltpu.roll(factor, HALF, 1)
    low_new, high_new = jnp.exp(new_low - low_top), jnp.exp(new_high - high_top)
    low_total = jnp.sum(totals[:RING], axis=0, keepdims=True) + new_low * pltpu.roll(low_new, HALF, 1)
    high_total = jnp.sum(totals[RING:], axis=0, keepdims=True) + new_high * pltpu.roll(high_new, HALF, 1)
    low_share, high_share = pltpu.roll(low_total, 128 - HALF, 1), pltpu.roll(high_total, 128 - HALF, 1)
    factors = spread_rows(
        jnp.concatenate(
            [factor / over(low_share, high_share), low_new / low_share, high_new / high_share], axis=0
        )
    )
    attended = jnp.concatenate(
        [
            ring_acc(zb, factors, 0) + new_acc[:, :128] * factors[128:136],
            ring_acc(zb, factors, RING) + new_acc[:, 128:] * factors[136:144],
        ],
        axis=1,
    )
    attended = attended.astype(BF16)

    def push_rows(half, peer):
        part = mixb.at[tp, :, pl.ds(half * 2 * W, 2 * W)]
        push(part, part, 4, recv.at[3], peer)

    for half in range(2):
        lanes = slice(half * 2 * W, (half + 1) * 2 * W)
        mixed = jnp.dot(attended, wobuf[:, lanes], preferred_element_type=F32)
        for t in (2 * half, 2 * half + 1):
            part = mixed[:, t % 2 * W : (t % 2 + 1) * W]
            mixb[tp, :, t * W : (t + 1) * W] = part + jnp.where(tp == t, own_hidden, 0.0)
        push_rows(half, tp_peers[0])
    for half in range(2):
        for peer in tp_peers[1:]:
            push_rows(half, peer)
    arrived(mixb.at[pl.ds(0, 3)], recv.at[3])
    resid = []
    for t in range(TP):
        lanes = slice(t * W, (t + 1) * W)
        resid.append((mixb[0, :, lanes] + mixb[1, :, lanes]) + (mixb[2, :, lanes] + mixb[3, :, lanes]))
    mean = jnp.sum((resid[0] + resid[1]) + (resid[2] + resid[3]), axis=1, keepdims=True) / D
    centred = [part - mean for part in resid]
    square = [part * part for part in centred]
    var = jnp.sum((square[0] + square[1]) + (square[2] + square[3]), axis=1, keepdims=True) / D
    own = centred[0]
    for t in range(1, TP):
        own = jnp.where(tp == t, centred[t], own)
    fin[c] = own / jnp.sqrt(var + 1e-05) * gbuf[...] + bbuf[...]
    push(fin.at[c], fin.at[c], 5, recv.at[4], sibling)

    @pl.when(c == 1)
    def _():
        arrived(gath.at[pl.ds(0, 3)], sent.at[0])
        arrived(qkv.at[0], sent.at[6])
        arrived(qkv.at[pl.ds(1, 2)], sent.at[7])

    arrived(crecv, sent.at[1])
    wait_ring(yb, sent.at[2])
    wait_ring(zb, sent.at[3])
    arrived(mixb.at[pl.ds(0, 3)], sent.at[4])
    arrived(fin.at[0], recv.at[4])
    out[...] = jnp.concatenate([fin[0], fin[1]], axis=0).astype(BF16)
    arrived(fin.at[0], sent.at[5])


def hand_out(o_in, k_in, v_in, o_out, k_out, v_out, sem):
    copies = [pltpu.make_async_copy(o_in, o_out, sem.at[0])]
    for i in range(4):
        part = pl.ds(i * B // 4, B // 4)
        copies.append(pltpu.make_async_copy(k_in.at[part], k_out.at[part], sem.at[1 + 2 * i]))
        copies.append(pltpu.make_async_copy(v_in.at[part], v_out.at[part], sem.at[2 + 2 * i]))
    for copy in copies:
        copy.start()
    for copy in copies:
        copy.wait()


def body(hidden_in, w_qkv, w_out, key_cache, value_cache, lengths, ln_gain, ln_bias):
    hbm = pl.BlockSpec(memory_space=pl.ANY)
    vmem = pl.BlockSpec(memory_space=pltpu.VMEM)
    cache = (B, SPAN, W)
    dma = pltpu.SemaphoreType.DMA
    done = pl.pallas_call(
        kernel,
        out_shape=(pltpu.VMEM((B, W), BF16), pltpu.VMEM(cache, BF16), pltpu.VMEM(cache, BF16)),
        in_specs=[hbm] * 8,
        out_specs=(vmem, vmem, vmem),
        scratch_shapes=[
            pltpu.SMEM((B,), jnp.int32),
            pltpu.VMEM((W, B * SPAN), BF16),
            pltpu.VMEM((TP, B, W), BF16),
            pltpu.VMEM((3, B, W), BF16),
            pltpu.VMEM((3, D, W), BF16),
            pltpu.VMEM((W, D), BF16),
            pltpu.VMEM((1, W), F32),
            pltpu.VMEM((1, W), F32),
            pltpu.VMEM((2, 3, HALF, W), F32),
            pltpu.VMEM((3, HALF, W), F32),
            pltpu.VMEM((2 * RING * SLOT, 128), F32),
            pltpu.VMEM((2 * RING * SLOT, 128), F32),
            pltpu.VMEM((TP, HALF, D), F32),
            pltpu.VMEM((2, HALF, W), F32),
            dma((9,)), dma((3,)), dma((7,)), dma((8,)), pltpu.SemaphoreType.REGULAR,
        ],
        compiler_params=pltpu.CompilerParams(collective_id=0, has_side_effects=True),
        name="sublayer",
    )(
        lengths, hidden_in, w_qkv, w_out, key_cache, value_cache,
        ln_gain.reshape(1, W), ln_bias.reshape(1, W),
    )
    return pl.pallas_call(
        hand_out,
        out_shape=(
            jax.ShapeDtypeStruct((B, W), BF16),
            jax.ShapeDtypeStruct(cache, BF16),
            jax.ShapeDtypeStruct(cache, BF16),
        ),
        in_specs=[vmem] * 3,
        out_specs=(hbm, hbm, hbm),
        scratch_shapes=[dma((9,))],
        name="hand_out",
    )(*[pltpu.with_memory_space_constraint(part, pltpu.VMEM) for part in done])


def solution(mesh):
    in_specs = (
        P(None, "tp"),
        P(None, None, "tp"),
        P("tp", None),
        P(None, "seq", "tp"),
        P(None, "seq", "tp"),
        P(),
        P("tp"),
        P("tp"),
    )
    out_specs = (P(None, "tp"), P(None, "seq", "tp"), P(None, "seq", "tp"))
    return jax.shard_map(body, mesh=mesh, in_specs=in_specs, out_specs=out_specs, check_vma=False)
```

```python
import jax
import jax.numpy as jnp
from jax import lax
from jax.experimental import pallas as pl
from jax.experimental.pallas import tpu as pltpu
from jax.sharding import PartitionSpec as P

D = 1024
HD = 64
B = 16
HALF = 8
W = 256
TP = 4
RING = 8
SPAN = 64
SLOT = 16
SENT = 9
NEG = -1e30
F32 = jnp.float32
BF16 = jnp.bfloat16
MESH = pl.DeviceIdType.MESH


def iota(shape, dim):
    return lax.broadcasted_iota(jnp.int32, shape, dim)


def split_dot(rows, matrix):
    upper = rows.astype(BF16)
    lower = (rows - upper.astype(F32)).astype(BF16)
    both = jnp.dot(jnp.concatenate([upper, lower], axis=0), matrix, preferred_element_type=F32)
    return both[: rows.shape[0]] + both[rows.shape[0] :]


def to_row(tops, totals):
    lane, request = iota((HALF, W), 1) % HD, iota((HALF, W), 0)
    picked = jnp.where(lane == request, tops, jnp.where(lane == request + HALF, totals, 0.0))
    row = jnp.sum(picked, axis=0, keepdims=True)
    return row[:, :128], row[:, 128:]


def kernel(
    lengths, hid, wqkv, wout, kc, vc, gain, bias,
    out, kbuf, vbuf,
    lens, across, gath, qkv, wbuf, wobuf, gbuf, bbuf,
    csend, crecv, yb, zb, mixb, fin,
    lsem, hsem, recv, sent, ready,
):
    seq = lax.axis_index("seq")
    tp = lax.axis_index("tp")
    y, z, c = seq // 16, (seq % 16) // 2, seq % 2

    loads = [
        pltpu.make_async_copy(hid, gath.at[tp], lsem.at[0]),
        pltpu.make_async_copy(wqkv.at[0], wbuf.at[0], lsem.at[1]),
        pltpu.make_async_copy(kc, kbuf, lsem.at[2]),
        pltpu.make_async_copy(vc, vbuf, lsem.at[3]),
        pltpu.make_async_copy(wqkv.at[pl.ds(1, 2)], wbuf.at[pl.ds(1, 2)], lsem.at[4]),
        pltpu.make_async_copy(wout, wobuf, lsem.at[5]),
        pltpu.make_async_copy(gain, gbuf, lsem.at[6]),
        pltpu.make_async_copy(bias, bbuf, lsem.at[7]),
        pltpu.make_async_copy(lengths, lens, lsem.at[8]),
    ]
    tp_peers = [(seq, lax.rem(tp + d, TP)) for d in (2, 1, 3)]
    y_peers = [(lax.rem(y + d, RING) * 16 + z * 2 + c, tp) for d in (4, 3, 5, 2, 6, 1, 7)]
    z_peers = [(y * 16 + lax.rem(z + d, RING) * 2 + c, tp) for d in (4, 3, 5, 2, 6, 1, 7)]
    sibling = (y * 16 + z * 2 + (1 - c), tp)
    y_zero = [(lax.rem(y + d, RING) * 16 + z * 2, tp) for d in (4, 3, 5, 2, 6, 1, 7)]
    z_zero = [(y * 16 + lax.rem(z + d, RING) * 2, tp) for d in (4, 3, 5, 2, 6, 1, 7)]

    barrier = pltpu.get_barrier_semaphore()

    def signal(peer):
        pl.semaphore_signal(barrier, inc=1, device_id=peer, device_id_type=MESH)

    @pl.when(c == 1)
    def _():
        for peer in tp_peers:
            signal(peer)
        loads[0].start()
        for z_peer, y_peer in zip(z_zero, y_zero):
            signal(z_peer)
            signal(y_peer)
        signal(sibling)
        for index in (1, 8, 2, 3, 4, 5, 6, 7):
            loads[index].start()
        loads[0].wait()
        pl.semaphore_wait(barrier, 4)

    @pl.when(c == 0)
    def _():
        signal(sibling)
        for z_peer, y_peer in zip(z_peers, y_peers):
            signal(z_peer)
            signal(y_peer)
        for peer in tp_peers:
            signal(peer)
        for index in (8, 2, 3, 0, 5, 6, 7):
            loads[index].start()

    def push(src, dst, stage, recv_sem, peer):
        pltpu.make_async_remote_copy(
            src, dst, sent.at[stage], recv_sem, device_id=peer, device_id_type=MESH
        ).start()

    def arrived(ref, sem):
        pltpu.make_async_copy(ref, ref, sem).wait()

    def project(index, t):
        rows = pl.ds(pl.multiple_of(t * W, W), W)
        return jnp.dot(gath[t], wbuf[index, rows, :], preferred_element_type=F32)

    @pl.when(c == 1)
    def _():
        for i, peer in enumerate(tp_peers):
            push(gath.at[tp], gath.at[tp], 0, hsem.at[i], peer)

    column_head = iota((B, W), 1) // HD
    row_b = iota((B, 1), 0)
    loads[8].wait()
    local_len = jnp.zeros((B, 1), jnp.int32)
    for b in range(B):
        local_len = jnp.where(row_b == b, lens[b] - seq * SPAN, local_len)
    row_len = jnp.concatenate([local_len] * 4, axis=0)
    request = iota((4 * B, 128), 0) % B
    lane = iota((4 * B, 128), 1)
    valid = jnp.logical_and(lane // SPAN == request % 2, lane % SPAN < row_len)
    pair = request // 2
    loads[2].wait()
    across[...] = kbuf[...].reshape(B * SPAN, W).T
    same_head = jnp.where(iota((128, 128), 0) // HD == iota((128, 128), 1) // HD, 1.0, 0.0).astype(BF16)

    @pl.when(c == 1)
    def _():
        loads[1].wait()
        acc = project(0, tp)
        for i, d in ((1, 1), (2, 3), (0, 2)):
            t = lax.rem(tp + TP - d, TP)
            arrived(gath.at[t], hsem.at[i])
            acc = acc + project(0, t)
        qkv[0] = acc.astype(BF16)
        push(qkv.at[0], qkv.at[0], 6, recv.at[5], sibling)

    @pl.when(c == 0)
    def _():
        loads[0].wait()
        arrived(qkv.at[0], recv.at[5])

    query = qkv[0]

    spread = jnp.concatenate(
        [jnp.where(column_head == h, query.astype(F32), 0.0) for h in range(4)], axis=0
    ).astype(BF16)
    every = jnp.dot(spread, across[...], preferred_element_type=F32)
    scores = every[:, :128]
    for j in range(1, 8):
        scores = jnp.where(pair == j, every[:, j * 128 : j * 128 + 128], scores)
    scores = jnp.where(valid, scores * HD ** (-0.5), NEG)
    top = jnp.max(scores, axis=1, keepdims=True)
    weights = jnp.where(valid, jnp.exp(scores - top), 0.0)
    total = jnp.sum(weights, axis=1, keepdims=True)
    upper = weights.astype(BF16).astype(F32)
    lower = weights - upper
    wide = jnp.concatenate(
        [
            jnp.concatenate([jnp.where(pair == j, part, 0.0).astype(BF16) for j in range(8)], axis=1)
            for part in (upper, lower)
        ],
        axis=0,
    )
    loads[3].wait()
    both = jnp.dot(wide, vbuf[...].reshape(B * SPAN, W), preferred_element_type=F32)
    summed = both[: 4 * B] + both[4 * B :]

    def fold(rows):
        result = jnp.broadcast_to(rows[0:B], (B, W))
        for h in range(1, 4):
            result = jnp.where(column_head == h, rows[h * B : (h + 1) * B], result)
        return result

    for core in range(2):
        for i, part in enumerate((fold(summed), fold(total), fold(top))):
            csend[core, i] = part[core * HALF : (core + 1) * HALF]
    push(csend.at[1 - c], crecv, 1, recv.at[0], sibling)

    @pl.when(c == 1)
    def _():
        loads[4].wait()
        for index in (1, 2):
            qkv[index] = sum(project(index, t) for t in range(TP)).astype(BF16)
        push(qkv.at[pl.ds(1, 2)], qkv.at[pl.ds(1, 2)], 7, recv.at[6], sibling)

    @pl.when(c == 0)
    def _():
        pl.semaphore_wait(barrier, 32)
        pl.semaphore_signal(ready, inc=1, device_id=sibling, device_id_type=MESH)

    arrived(crecv, recv.at[0])
    my_acc, my_total, my_top = csend[c, 0], csend[c, 1], csend[c, 2]
    both_top = jnp.maximum(my_top, crecv[2])
    mine, other = jnp.exp(my_top - both_top), jnp.exp(crecv[2] - both_top)
    both_acc = my_acc * mine + crecv[0] * other
    both_total = my_total * mine + crecv[1] * other

    def place(ref, slot, acc, row):
        base = pl.multiple_of(slot * SLOT, 8)
        ref[pl.ds(base, 8), :] = acc
        ref[pl.ds(base + 8, 1), :] = row

    def slot_of(ref, slot):
        return ref.at[pl.ds(pl.multiple_of(slot * SLOT, 8), SENT), :]

    def wait_ring(ref, sem):
        arrived(ref.at[pl.ds(0, 14 * SENT), :], sem)

    def push_ring(ref, slot_y, slot_z, stage, recv_sem):
        for y_peer, z_peer in zip(y_peers, z_peers):
            push(slot_of(ref, slot_y), slot_of(ref, slot_y), stage, recv_sem, y_peer)
            push(slot_of(ref, slot_z), slot_of(ref, slot_z), stage, recv_sem, z_peer)

    def spread_rows(rows):
        keep = iota((HALF, 128), 1) % HD == iota((HALF, 128), 0)
        return split_dot(
            jnp.concatenate(
                [jnp.where(keep, rows[s : s + 1], 0.0) for s in range(rows.shape[0])], axis=0
            ),
            same_head,
        )

    def ring_acc(ref, factors, first):
        acc = None
        for s in range(first, first + RING):
            part = ref[s * SLOT : s * SLOT + 8, :] * factors[s * 8 : s * 8 + 8]
            acc = part if acc is None else acc + part
        return acc

    def over(first, second):
        return jnp.where(iota((2 * RING, 128), 0) < RING, first, second)

    low_row, high_row = to_row(both_top, both_total)
    place(yb, y, both_acc[:, :128], low_row)
    place(yb, RING + z, both_acc[:, 128:], high_row)

    @pl.when(c == 1)
    def _():
        pl.semaphore_wait(ready, 1)

    push_ring(yb, y, RING + z, 2, recv.at[1])

    @pl.when(c == 0)
    def _():
        arrived(qkv.at[pl.ds(1, 2)], recv.at[6])

    new_key, new_value = qkv[1], qkv[2]
    product = query.astype(F32) * new_key.astype(F32)
    halves = split_dot(jnp.concatenate([product[:, :128], product[:, 128:]], axis=0), same_head)
    new_score = jnp.concatenate([halves[:B], halves[B:]], axis=1) * HD ** (-0.5)

    def own_half(rows):
        return jnp.where(c == 0, rows[:HALF], rows[HALF:])

    new_low, new_high = to_row(own_half(new_score), jnp.ones((HALF, W), F32))
    new_acc = own_half(new_value.astype(F32))
    position = iota((SPAN, W), 0)
    for b in range(B):
        hit = position == lens[b] - seq * SPAN
        kbuf[b] = jnp.where(hit, new_key[b : b + 1].astype(F32), kbuf[b].astype(F32)).astype(BF16)
        vbuf[b] = jnp.where(hit, new_value[b : b + 1].astype(F32), vbuf[b].astype(F32)).astype(BF16)
    max_lane = iota((1, 128), 1) % HD < HALF
    wait_ring(yb, recv.at[1])
    rows = yb[pl.ds(8, 2 * RING, stride=SLOT), :]
    low_top = jnp.max(rows[:RING], axis=0, keepdims=True)
    high_top = jnp.max(rows[RING:], axis=0, keepdims=True)
    factor = jnp.exp(rows - over(low_top, high_top))
    totals = rows * pltpu.roll(factor, HALF, 1)
    low_total = jnp.sum(totals[:RING], axis=0, keepdims=True)
    high_total = jnp.sum(totals[RING:], axis=0, keepdims=True)
    factors = spread_rows(factor)
    place(zb, z, ring_acc(yb, factors, 0), jnp.where(max_lane, low_top, low_total))
    place(zb, RING + y, ring_acc(yb, factors, RING), jnp.where(max_lane, high_top, high_total))
    push_ring(zb, RING + y, z, 3, recv.at[2])

    own_hidden = own_half(gath[tp].astype(F32))
    loads[5].wait()
    loads[6].wait()
    loads[7].wait()

    wait_ring(zb, recv.at[2])
    rows = zb[pl.ds(8, 2 * RING, stride=SLOT), :]
    low_top = jnp.maximum(jnp.max(rows[:RING], axis=0, keepdims=True), new_low)
    high_top = jnp.maximum(jnp.max(rows[RING:], axis=0, keepdims=True), new_high)
    factor = jnp.exp(rows - over(low_top, high_top))
    totals = rows * pltpu.roll(factor, HALF, 1)
    low_new, high_new = jnp.exp(new_low - low_top), jnp.exp(new_high - high_top)
    low_total = jnp.sum(totals[:RING], axis=0, keepdims=True) + new_low * pltpu.roll(low_new, HALF, 1)
    high_total = jnp.sum(totals[RING:], axis=0, keepdims=True) + new_high * pltpu.roll(high_new, HALF, 1)
    low_share, high_share = pltpu.roll(low_total, 128 - HALF, 1), pltpu.roll(high_total, 128 - HALF, 1)
    factors = spread_rows(
        jnp.concatenate(
            [factor / over(low_share, high_share), low_new / low_share, high_new / high_share], axis=0
        )
    )
    attended = jnp.concatenate(
        [
            ring_acc(zb, factors, 0) + new_acc[:, :128] * factors[128:136],
            ring_acc(zb, factors, RING) + new_acc[:, 128:] * factors[136:144],
        ],
        axis=1,
    )
    attended = attended.astype(BF16)
    for half in range(2):
        lanes = slice(half * 2 * W, (half + 1) * 2 * W)
        mixed = jnp.dot(attended, wobuf[:, lanes], preferred_element_type=F32)
        for t in (2 * half, 2 * half + 1):
            part = mixed[:, t % 2 * W : (t % 2 + 1) * W]
            mixb[tp, :, t * W : (t + 1) * W] = part + jnp.where(tp == t, own_hidden, 0.0)
    for peer in tp_peers:
        push(mixb.at[tp], mixb.at[tp], 4, recv.at[3], peer)
    arrived(mixb.at[pl.ds(0, 3)], recv.at[3])
    resid = []
    for t in range(TP):
        lanes = slice(t * W, (t + 1) * W)
        resid.append((mixb[0, :, lanes] + mixb[1, :, lanes]) + (mixb[2, :, lanes] + mixb[3, :, lanes]))
    mean = jnp.sum((resid[0] + resid[1]) + (resid[2] + resid[3]), axis=1, keepdims=True) / D
    centred = [part - mean for part in resid]
    square = [part * part for part in centred]
    var = jnp.sum((square[0] + square[1]) + (square[2] + square[3]), axis=1, keepdims=True) / D
    own = centred[0]
    for t in range(1, TP):
        own = jnp.where(tp == t, centred[t], own)
    fin[c] = own / jnp.sqrt(var + 1e-05) * gbuf[...] + bbuf[...]
    push(fin.at[c], fin.at[c], 5, recv.at[4], sibling)

    @pl.when(c == 1)
    def _():
        arrived(gath.at[pl.ds(0, 3)], sent.at[0])
        arrived(qkv.at[0], sent.at[6])
        arrived(qkv.at[pl.ds(1, 2)], sent.at[7])

    arrived(crecv, sent.at[1])
    wait_ring(yb, sent.at[2])
    wait_ring(zb, sent.at[3])
    arrived(mixb.at[pl.ds(0, 3)], sent.at[4])
    arrived(fin.at[0], recv.at[4])
    out[...] = jnp.concatenate([fin[0], fin[1]], axis=0).astype(BF16)
    arrived(fin.at[0], sent.at[5])


def hand_out(o_in, k_in, v_in, o_out, k_out, v_out, sem):
    copies = [pltpu.make_async_copy(o_in, o_out, sem.at[0])]
    for i in range(4):
        part = pl.ds(i * B // 4, B // 4)
        copies.append(pltpu.make_async_copy(k_in.at[part], k_out.at[part], sem.at[1 + 2 * i]))
        copies.append(pltpu.make_async_copy(v_in.at[part], v_out.at[part], sem.at[2 + 2 * i]))
    for copy in copies:
        copy.start()
    for copy in copies:
        copy.wait()


def body(hidden_in, w_qkv, w_out, key_cache, value_cache, lengths, ln_gain, ln_bias):
    hbm = pl.BlockSpec(memory_space=pl.ANY)
    vmem = pl.BlockSpec(memory_space=pltpu.VMEM)
    cache = (B, SPAN, W)
    dma = pltpu.SemaphoreType.DMA
    done = pl.pallas_call(
        kernel,
        out_shape=(pltpu.VMEM((B, W), BF16), pltpu.VMEM(cache, BF16), pltpu.VMEM(cache, BF16)),
        in_specs=[hbm] * 8,
        out_specs=(vmem, vmem, vmem),
        scratch_shapes=[
            pltpu.SMEM((B,), jnp.int32),
            pltpu.VMEM((W, B * SPAN), BF16),
            pltpu.VMEM((TP, B, W), BF16),
            pltpu.VMEM((3, B, W), BF16),
            pltpu.VMEM((3, D, W), BF16),
            pltpu.VMEM((W, D), BF16),
            pltpu.VMEM((1, W), F32),
            pltpu.VMEM((1, W), F32),
            pltpu.VMEM((2, 3, HALF, W), F32),
            pltpu.VMEM((3, HALF, W), F32),
            pltpu.VMEM((2 * RING * SLOT, 128), F32),
            pltpu.VMEM((2 * RING * SLOT, 128), F32),
            pltpu.VMEM((TP, HALF, D), F32),
            pltpu.VMEM((2, HALF, W), F32),
            dma((9,)), dma((3,)), dma((7,)), dma((8,)), pltpu.SemaphoreType.REGULAR,
        ],
        compiler_params=pltpu.CompilerParams(collective_id=0, has_side_effects=True),
        name="sublayer",
    )(
        lengths, hidden_in, w_qkv, w_out, key_cache, value_cache,
        ln_gain.reshape(1, W), ln_bias.reshape(1, W),
    )
    return pl.pallas_call(
        hand_out,
        out_shape=(
            jax.ShapeDtypeStruct((B, W), BF16),
            jax.ShapeDtypeStruct(cache, BF16),
            jax.ShapeDtypeStruct(cache, BF16),
        ),
        in_specs=[vmem] * 3,
        out_specs=(hbm, hbm, hbm),
        scratch_shapes=[dma((9,))],
        name="hand_out",
    )(*[pltpu.with_memory_space_constraint(part, pltpu.VMEM) for part in done])


def solution(mesh):
    in_specs = (
        P(None, "tp"),
        P(None, None, "tp"),
        P("tp", None),
        P(None, "seq", "tp"),
        P(None, "seq", "tp"),
        P(),
        P("tp"),
        P("tp"),
    )
    out_specs = (P(None, "tp"), P(None, "seq", "tp"), P(None, "seq", "tp"))
    return jax.shard_map(body, mesh=mesh, in_specs=in_specs, out_specs=out_specs, check_vma=False)
```
